256 devices in a mesh: tile: 64 (over z, x, core), height: 4 (over y).
Axes of the slice: x: 4, y: 4, z: 8, core: 2. Of those that a mesh axis runs over, the one named last changes fastest.
Arguments:
- material: int32 [32, 2048, 128], P('height', 'tile'), may hold values from 0 to 2
- clamped: int32 [32, 2048, 128], P('height', 'tile'), may hold values from 0 to 1, as said below
- stiffness_table: float32 [3], replicated, may hold values from 0.5 to 4
- eigenstrain: float32 [3, 3], replicated, may hold values from -6 to 6
Outputs:
- displacement: float32 [3, 32, 2048, 128], P(None, 'height', 'tile')
The draws below stay inside these ranges and needn't reach their ends.
Inputs may be any that keep to these rules, and one draw needn't show every extreme that they name: `clamped`: only voxels of the lowest 2 layers can be 1; in those layers 0 and 1 are equally likely.
All inputs are finite; a program needn't handle non-finite values.
Results may differ from the reference program's by a relative error of at most 0.00016.
Values sent between devices are 32-bit elements; how exact they have to be, the bound alone decides.
A program may use at most 128 MiB of HBM per device.

```python
import math
import jax
import jax.numpy as jnp
from jax import lax

CY = 128
NLABEL = 3
LEVELS = 3
PRE = 2
POST = 1
COARSE_SWEEPS = 6
CLAMP_LAYERS = 2
NZ = 32
BX = 2048


def draw_clamped(key, part):
    joined = jax.random.randint(key, (NZ, BX, CY), 0, 2, dtype=jnp.int32)
    layer_idx = lax.broadcasted_iota(jnp.int32, (NZ, BX, CY), 0)
    return jnp.where(layer_idx < CLAMP_LAYERS, joined, jnp.zeros_like(joined))


def plant(entries, stream_key, smallest, largest):
    extent = entries.shape
    index_at = [jax.random.randint(jax.random.fold_in(stream_key, axis), (), 0, extent[axis]) for axis in range(len(extent))]
    entries = entries.at[tuple(index_at)].set(smallest)
    longest = extent.index(max(extent))
    index_at[longest] = (index_at[longest] + 1) % extent[longest]
    return entries.at[tuple(index_at)].set(largest)


def gaussian(rng, shape, spread, bound, held_as=jnp.bfloat16):
    return jnp.clip(spread * jax.random.normal(rng, shape, jnp.float32), -bound, bound).astype(held_as)


def setup_inputs(seed: int = 0) -> dict:
    seeds = jax.random.split(jax.random.key(seed), 5)
    material = plant(jax.random.randint(seeds[0], (NZ, BX, CY), 0, 3), jax.random.fold_in(seeds[0], 1), 0, 2).astype(jnp.int32)
    clamped = draw_clamped(jax.random.fold_in(seeds[4], 71), 0)
    stiffness_table = jnp.clip(jnp.exp(jax.random.uniform(seeds[2], (NLABEL,), jnp.float32, math.log(0.5), math.log(4.0))), 0.5, 4.0)
    eigenstrain = gaussian(seeds[3], (NLABEL, 3), 2.0, 6.0, jnp.float32)
    return {"material": material, "clamped": clamped, "stiffness_table": stiffness_table, "eigenstrain": eigenstrain}


GAMMA = 1.0
PENALTY = 50.0
OMEGA = 0.6


def lookup(labels, table):
    result = jnp.zeros(labels.shape, table.dtype)
    for label_id in range(NLABEL):
        result = result + (labels == label_id).astype(table.dtype) * table[label_id]
    return result


def block_sum(field):
    dims_now = field.shape
    shaped = field.reshape(dims_now[0], dims_now[1] // 2, 2, dims_now[2] // 2, 2, dims_now[3] // 2, 2)
    return shaped.sum(axis=(2, 4, 6))


def prolong(field):
    return jnp.repeat(jnp.repeat(jnp.repeat(field, 2, axis=1), 2, axis=2), 2, axis=3)


def direction_factor(direction, dtype):
    return jnp.where(jnp.arange(3) == direction, 1.0 + GAMMA, 1.0).astype(dtype).reshape(3, 1, 1, 1)


def lower_of(field, axis_dim):
    widths = [(0, 0)] * 4
    widths[axis_dim] = (1, 0)
    return lax.slice_in_dim(jnp.pad(field, widths), 0, field.shape[axis_dim], axis=axis_dim)


def upper_of(field, axis_dim):
    widths = [(0, 0)] * 4
    widths[axis_dim] = (0, 1)
    return lax.slice_in_dim(jnp.pad(field, widths), 1, field.shape[axis_dim] + 1, axis=axis_dim)


def grid_pairs(field):
    return [(lower_of(field, direction + 1), upper_of(field, direction + 1)) for direction in range(3)]


def coefficients(stiffness, spring, pairs):
    k_lower, k_upper = [], []
    diagonal = jnp.broadcast_to(spring, (3,) + spring.shape[1:])
    for direction in range(3):
        lower_nb, upper_nb = pairs[direction]
        low_face = 0.5 * (stiffness + lower_nb)
        high_face = 0.5 * (stiffness + upper_nb)
        diagonal = diagonal + direction_factor(direction, stiffness.dtype) * (low_face + high_face)
        k_lower.append(low_face)
        k_upper.append(high_face)
    return k_lower, k_upper, diagonal


def apply_operator(motion, spring, k_lower, k_upper, pairs):
    result = spring * motion
    for direction in range(3):
        lower_nb, upper_nb = pairs[direction]
        term = k_lower[direction] * (motion - lower_nb) + k_upper[direction] * (motion - upper_nb)
        result = result + direction_factor(direction, motion.dtype) * term
    return result


def smooth_from_zero(source, spring, terms, sweeps, pairs_fn):
    k_lower, k_upper, diagonal = terms
    motion = OMEGA * source / diagonal
    for turn_idx in range(sweeps - 1):
        motion = motion + OMEGA * (source - apply_operator(motion, spring, k_lower, k_upper, pairs_fn(motion))) / diagonal
    return motion


def reference(material, clamped, stiffness_table, eigenstrain):
    labels = material[None]
    stiffness = lookup(labels, stiffness_table)
    spring = PENALTY * clamped[None].astype(jnp.float32)
    pieces = []
    for component in range(3):
        stress = stiffness * lookup(labels, eigenstrain[:, component])
        pieces.append(0.5 * (lower_of(stress, component + 1) - upper_of(stress, component + 1)))
    source = jnp.concatenate(pieces, 0)
    saved = []
    for grid_level in range(LEVELS):
        terms = coefficients(stiffness, spring, grid_pairs(stiffness))
        motion = smooth_from_zero(source, spring, terms, PRE, grid_pairs)
        remain = source - apply_operator(motion, spring, terms[0], terms[1], grid_pairs(motion))
        saved.append((motion, source, spring, terms))
        source = block_sum(remain)
        stiffness = 0.5 * block_sum(stiffness)
        spring = block_sum(spring)
    terms = coefficients(stiffness, spring, grid_pairs(stiffness))
    motion = smooth_from_zero(source, spring, terms, COARSE_SWEEPS, grid_pairs)
    for grid_level in reversed(range(LEVELS)):
        level_motion, level_source, level_spring, terms = saved[grid_level]
        k_lower, k_upper, diagonal = terms
        motion = level_motion + prolong(motion)
        for turn_idx in range(POST):
            motion = motion + OMEGA * (level_source - apply_operator(motion, level_spring, k_lower, k_upper, grid_pairs(motion))) / diagonal
    return motion
```

```python
import functools

import jax
import jax.numpy as jnp
from jax import lax
from jax.experimental import pallas as pl
from jax.experimental.pallas import tpu as pltpu
from jax.sharding import PartitionSpec as P

PENALTY = 50.0
OMEGA = 0.6
KEEP = 1.0 - OMEGA
F32 = jnp.float32
HI = lax.Precision.HIGHEST
NEAR = tuple((dt, dh) for dt in (-1, 0, 1) for dh in (-1, 0, 1) if (dt, dh) != (0, 0))
FAR = tuple((dt, k) for dt in (-2, -1, 0, 1, 2) for k in (0, 1, 2, 3) if (dt, k) != (0, 0))


def iota(shape, axis):
    return lax.broadcasted_iota(jnp.int32, shape, axis)


def one_hot(shape, cond):
    return jnp.where(cond(iota(shape, 0), iota(shape, 1)), 1.0, 0.0).astype(F32)


def dot(a, b):
    return jnp.dot(a, b, preferred_element_type=F32, precision=HI)


def kernel(
    heights,
    tiles,
    mat_hbm,
    clamp_hbm,
    table,
    eigen,
    out,
    mat,
    cl,
    m_lo, m_hi, m_side, m_corner, m_stage,
    q1, q1_vert, q1_side, q1_stage,
    q2, q2_own,
    b1_vert, b1_side, b1_stage,
    b2, b2_own,
    S, SG, HZ, HR, HC, BB, WH, DD, V0, V1, RS,
    S1, HZ1, HR1, HC1, BB1, WH1, DD1, VA1, VB1, RS1, PO1,
    HZ2, HR2, HC2, WH2, DD2, VA2, VB2, PO2, T1,
    S3, HZ3, HR3, HC3, WH3, BB3, V3,
    T0, R4,
    local_sem,
    m_send, m_recv, q1_send, q1_recv, q2_send, q2_recv, b1_send, b1_recv, b2_send, b2_recv,
):
    i = lax.axis_index("tile")
    h = lax.axis_index("height")

    in_mat = pltpu.make_async_copy(mat_hbm, mat, local_sem.at[0])
    in_cl = pltpu.make_async_copy(clamp_hbm.at[pl.ds(0, 2)], cl, local_sem.at[1])
    in_mat.start()
    in_cl.start()

    def tile_ok(dt):
        return jnp.logical_and(i + dt >= 0, i + dt < tiles)

    def near_ok(dt, dh):
        return jnp.logical_and(tile_ok(dt), jnp.logical_and(h + dh >= 0, h + dh < heights))

    def far_id(dt, k):
        return {"tile": i + dt, "height": lax.rem(h + k, heights)}

    barrier = pltpu.get_barrier_semaphore()
    for dt, k in FAR:
        @pl.when(tile_ok(dt))
        def _():
            pl.semaphore_signal(
                barrier, inc=1, device_id=far_id(dt, k), device_id_type=pl.DeviceIdType.MESH
            )
    reach = sum(tile_ok(dt).astype(jnp.int32) for dt in (-2, -1, 0, 1, 2))

    in_mat.wait()
    in_cl.wait()
    for z in range(8):
        m_stage[0, z] = mat[z, 0:4]
        m_stage[1, z] = mat[z, 28:32]
    for z in range(2):
        m_stage[0, 8 + z] = cl[z, 0:4]
        m_stage[1, 8 + z] = cl[z, 28:32]

    pl.semaphore_wait(barrier, 4 * reach - 1)

    def near_copies(send, recv, refs):
        copies = []
        for k, (dt, dh) in enumerate(NEAR):
            src, dst = refs(dt, dh)
            copy = pltpu.make_async_remote_copy(
                src_ref=src, dst_ref=dst, send_sem=send.at[k], recv_sem=recv.at[k],
                device_id={"tile": i + dt, "height": h + dh},
                device_id_type=pl.DeviceIdType.MESH,
            )
            copies.append((copy, near_ok(dt, dh), near_ok(-dt, -dh)))
        return copies

    def far_copies(send, recv, own, field):
        copies = []
        for k, (dt, dh) in enumerate(FAR):
            copy = pltpu.make_async_remote_copy(
                src_ref=own,
                dst_ref=field.at[pl.ds(2 * h, 2), pl.ds(8 * (2 - dt), 8)],
                send_sem=send.at[k], recv_sem=recv.at[k],
                device_id=far_id(dt, dh), device_id_type=pl.DeviceIdType.MESH,
            )
            copies.append((copy, tile_ok(dt), tile_ok(-dt)))
        return copies

    def start(copies):
        for copy, sends, _ in copies:
            @pl.when(sends)
            def _():
                copy.start()

    def wait_recv(copies):
        for copy, _, receives in copies:
            @pl.when(receives)
            def _():
                copy.wait_recv()

    def wait_send(copies):
        for copy, sends, _ in copies:
            @pl.when(sends)
            def _():
                copy.wait_send()

    def label_refs(dt, dh):
        if dt == 0:
            return (mat.at[pl.ds(5, 3)], m_lo) if dh > 0 else (mat.at[pl.ds(0, 3)], m_hi)
        side = 0 if dt < 0 else 1
        if dh == 0:
            return m_stage.at[side], m_side.at[side]
        first = 6 if dh > 0 else 0
        return m_stage.at[side, pl.ds(first, 2)], m_corner.at[side, 0 if dh < 0 else 1]

    label_moves = near_copies(m_send, m_recv, label_refs)
    start(label_moves)

    st = [table[n] for n in range(3)]
    stress = [[table[n] * eigen[n, c] for c in range(3)] for n in range(3)]

    def look(m, values):
        return jnp.where(
            m == 0, values[0], jnp.where(m == 1, values[1], jnp.where(m == 2, values[2], 0.0))
        )

    take_lo = one_hot((128, 128), lambda l, j: jnp.logical_and(j < 64, l // 2 == j))
    take_hi = one_hot((128, 128), lambda l, j: l // 2 == j - 64)
    lowest = jnp.where(h == 0, 1.0, 0.0).astype(F32)

    for z in range(4):
        R4[0, z] = look(mat[2 * z], st) + look(mat[2 * z + 1], st)
    R4[1, 0] = (cl[0] + cl[1]).astype(F32)
    s_rows = jnp.concatenate(
        [R4[0, z, pl.ds(0, 16, 2)] + R4[0, z, pl.ds(1, 16, 2)] for z in range(4)], axis=0
    )
    p_rows = R4[1, 0, pl.ds(0, 16, 2)] + R4[1, 0, pl.ds(1, 16, 2)]
    s_one = dot(0.5 * s_rows, take_lo).reshape(4, 16, 128)
    p_one = dot((2.0 * PENALTY * lowest) * p_rows, take_hi)
    q1[0] = s_one[0] + p_one
    for z in range(1, 4):
        q1[z] = s_one[z]
    for z in range(4):
        q1_stage[0, z] = q1[z, 0:4]
        q1_stage[1, z] = q1[z, 12:16]

    def q1_refs(dt, dh):
        if dt == 0:
            return q1, q1_vert.at[0 if dh > 0 else 1]
        side = 0 if dt < 0 else 1
        return q1_stage.at[side], q1_side.at[side, dh + 1]

    q1_moves = near_copies(q1_send, q1_recv, q1_refs)
    start(q1_moves)

    for z in range(2):
        R4[1, z, 0:16] = q1[2 * z] + q1[2 * z + 1]
    q_rows = jnp.concatenate(
        [R4[1, z, pl.ds(0, 8, 2)] + R4[1, z, pl.ds(1, 8, 2)] for z in range(2)], axis=0
    )
    l, j = iota((128, 128), 0), iota((128, 128), 1)
    down_q = jnp.where(
        jnp.logical_and(j < 96, jnp.logical_and(l < 64, l // 2 == j % 32)), 0.5,
        jnp.where(jnp.logical_and(j >= 96, l // 2 == j - 64), 1.0, 0.0),
    ).astype(F32)
    q2_own[...] = dot(q_rows, down_q).reshape(2, 8, 128)
    q2_moves = far_copies(q2_send, q2_recv, q2_own, q2)
    start(q2_moves)
    q2[pl.ds(2 * h, 2), 16:24] = q2_own[...]

    lane = iota((40, 128), 1)
    sub8 = iota((8, 128), 0)
    wait_recv(label_moves)
    below, above = h > 0, h < heights - 1
    before, after = i > 0, i < tiles - 1

    def side_rows(z, ref_of):
        lo_ok, lo = ref_of(1)
        hi_ok, hi = ref_of(0)
        return jnp.concatenate([jnp.where(hi_ok, hi, -1), jnp.where(lo_ok, lo, -1)], axis=0)

    def labels(z):
        if z < 0:
            centre = jnp.where(below, m_lo[z + 3], -1)
            if z < -2:
                return jnp.concatenate([centre, jnp.full((8, 128), -1, jnp.int32)], axis=0)
            sides = side_rows(
                z, lambda s: (jnp.logical_and(below, before if s else after), m_corner[s, 1, z + 2])
            )
        elif z < 8:
            centre = mat[z]
            sides = side_rows(z, lambda s: (before if s else after, m_side[s, z]))
        else:
            centre = jnp.where(above, m_hi[z - 8], -1)
            if z > 9:
                return jnp.concatenate([centre, jnp.full((8, 128), -1, jnp.int32)], axis=0)
            sides = side_rows(
                z, lambda s: (jnp.logical_and(above, before if s else after), m_corner[s, 0, z - 8])
            )
        return jnp.concatenate([centre, sides], axis=0)

    for z in range(-3, 11):
        m = labels(z)
        S[z + 3] = look(m, st)
        for c in range(3):
            SG[c, z + 3] = look(m, [stress[n][c] for n in range(3)])
    for z in range(-3, 10):
        HZ[z + 3] = S[z + 3] + S[z + 4]

    def spring0(z):
        sides = jnp.concatenate(
            [jnp.where(after, m_side[0, 8 + z], 0), jnp.where(before, m_side[1, 8 + z], 0)], axis=0
        )
        return (2.0 * PENALTY * lowest) * jnp.concatenate([cl[z], sides], axis=0).astype(F32)

    for z in range(-2, 10):
        s = S[z + 3]
        s_r = pltpu.roll(s, 39, 0)
        s_c = jnp.where(lane < 127, pltpu.roll(s, 127, 1), 0.0)
        h_ru = s + s_r
        h_rl = pltpu.roll(h_ru, 1, 0)
        f_cu = s + s_c
        f_cl = s + jnp.where(lane > 0, pltpu.roll(s, 1, 1), 0.0)
        HR[0, z + 2] = h_rl
        HR[1, z + 2] = h_ru
        HC[0, z + 2] = jnp.where(lane > 0, f_cl, 0.0)
        HC[1, z + 2] = jnp.where(lane < 127, f_cu, 0.0)
        f = [HZ[z + 2] + HZ[z + 3], h_rl + h_ru, f_cl + f_cu]
        total = f[0] + f[1] + f[2]
        if 0 <= z < 2:
            total = total + spring0(z)
        g0 = SG[0, z + 2] - SG[0, z + 4]
        x = SG[1, z + 3]
        g1 = pltpu.roll(x, 1, 0) - pltpu.roll(x, 39, 0)
        x = SG[2, z + 3]
        g2 = jnp.where(lane > 0, pltpu.roll(x, 1, 1), 0.0) - jnp.where(
            lane < 127, pltpu.roll(x, 127, 1), 0.0
        )
        for c, g in enumerate((g0, g1, g2)):
            d = total + f[c]
            w = jnp.where(s > 0.0, OMEGA / jnp.where(s > 0.0, d, 1.0), 0.0)
            BB[c, z + 2] = g
            WH[c, z + 2] = w
            if 0 <= z < 8:
                DD[c, z] = d
            V0[c, z + 2] = w * g

    def apply0(v, off, c, z):
        x = v[c, z + off]
        a = HZ[z + 2] * v[c, z + off - 1] + HZ[z + 3] * v[c, z + off + 1]
        b = HR[0, z + 2] * pltpu.roll(x, 1, 0) + HR[1, z + 2] * pltpu.roll(x, 39, 0)
        e = HC[0, z + 2] * pltpu.roll(x, 1, 1) + HC[1, z + 2] * pltpu.roll(x, 127, 1)
        return x, (a + b + e) + (a, b, e)[c]

    for z in range(-1, 9):
        for c in range(3):
            x, n = apply0(V0, 2, c, z)
            V1[c, z + 1] = KEEP * x + WH[c, z + 2] * (BB[c, z + 2] + n)

    for z in range(4):
        for c in range(3):
            total = None
            for k in range(2):
                x, n = apply0(V1, 1, c, 2 * z + k)
                r = BB[c, 2 * z + k + 2] + n - DD[c, 2 * z + k] * x
                total = r[0:32] if total is None else total + r[0:32]
            RS[c, z] = total

    def row_pairs(ref, c, n):
        return jnp.concatenate(
            [ref[c, z, pl.ds(0, n, 2)] + ref[c, z, pl.ds(1, n, 2)] for z in range(ref.shape[1])], axis=0
        )

    r0, r1, r2 = (row_pairs(RS, c, 16) for c in range(3))
    new = [dot(r0, take_lo) + dot(r1, take_hi), dot(r2, take_lo)]
    for t in range(2):
        value = new[t].reshape(4, 16, 128)
        for z in range(4):
            BB1[t, z + 3, 0:16] = value[z]
            b1_stage[0, t, z] = value[z, 0:4]
            b1_stage[1, t, z] = value[z, 12:16]

    def b1_refs(dt, dh):
        if dt == 0:
            first = 4 if dh > 0 else 3
            return BB1.at[:, pl.ds(first, 3), pl.ds(0, 16)], b1_vert.at[0 if dh > 0 else 1]
        side = 0 if dt < 0 else 1
        if dh == 0:
            return b1_stage.at[side], b1_side.at[side, 0]
        first = 2 if dh > 0 else 0
        return (
            b1_stage.at[side, :, pl.ds(first, 2)],
            b1_side.at[side, 2 if dh > 0 else 1, :, pl.ds(first, 2)],
        )

    b1_moves = near_copies(b1_send, b1_recv, b1_refs)
    start(b1_moves)

    lane1 = iota((24, 128), 1)
    col1 = lane1 % 64
    wait_recv(q1_moves)

    def both(x):
        return jnp.where(iota(x.shape, len(x.shape) - 1) < 64, x, 0.0)

    for z in range(-4, 8):
        if z < 0:
            centre = jnp.where(below, q1_vert[0, z + 4], 0.0)
            lo = jnp.where(jnp.logical_and(below, before), q1_side[1, 2, z + 4], 0.0)
            hi = jnp.where(jnp.logical_and(below, after), q1_side[0, 2, z + 4], 0.0)
        elif z < 4:
            centre = q1[z]
            lo = jnp.where(before, q1_side[1, 1, z], 0.0)
            hi = jnp.where(after, q1_side[0, 1, z], 0.0)
        else:
            centre = jnp.where(above, q1_vert[1, z - 4], 0.0)
            lo = jnp.where(jnp.logical_and(above, before), q1_side[1, 0, z - 4], 0.0)
            hi = jnp.where(jnp.logical_and(above, after), q1_side[0, 0, z - 4], 0.0)
        q = jnp.concatenate([centre, hi, lo], axis=0)
        other = pltpu.roll(q, 64, 1)
        S1[z + 4] = jnp.where(lane1 < 64, q, other)
        if z == 0:
            spring1 = jnp.where(lane1 < 64, other, q)
    for z in range(-4, 7):
        HZ1[z + 4] = S1[z + 4] + S1[z + 5]
    for z in range(-3, 7):
        s = S1[z + 4]
        h_ru = s + pltpu.roll(s, 23, 0)
        h_rl = pltpu.roll(h_ru, 1, 0)
        f_cu = s + jnp.where(col1 < 63, pltpu.roll(s, 127, 1), 0.0)
        f_cl = s + jnp.where(col1 > 0, pltpu.roll(s, 1, 1), 0.0)
        HR1[0, z + 3] = h_rl
        HR1[1, z + 3] = h_ru
        HC1[0, z + 3] = jnp.where(col1 > 0, f_cl, 0.0)
        HC1[1, z + 3] = jnp.where(col1 < 63, f_cu, 0.0)
        f = [HZ1[z + 3] + HZ1[z + 4], h_rl + h_ru, f_cl + f_cu]
        total = f[0] + f[1] + f[2]
        if z == 0:
            total = total + spring1
        for t in range(2):
            d = total + (jnp.where(lane1 < 64, f[0], f[1]) if t == 0 else f[2])
            WH1[t, z + 3] = jnp.where(s > 0.0, OMEGA / jnp.where(s > 0.0, d, 1.0), 0.0)
            if 0 <= z < 4:
                DD1[t, z] = d

    wait_recv(b1_moves)
    for t in range(2):
        for z in range(-3, 7):
            if z < 0:
                BB1[t, z + 3, 0:16] = jnp.where(below, b1_vert[0, t, z + 3], 0.0)
                if z < -2:
                    lo = jnp.zeros((4, 128), F32)
                    hi = lo
                else:
                    lo = jnp.where(jnp.logical_and(below, before), b1_side[1, 2, t, z + 4], 0.0)
                    hi = jnp.where(jnp.logical_and(below, after), b1_side[0, 2, t, z + 4], 0.0)
            elif z < 4:
                lo = jnp.where(before, b1_side[1, 0, t, z], 0.0)
                hi = jnp.where(after, b1_side[0, 0, t, z], 0.0)
            else:
                BB1[t, z + 3, 0:16] = jnp.where(above, b1_vert[1, t, z - 4], 0.0)
                if z > 5:
                    lo = jnp.zeros((4, 128), F32)
                    hi = lo
                else:
                    lo = jnp.where(jnp.logical_and(above, before), b1_side[1, 1, t, z - 4], 0.0)
                    hi = jnp.where(jnp.logical_and(above, after), b1_side[0, 1, t, z - 4], 0.0)
            BB1[t, z + 3, 16:24] = jnp.concatenate([hi, lo], axis=0)

    for z in range(-3, 7):
        for t in range(2):
            VA1[t, z + 3] = WH1[t, z + 3] * BB1[t, z + 3]

    def apply1(v, off, t, z):
        x = v[t, z + off]
        a = HZ1[z + 3] * v[t, z + off - 1] + HZ1[z + 4] * v[t, z + off + 1]
        b = HR1[0, z + 3] * pltpu.roll(x, 1, 0) + HR1[1, z + 3] * pltpu.roll(x, 23, 0)
        e = HC1[0, z + 3] * pltpu.roll(x, 1, 1) + HC1[1, z + 3] * pltpu.roll(x, 127, 1)
        return x, (a + b + e) + (jnp.where(lane1 < 64, a, b) if t == 0 else e)

    for z in range(-2, 6):
        for t in range(2):
            x, n = apply1(VA1, 3, t, z)
            VB1[t, z + 2] = KEEP * x + WH1[t, z + 3] * (BB1[t, z + 3] + n)
    for z in range(2):
        for t in range(2):
            total = None
            for k in range(2):
                x, n = apply1(VB1, 2, t, 2 * z + k)
                r = BB1[t, 2 * z + k + 3] + n - DD1[t, 2 * z + k] * x
                total = r[0:16] if total is None else total + r[0:16]
            RS1[t, z] = total
    down_a = one_hot((128, 128), lambda l, j: l // 2 == j)
    down_b = one_hot((128, 128), lambda l, j: jnp.logical_and(l < 64, l // 2 == j - 64))
    b2_own[...] = (dot(row_pairs(RS1, 0, 8), down_a) + dot(row_pairs(RS1, 1, 8), down_b)).reshape(2, 8, 128)
    b2_moves = far_copies(b2_send, b2_recv, b2_own, b2)
    start(b2_moves)
    b2[pl.ds(2 * h, 2), 16:24] = b2_own[...]

    lane2 = iota((40, 128), 1)
    row2 = iota((40, 128), 0)
    col2 = lane2 % 32
    real = lane2 < 96
    slot = row2 // 8 + (i - 2)
    inside = jnp.logical_and(slot >= 0, slot < tiles)
    keep = jnp.logical_and(inside, real)
    wait_recv(q2_moves)

    def pick(a, b, e):
        return jnp.where(lane2 < 32, a, jnp.where(lane2 < 64, b, e))

    q = jnp.where(inside, q2[0], 0.0)
    spring2 = pick(pltpu.roll(q, 32, 1), pltpu.roll(q, 64, 1), pltpu.roll(q, 96, 1))
    odd_row, odd_col = row2 % 2 == 1, lane2 % 2 == 1

    def pair_sum(x):
        x = x + jnp.where(odd_row, pltpu.roll(x, 1, 0), pltpu.roll(x, 39, 0))
        return x + jnp.where(odd_col, pltpu.roll(x, 1, 1), pltpu.roll(x, 127, 1))

    def faces(s_of, depth, step, spring, hz, hr, hc, wh, dd):
        for z in range(depth - 1):
            hz[z] = s_of(z) + s_of(z + 1)
        for z in range(depth):
            s = s_of(z)
            h_ru = s + pltpu.roll(s, 40 - step, 0)
            h_rl = pltpu.roll(h_ru, step, 0)
            first, last = col2 < step, col2 >= 32 - step
            f_cu = s + jnp.where(last, 0.0, pltpu.roll(s, 128 - step, 1))
            f_cl = s + jnp.where(first, 0.0, pltpu.roll(s, step, 1))
            hr[0, z] = h_rl
            hr[1, z] = h_ru
            hc[0, z] = jnp.where(first, 0.0, f_cl)
            hc[1, z] = jnp.where(last, 0.0, f_cu)
            f_z = (hz[z - 1] if z > 0 else s) + (hz[z] if z < depth - 1 else s)
            f_r, f_c = h_rl + h_ru, f_cl + f_cu
            d = (f_z + f_r + f_c) + pick(f_z, f_r, f_c)
            if z == 0:
                d = d + spring
            wh[z] = jnp.where(s > 0.0, OMEGA / jnp.where(s > 0.0, d, 1.0), 0.0)
            if dd is not None:
                dd[z] = d

    def s2(z):
        return jnp.where(keep, q2[z], 0.0)

    faces(s2, 8, 1, spring2, HZ2, HR2, HC2, WH2, DD2)
    for z in range(4):
        S3[z] = 0.5 * pair_sum(s2(2 * z) + s2(2 * z + 1))
    faces(lambda z: S3[z], 4, 2, pair_sum(spring2), HZ3, HR3, HC3, WH3, None)

    def apply2(v, z, depth, step, hz, hr, hc):
        x = v[z]
        a = None
        if z > 0:
            a = hz[z - 1] * v[z - 1]
        if z < depth - 1:
            up = hz[z] * v[z + 1]
            a = up if a is None else a + up
        b = hr[0, z] * pltpu.roll(x, step, 0) + hr[1, z] * pltpu.roll(x, 40 - step, 0)
        e = hc[0, z] * pltpu.roll(x, step, 1) + hc[1, z] * pltpu.roll(x, 128 - step, 1)
        return x, (a + b + e) + pick(a, b, e)

    wait_recv(b2_moves)
    for z in range(8):
        b = jnp.where(keep, b2[z], 0.0)
        b2[z] = b
        VA2[z] = WH2[z] * b
    for z in range(8):
        x, n = apply2(VA2, z, 8, 1, HZ2, HR2, HC2)
        VB2[z] = KEEP * x + WH2[z] * (b2[z] + n)
    for z in range(4):
        total = None
        for k in range(2):
            x, n = apply2(VB2, 2 * z + k, 8, 1, HZ2, HR2, HC2)
            r = b2[2 * z + k] + n - DD2[2 * z + k] * x
            total = r if total is None else total + r
        total = pair_sum(total)
        BB3[z] = total
        V3[0, z] = WH3[z] * total
    for turn in range(5):
        now, later = turn % 2, (turn + 1) % 2
        for z in range(4):
            x, n = apply2(V3.at[now], z, 4, 2, HZ3, HR3, HC3)
            V3[later, z] = KEEP * x + WH3[z] * (BB3[z] + n)
    for z in range(8):
        VB2[z] = VB2[z] + V3[1, z // 2]
    PO2[0] = jnp.zeros((24, 128), F32)
    PO2[9] = jnp.zeros((24, 128), F32)
    for z in range(8):
        x, n = apply2(VB2, z, 8, 1, HZ2, HR2, HC2)
        PO2[z + 1] = (KEEP * x + WH2[z] * (b2[z] + n))[8:32]

    up_a = one_hot((128, 128), lambda l, j: l == j // 2)
    up_b = one_hot((128, 128), lambda l, j: jnp.logical_and(j < 64, l == 64 + j // 2))
    coarse = PO2[pl.ds(2 * h, 4)].reshape(96, 128)
    for t, m in enumerate((up_a, up_b)):
        e = dot(coarse, m).reshape(4, 24, 128)
        for k in range(4):
            T1[t, k, pl.ds(0, 24, 2)] = e[k]
            T1[t, k, pl.ds(1, 24, 2)] = e[k]
    for z in range(-2, 6):
        for t in range(2):
            k = (z + 2) // 2
            tail = jnp.where(sub8 < 4, T1[t, k, 32:40], T1[t, k, 8:16])
            e = jnp.concatenate([T1[t, k, 16:32], tail], axis=0)
            VB1[t, z + 2] = VB1[t, z + 2] + e
    for z in range(-1, 5):
        for t in range(2):
            x, n = apply1(VB1, 2, t, z)
            PO1[t, z + 1] = KEEP * x + WH1[t, z + 3] * (BB1[t, z + 3] + n)

    up_lo = one_hot((128, 128), lambda l, j: l == j // 2)
    up_hi = one_hot((128, 128), lambda l, j: l == 64 + j // 2)
    for c in range(3):
        e = dot(PO1[c // 2].reshape(144, 128), up_hi if c == 1 else up_lo).reshape(6, 24, 128)
        for k in range(6):
            T0[c, k, pl.ds(0, 24, 2)] = e[k]
            T0[c, k, pl.ds(1, 24, 2)] = e[k]
    for z in range(-1, 9):
        for c in range(3):
            k = (z + 2) // 2
            tail = jnp.where(sub8 < 4, T0[c, k, 32:40], T0[c, k, 40:48])
            V1[c, z + 1] = V1[c, z + 1] + jnp.concatenate([T0[c, k, 0:32], tail], axis=0)
    for z in range(8):
        for c in range(3):
            x, n = apply0(V1, 1, c, z)
            out[c, z] = (KEEP * x + WH[c, z + 2] * (BB[c, z + 2] + n))[0:32]

    for moves in (label_moves, q1_moves, q2_moves, b1_moves, b2_moves):
        wait_send(moves)


def solution(mesh):
    heights, tiles = mesh.shape["height"], mesh.shape["tile"]

    def vmem(*shape, dtype=F32):
        return pltpu.VMEM(shape, dtype)

    i32 = jnp.int32
    scratch = [
        vmem(8, 32, 128, dtype=i32), vmem(2, 32, 128, dtype=i32),
        vmem(3, 32, 128, dtype=i32), vmem(3, 32, 128, dtype=i32),
        vmem(2, 10, 4, 128, dtype=i32), vmem(2, 2, 2, 4, 128, dtype=i32), vmem(2, 10, 4, 128, dtype=i32),
        vmem(4, 16, 128), vmem(2, 4, 16, 128), vmem(2, 3, 4, 4, 128), vmem(2, 4, 4, 128),
        vmem(8, 40, 128), vmem(2, 8, 128),
        vmem(2, 2, 3, 16, 128), vmem(2, 3, 2, 4, 4, 128), vmem(2, 2, 4, 4, 128),
        vmem(8, 40, 128), vmem(2, 8, 128),
        vmem(14, 40, 128), vmem(3, 14, 40, 128), vmem(13, 40, 128), vmem(2, 12, 40, 128), vmem(2, 12, 40, 128),
        vmem(3, 12, 40, 128), vmem(3, 12, 40, 128), vmem(3, 8, 40, 128), vmem(3, 12, 40, 128),
        vmem(3, 10, 40, 128), vmem(3, 4, 32, 128),
        vmem(12, 24, 128), vmem(11, 24, 128), vmem(2, 10, 24, 128), vmem(2, 10, 24, 128), vmem(2, 10, 24, 128),
        vmem(2, 10, 24, 128), vmem(2, 4, 24, 128), vmem(2, 10, 24, 128), vmem(2, 8, 24, 128),
        vmem(2, 2, 16, 128), vmem(2, 6, 24, 128),
        vmem(7, 40, 128), vmem(2, 8, 40, 128), vmem(2, 8, 40, 128), vmem(8, 40, 128), vmem(8, 40, 128),
        vmem(8, 40, 128), vmem(8, 40, 128), vmem(10, 24, 128), vmem(2, 4, 48, 128),
        vmem(4, 40, 128), vmem(3, 40, 128), vmem(2, 4, 40, 128), vmem(2, 4, 40, 128), vmem(4, 40, 128),
        vmem(4, 40, 128), vmem(2, 4, 40, 128),
        vmem(3, 6, 48, 128), vmem(2, 4, 32, 128),
        pltpu.SemaphoreType.DMA((2,)),
    ]
    for count in (8, 8, 19, 8, 19):
        scratch += [pltpu.SemaphoreType.DMA((count,)), pltpu.SemaphoreType.DMA((count,))]

    def local(material, clamped, stiffness_table, eigenstrain):
        return pl.pallas_call(
            functools.partial(kernel, heights, tiles),
            out_shape=jax.ShapeDtypeStruct((3, 8, 32, 128), F32),
            in_specs=[
                pl.BlockSpec(memory_space=pl.ANY),
                pl.BlockSpec(memory_space=pl.ANY),
                pl.BlockSpec(memory_space=pltpu.SMEM),
                pl.BlockSpec(memory_space=pltpu.SMEM),
            ],
            out_specs=pl.BlockSpec(memory_space=pltpu.VMEM),
            scratch_shapes=scratch,
            compiler_params=pltpu.CompilerParams(
                collective_id=0, has_side_effects=True, vmem_limit_bytes=40 * 1024 * 1024
            ),
        )(material, clamped, stiffness_table, eigenstrain)

    in_specs = (P("height", "tile", None), P("height", "tile", None), P(), P())
    out_specs = P(None, "height", "tile", None)
    return jax.shard_map(local, mesh=mesh, in_specs=in_specs, out_specs=out_specs, check_vma=False)
```

```python
import functools

import jax
import jax.numpy as jnp
from jax import lax
from jax.experimental import pallas as pl
from jax.experimental.pallas import tpu as pltpu
from jax.sharding import PartitionSpec as P

PENALTY = 50.0
OMEGA = 0.6
KEEP = 1.0 - OMEGA
F32 = jnp.float32
HI = lax.Precision.HIGHEST
NEAR = ((-1, -1), (-1, 1), (1, -1), (1, 1), (-1, 0), (1, 0), (0, -1), (0, 1))
FAR = tuple(
    sorted(
        ((dt, k) for dt in (-2, -1, 0, 1, 2) for k in (0, 1, 2, 3) if (dt, k) != (0, 0)),
        key=lambda move: (-abs(move[0]), -min(move[1], 4 - move[1]), move),
    )
)


def iota(shape, axis):
    return lax.broadcasted_iota(jnp.int32, shape, axis)


def one_hot(shape, cond):
    return jnp.where(cond(iota(shape, 0), iota(shape, 1)), 1.0, 0.0).astype(F32)


def dot(a, b):
    return jnp.dot(a, b, preferred_element_type=F32, precision=HI)


def kernel(
    heights,
    tiles,
    mat_hbm,
    clamp_hbm,
    table_hbm,
    eigen_hbm,
    out,
    table,
    eigen,
    mat,
    cl,
    m_lo, m_hi, m_side, m_corner, m_stage,
    q1, q1_vert, q1_side, q1_stage,
    q2, q2_own,
    b1_vert, b1_side, b1_stage,
    b2, b2_own,
    S, SG, HZ, HR, HC, BB, WH, DD, V0, V1, RS,
    S1, HZ1, HR1, HC1, BB1, WH1, DD1, VA1, VB1, RS1, PO1,
    HZ2, HR2, HC2, WH2, DD2, VA2, VB2, PO2, T1,
    S3, HZ3, HR3, HC3, WH3, BB3, V3,
    T0, R4,
    local_sem,
    m_send, m_recv, q1_send, q1_recv, q2_send, q2_recv, b1_send, b1_recv, b2_send, b2_recv,
):
    i = lax.axis_index("tile")
    h = lax.axis_index("height")

    in_mat = pltpu.make_async_copy(mat_hbm, mat, local_sem.at[0])
    in_cl = pltpu.make_async_copy(clamp_hbm.at[pl.ds(0, 2)], cl, local_sem.at[1])
    in_table = pltpu.make_async_copy(table_hbm, table, local_sem.at[2])
    in_eigen = pltpu.make_async_copy(eigen_hbm, eigen, local_sem.at[3])

    def tile_ok(dt):
        return jnp.logical_and(i + dt >= 0, i + dt < tiles)

    def near_ok(dt, dh):
        return jnp.logical_and(tile_ok(dt), jnp.logical_and(h + dh >= 0, h + dh < heights))

    def far_id(dt, k):
        return {"tile": i + dt, "height": lax.rem(h + k, heights)}

    in_mat.start()
    barrier = pltpu.get_barrier_semaphore()
    for dt, k in FAR:
        @pl.when(tile_ok(dt))
        def _():
            pl.semaphore_signal(
                barrier, inc=1, device_id=far_id(dt, k), device_id_type=pl.DeviceIdType.MESH
            )
    reach = sum(tile_ok(dt).astype(jnp.int32) for dt in (-2, -1, 0, 1, 2))

    in_cl.start()
    in_table.start()
    in_eigen.start()
    in_mat.wait()
    in_cl.wait()
    for z in range(8):
        m_stage[0, z] = mat[z, 0:4]
        m_stage[1, z] = mat[z, 28:32]
    for z in range(2):
        m_stage[0, 8 + z] = cl[z, 0:4]
        m_stage[1, 8 + z] = cl[z, 28:32]

    pl.semaphore_wait(barrier, 4 * reach - 1)

    def near_copies(send, recv, refs):
        copies = []
        for k, (dt, dh) in enumerate(NEAR):
            src, dst = refs(dt, dh)
            copy = pltpu.make_async_remote_copy(
                src_ref=src, dst_ref=dst, send_sem=send.at[k], recv_sem=recv.at[k],
                device_id={"tile": i + dt, "height": h + dh},
                device_id_type=pl.DeviceIdType.MESH,
            )
            copies.append((copy, near_ok(dt, dh), near_ok(-dt, -dh)))
        return copies

    def far_copies(send, recv, own, field):
        copies = []
        for k, (dt, dh) in enumerate(FAR):
            copy = pltpu.make_async_remote_copy(
                src_ref=own,
                dst_ref=field.at[pl.ds(2 * h, 2), pl.ds(8 * (2 - dt), 8)],
                send_sem=send.at[k], recv_sem=recv.at[k],
                device_id=far_id(dt, dh), device_id_type=pl.DeviceIdType.MESH,
            )
            copies.append((copy, tile_ok(dt), tile_ok(-dt)))
        return copies

    def start(copies):
        for copy, sends, _ in copies:
            @pl.when(sends)
            def _():
                copy.start()

    def wait_recv(copies):
        for copy, _, receives in copies:
            @pl.when(receives)
            def _():
                copy.wait_recv()

    def wait_send(copies):
        for copy, sends, _ in copies:
            @pl.when(sends)
            def _():
                copy.wait_send()

    def label_refs(dt, dh):
        if dt == 0:
            return (mat.at[pl.ds(5, 3)], m_lo) if dh > 0 else (mat.at[pl.ds(0, 3)], m_hi)
        side = 0 if dt < 0 else 1
        if dh == 0:
            return m_stage.at[side], m_side.at[side]
        first = 6 if dh > 0 else 0
        return m_stage.at[side, pl.ds(first, 2)], m_corner.at[side, 0 if dh < 0 else 1]

    label_moves = near_copies(m_send, m_recv, label_refs)
    start(label_moves)

    in_table.wait()
    in_eigen.wait()

    st = [table[n] for n in range(3)]
    stress = [[table[n] * eigen[n, c] for c in range(3)] for n in range(3)]

    def look(m, values):
        return jnp.where(
            m == 0, values[0], jnp.where(m == 1, values[1], jnp.where(m == 2, values[2], 0.0))
        )

    take_lo = one_hot((128, 128), lambda l, j: jnp.logical_and(j < 64, l // 2 == j))
    take_hi = one_hot((128, 128), lambda l, j: l // 2 == j - 64)
    lowest = jnp.where(h == 0, 1.0, 0.0).astype(F32)

    for z in range(4):
        R4[0, z] = look(mat[2 * z], st) + look(mat[2 * z + 1], st)
    R4[1, 0] = (cl[0] + cl[1]).astype(F32)
    s_rows = jnp.concatenate(
        [R4[0, z, pl.ds(0, 16, 2)] + R4[0, z, pl.ds(1, 16, 2)] for z in range(4)], axis=0
    )
    p_rows = R4[1, 0, pl.ds(0, 16, 2)] + R4[1, 0, pl.ds(1, 16, 2)]
    s_one = dot(0.5 * s_rows, take_lo).reshape(4, 16, 128)
    p_one = dot((2.0 * PENALTY * lowest) * p_rows, take_hi)
    q1[0] = s_one[0] + p_one
    for z in range(1, 4):
        q1[z] = s_one[z]
    for z in range(4):
        q1_stage[0, z] = q1[z, 0:4]
        q1_stage[1, z] = q1[z, 12:16]

    def q1_refs(dt, dh):
        if dt == 0:
            return q1, q1_vert.at[0 if dh > 0 else 1]
        side = 0 if dt < 0 else 1
        return q1_stage.at[side], q1_side.at[side, dh + 1]

    q1_moves = near_copies(q1_send, q1_recv, q1_refs)
    start(q1_moves)

    for z in range(2):
        R4[1, z, 0:16] = q1[2 * z] + q1[2 * z + 1]
    q_rows = jnp.concatenate(
        [R4[1, z, pl.ds(0, 8, 2)] + R4[1, z, pl.ds(1, 8, 2)] for z in range(2)], axis=0
    )
    l, j = iota((128, 128), 0), iota((128, 128), 1)
    down_q = jnp.where(
        jnp.logical_and(j < 96, jnp.logical_and(l < 64, l // 2 == j % 32)), 0.5,
        jnp.where(jnp.logical_and(j >= 96, l // 2 == j - 64), 1.0, 0.0),
    ).astype(F32)
    q2_own[...] = dot(q_rows, down_q).reshape(2, 8, 128)
    q2_moves = far_copies(q2_send, q2_recv, q2_own, q2)
    start(q2_moves)
    q2[pl.ds(2 * h, 2), 16:24] = q2_own[...]

    lane = iota((40, 128), 1)
    sub8 = iota((8, 128), 0)
    wait_recv(label_moves)
    below, above = h > 0, h < heights - 1
    before, after = i > 0, i < tiles - 1

    def side_rows(z, ref_of):
        lo_ok, lo = ref_of(1)
        hi_ok, hi = ref_of(0)
        return jnp.concatenate([jnp.where(hi_ok, hi, -1), jnp.where(lo_ok, lo, -1)], axis=0)

    def labels(z):
        if z < 0:
            centre = jnp.where(below, m_lo[z + 3], -1)
            if z < -2:
                return jnp.concatenate([centre, jnp.full((8, 128), -1, jnp.int32)], axis=0)
            sides = side_rows(
                z, lambda s: (jnp.logical_and(below, before if s else after), m_corner[s, 1, z + 2])
            )
        elif z < 8:
            centre = mat[z]
            sides = side_rows(z, lambda s: (before if s else after, m_side[s, z]))
        else:
            centre = jnp.where(above, m_hi[z - 8], -1)
            if z > 9:
                return jnp.concatenate([centre, jnp.full((8, 128), -1, jnp.int32)], axis=0)
            sides = side_rows(
                z, lambda s: (jnp.logical_and(above, before if s else after), m_corner[s, 0, z - 8])
            )
        return jnp.concatenate([centre, sides], axis=0)

    for z in range(-3, 11):
        m = labels(z)
        S[z + 3] = look(m, st)
        for c in range(3):
            SG[c, z + 3] = look(m, [stress[n][c] for n in range(3)])
    for z in range(-3, 10):
        HZ[z + 3] = S[z + 3] + S[z + 4]

    def spring0(z):
        sides = jnp.concatenate(
            [jnp.where(after, m_side[0, 8 + z], 0), jnp.where(before, m_side[1, 8 + z], 0)], axis=0
        )
        return (2.0 * PENALTY * lowest) * jnp.concatenate([cl[z], sides], axis=0).astype(F32)

    for z in range(-2, 10):
        s = S[z + 3]
        s_r = pltpu.roll(s, 39, 0)
        s_c = jnp.where(lane < 127, pltpu.roll(s, 127, 1), 0.0)
        h_ru = s + s_r
        h_rl = pltpu.roll(h_ru, 1, 0)
        f_cu = s + s_c
        f_cl = s + jnp.where(lane > 0, pltpu.roll(s, 1, 1), 0.0)
        HR[0, z + 2] = h_rl
        HR[1, z + 2] = h_ru
        HC[0, z + 2] = jnp.where(lane > 0, f_cl, 0.0)
        HC[1, z + 2] = jnp.where(lane < 127, f_cu, 0.0)
        f = [HZ[z + 2] + HZ[z + 3], h_rl + h_ru, f_cl + f_cu]
        total = f[0] + f[1] + f[2]
        if 0 <= z < 2:
            total = total + spring0(z)
        g0 = SG[0, z + 2] - SG[0, z + 4]
        x = SG[1, z + 3]
        g1 = pltpu.roll(x, 1, 0) - pltpu.roll(x, 39, 0)
        x = SG[2, z + 3]
        g2 = jnp.where(lane > 0, pltpu.roll(x, 1, 1), 0.0) - jnp.where(
            lane < 127, pltpu.roll(x, 127, 1), 0.0
        )
        for c, g in enumerate((g0, g1, g2)):
            d = total + f[c]
            w = jnp.where(s > 0.0, OMEGA / jnp.where(s > 0.0, d, 1.0), 0.0)
            BB[c, z + 2] = g
            WH[c, z + 2] = w
            if 0 <= z < 8:
                DD[c, z] = d
            V0[c, z + 2] = w * g

    def apply0(v, off, c, z):
        x = v[c, z + off]
        a = HZ[z + 2] * v[c, z + off - 1] + HZ[z + 3] * v[c, z + off + 1]
        b = HR[0, z + 2] * pltpu.roll(x, 1, 0) + HR[1, z + 2] * pltpu.roll(x, 39, 0)
        e = HC[0, z + 2] * pltpu.roll(x, 1, 1) + HC[1, z + 2] * pltpu.roll(x, 127, 1)
        return x, (a + b + e) + (a, b, e)[c]

    for z in range(-1, 9):
        for c in range(3):
            x, n = apply0(V0, 2, c, z)
            V1[c, z + 1] = KEEP * x + WH[c, z + 2] * (BB[c, z + 2] + n)

    for z in range(4):
        for c in range(3):
            total = None
            for k in range(2):
                x, n = apply0(V1, 1, c, 2 * z + k)
                r = BB[c, 2 * z + k + 2] + n - DD[c, 2 * z + k] * x
                total = r[0:32] if total is None else total + r[0:32]
            RS[c, z] = total

    def row_pairs(ref, c, n):
        return jnp.concatenate(
            [ref[c, z, pl.ds(0, n, 2)] + ref[c, z, pl.ds(1, n, 2)] for z in range(ref.shape[1])], axis=0
        )

    r0, r1, r2 = (row_pairs(RS, c, 16) for c in range(3))
    new = [dot(r0, take_lo) + dot(r1, take_hi), dot(r2, take_lo)]
    for t in range(2):
        value = new[t].reshape(4, 16, 128)
        for z in range(4):
            BB1[t, z + 3, 0:16] = value[z]
            b1_stage[0, t, z] = value[z, 0:4]
            b1_stage[1, t, z] = value[z, 12:16]

    def b1_refs(dt, dh):
        if dt == 0:
            first = 4 if dh > 0 else 3
            return BB1.at[:, pl.ds(first, 3), pl.ds(0, 16)], b1_vert.at[0 if dh > 0 else 1]
        side = 0 if dt < 0 else 1
        if dh == 0:
            return b1_stage.at[side], b1_side.at[side, 0]
        first = 2 if dh > 0 else 0
        return (
            b1_stage.at[side, :, pl.ds(first, 2)],
            b1_side.at[side, 2 if dh > 0 else 1, :, pl.ds(first, 2)],
        )

    b1_moves = near_copies(b1_send, b1_recv, b1_refs)
    start(b1_moves)

    lane1 = iota((24, 128), 1)
    col1 = lane1 % 64
    wait_recv(q1_moves)

    def both(x):
        return jnp.where(iota(x.shape, len(x.shape) - 1) < 64, x, 0.0)

    for z in range(-4, 8):
        if z < 0:
            centre = jnp.where(below, q1_vert[0, z + 4], 0.0)
            lo = jnp.where(jnp.logical_and(below, before), q1_side[1, 2, z + 4], 0.0)
            hi = jnp.where(jnp.logical_and(below, after), q1_side[0, 2, z + 4], 0.0)
        elif z < 4:
            centre = q1[z]
            lo = jnp.where(before, q1_side[1, 1, z], 0.0)
            hi = jnp.where(after, q1_side[0, 1, z], 0.0)
        else:
            centre = jnp.where(above, q1_vert[1, z - 4], 0.0)
            lo = jnp.where(jnp.logical_and(above, before), q1_side[1, 0, z - 4], 0.0)
            hi = jnp.where(jnp.logical_and(above, after), q1_side[0, 0, z - 4], 0.0)
        q = jnp.concatenate([centre, hi, lo], axis=0)
        other = pltpu.roll(q, 64, 1)
        S1[z + 4] = jnp.where(lane1 < 64, q, other)
        if z == 0:
            spring1 = jnp.where(lane1 < 64, other, q)
    for z in range(-4, 7):
        HZ1[z + 4] = S1[z + 4] + S1[z + 5]
    for z in range(-3, 7):
        s = S1[z + 4]
        h_ru = s + pltpu.roll(s, 23, 0)
        h_rl = pltpu.roll(h_ru, 1, 0)
        f_cu = s + jnp.where(col1 < 63, pltpu.roll(s, 127, 1), 0.0)
        f_cl = s + jnp.where(col1 > 0, pltpu.roll(s, 1, 1), 0.0)
        HR1[0, z + 3] = h_rl
        HR1[1, z + 3] = h_ru
        HC1[0, z + 3] = jnp.where(col1 > 0, f_cl, 0.0)
        HC1[1, z + 3] = jnp.where(col1 < 63, f_cu, 0.0)
        f = [HZ1[z + 3] + HZ1[z + 4], h_rl + h_ru, f_cl + f_cu]
        total = f[0] + f[1] + f[2]
        if z == 0:
            total = total + spring1
        for t in range(2):
            d = total + (jnp.where(lane1 < 64, f[0], f[1]) if t == 0 else f[2])
            WH1[t, z + 3] = jnp.where(s > 0.0, OMEGA / jnp.where(s > 0.0, d, 1.0), 0.0)
            if 0 <= z < 4:
                DD1[t, z] = d

    wait_recv(b1_moves)
    for t in range(2):
        for z in range(-3, 7):
            if z < 0:
                BB1[t, z + 3, 0:16] = jnp.where(below, b1_vert[0, t, z + 3], 0.0)
                if z < -2:
                    lo = jnp.zeros((4, 128), F32)
                    hi = lo
                else:
                    lo = jnp.where(jnp.logical_and(below, before), b1_side[1, 2, t, z + 4], 0.0)
                    hi = jnp.where(jnp.logical_and(below, after), b1_side[0, 2, t, z + 4], 0.0)
            elif z < 4:
                lo = jnp.where(before, b1_side[1, 0, t, z], 0.0)
                hi = jnp.where(after, b1_side[0, 0, t, z], 0.0)
            else:
                BB1[t, z + 3, 0:16] = jnp.where(above, b1_vert[1, t, z - 4], 0.0)
                if z > 5:
                    lo = jnp.zeros((4, 128), F32)
                    hi = lo
                else:
                    lo = jnp.where(jnp.logical_and(above, before), b1_side[1, 1, t, z - 4], 0.0)
                    hi = jnp.where(jnp.logical_and(above, after), b1_side[0, 1, t, z - 4], 0.0)
            BB1[t, z + 3, 16:24] = jnp.concatenate([hi, lo], axis=0)

    for z in range(-3, 7):
        for t in range(2):
            VA1[t, z + 3] = WH1[t, z + 3] * BB1[t, z + 3]

    def apply1(v, off, t, z):
        x = v[t, z + off]
        a = HZ1[z + 3] * v[t, z + off - 1] + HZ1[z + 4] * v[t, z + off + 1]
        b = HR1[0, z + 3] * pltpu.roll(x, 1, 0) + HR1[1, z + 3] * pltpu.roll(x, 23, 0)
        e = HC1[0, z + 3] * pltpu.roll(x, 1, 1) + HC1[1, z + 3] * pltpu.roll(x, 127, 1)
        return x, (a + b + e) + (jnp.where(lane1 < 64, a, b) if t == 0 else e)

    for z in range(-2, 6):
        for t in range(2):
            x, n = apply1(VA1, 3, t, z)
            VB1[t, z + 2] = KEEP * x + WH1[t, z + 3] * (BB1[t, z + 3] + n)
    for z in range(2):
        for t in range(2):
            total = None
            for k in range(2):
                x, n = apply1(VB1, 2, t, 2 * z + k)
                r = BB1[t, 2 * z + k + 3] + n - DD1[t, 2 * z + k] * x
                total = r[0:16] if total is None else total + r[0:16]
            RS1[t, z] = total
    down_a = one_hot((128, 128), lambda l, j: l // 2 == j)
    down_b = one_hot((128, 128), lambda l, j: jnp.logical_and(l < 64, l // 2 == j - 64))
    b2_own[...] = (dot(row_pairs(RS1, 0, 8), down_a) + dot(row_pairs(RS1, 1, 8), down_b)).reshape(2, 8, 128)
    b2_moves = far_copies(b2_send, b2_recv, b2_own, b2)
    start(b2_moves)
    b2[pl.ds(2 * h, 2), 16:24] = b2_own[...]

    lane2 = iota((40, 128), 1)
    row2 = iota((40, 128), 0)
    col2 = lane2 % 32
    real = lane2 < 96
    slot = row2 // 8 + (i - 2)
    inside = jnp.logical_and(slot >= 0, slot < tiles)
    keep = jnp.logical_and(inside, real)
    wait_recv(q2_moves)

    def pick(a, b, e):
        return jnp.where(lane2 < 32, a, jnp.where(lane2 < 64, b, e))

    q = jnp.where(inside, q2[0], 0.0)
    spring2 = pick(pltpu.roll(q, 32, 1), pltpu.roll(q, 64, 1), pltpu.roll(q, 96, 1))
    odd_row, odd_col = row2 % 2 == 1, lane2 % 2 == 1

    def pair_sum(x):
        x = x + jnp.where(odd_row, pltpu.roll(x, 1, 0), pltpu.roll(x, 39, 0))
        return x + jnp.where(odd_col, pltpu.roll(x, 1, 1), pltpu.roll(x, 127, 1))

    def faces(s_of, depth, step, spring, hz, hr, hc, wh, dd):
        for z in range(depth - 1):
            hz[z] = s_of(z) + s_of(z + 1)
        for z in range(depth):
            s = s_of(z)
            h_ru = s + pltpu.roll(s, 40 - step, 0)
            h_rl = pltpu.roll(h_ru, step, 0)
            first, last = col2 < step, col2 >= 32 - step
            f_cu = s + jnp.where(last, 0.0, pltpu.roll(s, 128 - step, 1))
            f_cl = s + jnp.where(first, 0.0, pltpu.roll(s, step, 1))
            hr[0, z] = h_rl
            hr[1, z] = h_ru
            hc[0, z] = jnp.where(first, 0.0, f_cl)
            hc[1, z] = jnp.where(last, 0.0, f_cu)
            f_z = (hz[z - 1] if z > 0 else s) + (hz[z] if z < depth - 1 else s)
            f_r, f_c = h_rl + h_ru, f_cl + f_cu
            d = (f_z + f_r + f_c) + pick(f_z, f_r, f_c)
            if z == 0:
                d = d + spring
            wh[z] = jnp.where(s > 0.0, OMEGA / jnp.where(s > 0.0, d, 1.0), 0.0)
            if dd is not None:
                dd[z] = d

    def s2(z):
        return jnp.where(keep, q2[z], 0.0)

    faces(s2, 8, 1, spring2, HZ2, HR2, HC2, WH2, DD2)
    for z in range(4):
        S3[z] = 0.5 * pair_sum(s2(2 * z) + s2(2 * z + 1))
    faces(lambda z: S3[z], 4, 2, pair_sum(spring2), HZ3, HR3, HC3, WH3, None)

    def apply2(v, z, depth, step, hz, hr, hc):
        x = v[z]
        a = None
        if z > 0:
            a = hz[z - 1] * v[z - 1]
        if z < depth - 1:
            up = hz[z] * v[z + 1]
            a = up if a is None else a + up
        b = hr[0, z] * pltpu.roll(x, step, 0) + hr[1, z] * pltpu.roll(x, 40 - step, 0)
        e = hc[0, z] * pltpu.roll(x, step, 1) + hc[1, z] * pltpu.roll(x, 128 - step, 1)
        return x, (a + b + e) + pick(a, b, e)

    wait_recv(b2_moves)
    for z in range(8):
        b = jnp.where(keep, b2[z], 0.0)
        b2[z] = b
        VA2[z] = WH2[z] * b
    for z in range(8):
        x, n = apply2(VA2, z, 8, 1, HZ2, HR2, HC2)
        VB2[z] = KEEP * x + WH2[z] * (b2[z] + n)
    for z in range(4):
        total = None
        for k in range(2):
            x, n = apply2(VB2, 2 * z + k, 8, 1, HZ2, HR2, HC2)
            r = b2[2 * z + k] + n - DD2[2 * z + k] * x
            total = r if total is None else total + r
        total = pair_sum(total)
        BB3[z] = total
        V3[0, z] = WH3[z] * total
    for turn in range(5):
        now, later = turn % 2, (turn + 1) % 2
        for z in range(4):
            x, n = apply2(V3.at[now], z, 4, 2, HZ3, HR3, HC3)
            V3[later, z] = KEEP * x + WH3[z] * (BB3[z] + n)
    for z in range(8):
        VB2[z] = VB2[z] + V3[1, z // 2]
    PO2[0] = jnp.zeros((24, 128), F32)
    PO2[9] = jnp.zeros((24, 128), F32)
    for z in range(8):
        x, n = apply2(VB2, z, 8, 1, HZ2, HR2, HC2)
        PO2[z + 1] = (KEEP * x + WH2[z] * (b2[z] + n))[8:32]

    up_a = one_hot((128, 128), lambda l, j: l == j // 2)
    up_b = one_hot((128, 128), lambda l, j: jnp.logical_and(j < 64, l == 64 + j // 2))
    coarse = PO2[pl.ds(2 * h, 4)].reshape(96, 128)
    for t, m in enumerate((up_a, up_b)):
        e = dot(coarse, m).reshape(4, 24, 128)
        for k in range(4):
            T1[t, k, pl.ds(0, 24, 2)] = e[k]
            T1[t, k, pl.ds(1, 24, 2)] = e[k]
    for z in range(-2, 6):
        for t in range(2):
            k = (z + 2) // 2
            tail = jnp.where(sub8 < 4, T1[t, k, 32:40], T1[t, k, 8:16])
            e = jnp.concatenate([T1[t, k, 16:32], tail], axis=0)
            VB1[t, z + 2] = VB1[t, z + 2] + e
    for z in range(-1, 5):
        for t in range(2):
            x, n = apply1(VB1, 2, t, z)
            PO1[t, z + 1] = KEEP * x + WH1[t, z + 3] * (BB1[t, z + 3] + n)

    up_lo = one_hot((128, 128), lambda l, j: l == j // 2)
    up_hi = one_hot((128, 128), lambda l, j: l == 64 + j // 2)
    for c in range(3):
        e = dot(PO1[c // 2].reshape(144, 128), up_hi if c == 1 else up_lo).reshape(6, 24, 128)
        for k in range(6):
            T0[c, k, pl.ds(0, 24, 2)] = e[k]
            T0[c, k, pl.ds(1, 24, 2)] = e[k]
    for z in range(-1, 9):
        for c in range(3):
            k = (z + 2) // 2
            tail = jnp.where(sub8 < 4, T0[c, k, 32:40], T0[c, k, 40:48])
            V1[c, z + 1] = V1[c, z + 1] + jnp.concatenate([T0[c, k, 0:32], tail], axis=0)
    for z in range(8):
        for c in range(3):
            x, n = apply0(V1, 1, c, z)
            out[c, z] = (KEEP * x + WH[c, z + 2] * (BB[c, z + 2] + n))[0:32]

    for moves in (label_moves, q1_moves, q2_moves, b1_moves, b2_moves):
        wait_send(moves)


def solution(mesh):
    heights, tiles = mesh.shape["height"], mesh.shape["tile"]

    def vmem(*shape, dtype=F32):
        return pltpu.VMEM(shape, dtype)

    i32 = jnp.int32
    scratch = [
        pltpu.SMEM((3,), F32), pltpu.SMEM((3, 3), F32),
        vmem(8, 32, 128, dtype=i32), vmem(2, 32, 128, dtype=i32),
        vmem(3, 32, 128, dtype=i32), vmem(3, 32, 128, dtype=i32),
        vmem(2, 10, 4, 128, dtype=i32), vmem(2, 2, 2, 4, 128, dtype=i32), vmem(2, 10, 4, 128, dtype=i32),
        vmem(4, 16, 128), vmem(2, 4, 16, 128), vmem(2, 3, 4, 4, 128), vmem(2, 4, 4, 128),
        vmem(8, 40, 128), vmem(2, 8, 128),
        vmem(2, 2, 3, 16, 128), vmem(2, 3, 2, 4, 4, 128), vmem(2, 2, 4, 4, 128),
        vmem(8, 40, 128), vmem(2, 8, 128),
        vmem(14, 40, 128), vmem(3, 14, 40, 128), vmem(13, 40, 128), vmem(2, 12, 40, 128), vmem(2, 12, 40, 128),
        vmem(3, 12, 40, 128), vmem(3, 12, 40, 128), vmem(3, 8, 40, 128), vmem(3, 12, 40, 128),
        vmem(3, 10, 40, 128), vmem(3, 4, 32, 128),
        vmem(12, 24, 128), vmem(11, 24, 128), vmem(2, 10, 24, 128), vmem(2, 10, 24, 128), vmem(2, 10, 24, 128),
        vmem(2, 10, 24, 128), vmem(2, 4, 24, 128), vmem(2, 10, 24, 128), vmem(2, 8, 24, 128),
        vmem(2, 2, 16, 128), vmem(2, 6, 24, 128),
        vmem(7, 40, 128), vmem(2, 8, 40, 128), vmem(2, 8, 40, 128), vmem(8, 40, 128), vmem(8, 40, 128),
        vmem(8, 40, 128), vmem(8, 40, 128), vmem(10, 24, 128), vmem(2, 4, 48, 128),
        vmem(4, 40, 128), vmem(3, 40, 128), vmem(2, 4, 40, 128), vmem(2, 4, 40, 128), vmem(4, 40, 128),
        vmem(4, 40, 128), vmem(2, 4, 40, 128),
        vmem(3, 6, 48, 128), vmem(2, 4, 32, 128),
        pltpu.SemaphoreType.DMA((4,)),
    ]
    for count in (8, 8, 19, 8, 19):
        scratch += [pltpu.SemaphoreType.DMA((count,)), pltpu.SemaphoreType.DMA((count,))]

    def local(material, clamped, stiffness_table, eigenstrain):
        return pl.pallas_call(
            functools.partial(kernel, heights, tiles),
            out_shape=jax.ShapeDtypeStruct((3, 8, 32, 128), F32),
            in_specs=[
                pl.BlockSpec(memory_space=pltpu.HBM),
                pl.BlockSpec(memory_space=pltpu.HBM),
                pl.BlockSpec(memory_space=pltpu.HBM),
                pl.BlockSpec(memory_space=pltpu.HBM),
            ],
            out_specs=pl.BlockSpec(memory_space=pltpu.VMEM),
            scratch_shapes=scratch,
            compiler_params=pltpu.CompilerParams(
                collective_id=0, has_side_effects=True, vmem_limit_bytes=40 * 1024 * 1024
            ),
        )(*(pltpu.with_memory_space_constraint(x, pltpu.HBM) for x in (material, clamped, stiffness_table, eigenstrain)))

    in_specs = (P("height", "tile", None), P("height", "tile", None), P(), P())
    out_specs = P(None, "height", "tile", None)
    return jax.shard_map(local, mesh=mesh, in_specs=in_specs, out_specs=out_specs, check_vma=False)
```

```python
import functools

import jax
import jax.numpy as jnp
from jax import lax
from jax.experimental import pallas as pl
from jax.experimental.pallas import tpu as pltpu
from jax.sharding import PartitionSpec as P

PENALTY = 50.0
OMEGA = 0.6
KEEP = 1.0 - OMEGA
F32 = jnp.float32
HI = lax.Precision.HIGHEST
NEAR = ((-1, -1), (-1, 1), (1, -1), (1, 1), (-1, 0), (1, 0), (0, -1), (0, 1))
FAR = tuple(
    sorted(
        ((dt, k) for dt in (-2, -1, 0, 1, 2) for k in (0, 1, 2, 3) if (dt, k) != (0, 0)),
        key=lambda move: (-abs(move[0]), -min(move[1], 4 - move[1]), move),
    )
)


def iota(shape, axis):
    return lax.broadcasted_iota(jnp.int32, shape, axis)


def one_hot(shape, cond):
    return jnp.where(cond(iota(shape, 0), iota(shape, 1)), 1.0, 0.0).astype(F32)


def dot(a, b):
    return jnp.dot(a, b, preferred_element_type=F32, precision=HI)


def kernel(
    heights,
    tiles,
    mat_hbm,
    clamp_hbm,
    table_hbm,
    eigen_hbm,
    out,
    table,
    eigen,
    mat,
    cl,
    m_lo, m_hi, m_side, m_corner, m_stage,
    q1, q1_vert, q1_side, q1_stage,
    q2, q2_own,
    b1_vert, b1_side, b1_stage,
    b2, b2_own,
    S, SG, HZ, HR, HC, BB, WH, DD, V0, V1, RS,
    S1, HZ1, HR1, HC1, BB1, WH1, DD1, VA1, VB1, RS1, PO1,
    HZ2, HR2, HC2, WH2, DD2, VA2, VB2, PO2, T1,
    S3, HZ3, HR3, HC3, WH3, BB3, V3,
    T0, R4,
    local_sem,
    m_send, m_recv, q1_send, q1_recv, q2_send, q2_recv, b1_send, b1_recv, b2_send, b2_recv,
):
    i = lax.axis_index("tile")
    h = lax.axis_index("height")

    in_mat = pltpu.make_async_copy(mat_hbm, mat, local_sem.at[0])
    in_cl = pltpu.make_async_copy(clamp_hbm.at[pl.ds(0, 2)], cl, local_sem.at[1])
    in_table = pltpu.make_async_copy(table_hbm, table, local_sem.at[2])
    in_eigen = pltpu.make_async_copy(eigen_hbm, eigen, local_sem.at[3])

    def tile_ok(dt):
        return jnp.logical_and(i + dt >= 0, i + dt < tiles)

    def near_ok(dt, dh):
        return jnp.logical_and(tile_ok(dt), jnp.logical_and(h + dh >= 0, h + dh < heights))

    def far_id(dt, k):
        return {"tile": i + dt, "height": lax.rem(h + k, heights)}

    in_mat.start()
    barrier = pltpu.get_barrier_semaphore()
    for dt, dh in NEAR:
        @pl.when(near_ok(dt, dh))
        def _():
            pl.semaphore_signal(
                barrier, inc=1, device_id={"tile": i + dt, "height": h + dh},
                device_id_type=pl.DeviceIdType.MESH,
            )
    reach = sum(near_ok(dt, dh).astype(jnp.int32) for dt, dh in NEAR)

    in_cl.start()
    in_table.start()
    in_eigen.start()
    in_mat.wait()
    in_cl.wait()
    for z in range(8):
        m_stage[0, z] = mat[z, 0:4]
        m_stage[1, z] = mat[z, 28:32]
    for z in range(2):
        m_stage[0, 8 + z] = cl[z, 0:4]
        m_stage[1, 8 + z] = cl[z, 28:32]

    pl.semaphore_wait(barrier, reach)

    def near_copies(send, recv, refs):
        copies = []
        for k, (dt, dh) in enumerate(NEAR):
            src, dst = refs(dt, dh)
            copy = pltpu.make_async_remote_copy(
                src_ref=src, dst_ref=dst, send_sem=send.at[k], recv_sem=recv.at[k],
                device_id={"tile": i + dt, "height": h + dh},
                device_id_type=pl.DeviceIdType.MESH,
            )
            copies.append((copy, near_ok(dt, dh), near_ok(-dt, -dh)))
        return copies

    def far_copies(send, recv, own, field):
        copies = []
        for k, (dt, dh) in enumerate(FAR):
            copy = pltpu.make_async_remote_copy(
                src_ref=own,
                dst_ref=field.at[pl.ds(2 * h, 2), pl.ds(8 * (2 - dt), 8)],
                send_sem=send.at[k], recv_sem=recv.at[k],
                device_id=far_id(dt, dh), device_id_type=pl.DeviceIdType.MESH,
            )
            copies.append((copy, tile_ok(dt), tile_ok(-dt)))
        return copies

    def ends_apart(dh):
        if dh == 1:
            return h == heights - 1
        if dh == 3:
            return h == 0
        return None

    def start_far(copies, apart):
        for (_, dh), (copy, sends, _) in zip(FAR, copies):
            wide = ends_apart(dh)
            if wide is None:
                if apart:
                    continue
                cond = sends
            else:
                cond = jnp.logical_and(sends, wide if apart else jnp.logical_not(wide))

            @pl.when(cond)
            def _():
                copy.start()

    def start(copies):
        for copy, sends, _ in copies:
            @pl.when(sends)
            def _():
                copy.start()

    def wait_recv(copies):
        for copy, _, receives in copies:
            @pl.when(receives)
            def _():
                copy.wait_recv()

    def wait_send(copies):
        for copy, sends, _ in copies:
            @pl.when(sends)
            def _():
                copy.wait_send()

    def label_refs(dt, dh):
        if dt == 0:
            return (mat.at[pl.ds(5, 3)], m_lo) if dh > 0 else (mat.at[pl.ds(0, 3)], m_hi)
        side = 0 if dt < 0 else 1
        if dh == 0:
            return m_stage.at[side], m_side.at[side]
        first = 6 if dh > 0 else 0
        return m_stage.at[side, pl.ds(first, 2)], m_corner.at[side, 0 if dh < 0 else 1]

    label_moves = near_copies(m_send, m_recv, label_refs)
    start(label_moves)

    in_table.wait()
    in_eigen.wait()

    st = [table[n] for n in range(3)]
    stress = [[table[n] * eigen[n, c] for c in range(3)] for n in range(3)]

    def look(m, values):
        return jnp.where(
            m == 0, values[0], jnp.where(m == 1, values[1], jnp.where(m == 2, values[2], 0.0))
        )

    take_lo = one_hot((128, 128), lambda l, j: jnp.logical_and(j < 64, l // 2 == j))
    take_hi = one_hot((128, 128), lambda l, j: l // 2 == j - 64)
    lowest = jnp.where(h == 0, 1.0, 0.0).astype(F32)

    for z in range(4):
        R4[0, z] = look(mat[2 * z], st) + look(mat[2 * z + 1], st)
    R4[1, 0] = (cl[0] + cl[1]).astype(F32)
    s_rows = jnp.concatenate(
        [R4[0, z, pl.ds(0, 16, 2)] + R4[0, z, pl.ds(1, 16, 2)] for z in range(4)], axis=0
    )
    p_rows = R4[1, 0, pl.ds(0, 16, 2)] + R4[1, 0, pl.ds(1, 16, 2)]
    s_one = dot(0.5 * s_rows, take_lo).reshape(4, 16, 128)
    p_one = dot((2.0 * PENALTY * lowest) * p_rows, take_hi)
    q1[0] = s_one[0] + p_one
    for z in range(1, 4):
        q1[z] = s_one[z]
    for z in range(4):
        q1_stage[0, z] = q1[z, 0:4]
        q1_stage[1, z] = q1[z, 12:16]

    def q1_refs(dt, dh):
        if dt == 0:
            return q1, q1_vert.at[0 if dh > 0 else 1]
        side = 0 if dt < 0 else 1
        return q1_stage.at[side], q1_side.at[side, dh + 1]

    q1_moves = near_copies(q1_send, q1_recv, q1_refs)
    start(q1_moves)

    for z in range(2):
        R4[1, z, 0:16] = q1[2 * z] + q1[2 * z + 1]
    q_rows = jnp.concatenate(
        [R4[1, z, pl.ds(0, 8, 2)] + R4[1, z, pl.ds(1, 8, 2)] for z in range(2)], axis=0
    )
    l, j = iota((128, 128), 0), iota((128, 128), 1)
    down_q = jnp.where(
        jnp.logical_and(j < 96, jnp.logical_and(l < 64, l // 2 == j % 32)), 0.5,
        jnp.where(jnp.logical_and(j >= 96, l // 2 == j - 64), 1.0, 0.0),
    ).astype(F32)
    q2_own[...] = dot(q_rows, down_q).reshape(2, 8, 128)
    q2_moves = far_copies(q2_send, q2_recv, q2_own, q2)
    q2[pl.ds(2 * h, 2), 16:24] = q2_own[...]

    lane = iota((40, 128), 1)
    sub8 = iota((8, 128), 0)
    wait_recv(label_moves)
    below, above = h > 0, h < heights - 1
    before, after = i > 0, i < tiles - 1

    def side_rows(z, ref_of):
        lo_ok, lo = ref_of(1)
        hi_ok, hi = ref_of(0)
        return jnp.concatenate([jnp.where(hi_ok, hi, -1), jnp.where(lo_ok, lo, -1)], axis=0)

    def labels(z):
        if z < 0:
            centre = jnp.where(below, m_lo[z + 3], -1)
            if z < -2:
                return jnp.concatenate([centre, jnp.full((8, 128), -1, jnp.int32)], axis=0)
            sides = side_rows(
                z, lambda s: (jnp.logical_and(below, before if s else after), m_corner[s, 1, z + 2])
            )
        elif z < 8:
            centre = mat[z]
            sides = side_rows(z, lambda s: (before if s else after, m_side[s, z]))
        else:
            centre = jnp.where(above, m_hi[z - 8], -1)
            if z > 9:
                return jnp.concatenate([centre, jnp.full((8, 128), -1, jnp.int32)], axis=0)
            sides = side_rows(
                z, lambda s: (jnp.logical_and(above, before if s else after), m_corner[s, 0, z - 8])
            )
        return jnp.concatenate([centre, sides], axis=0)

    for z in range(-3, 11):
        m = labels(z)
        S[z + 3] = look(m, st)
        for c in range(3):
            SG[c, z + 3] = look(m, [stress[n][c] for n in range(3)])
    for z in range(-3, 10):
        HZ[z + 3] = S[z + 3] + S[z + 4]

    def spring0(z):
        sides = jnp.concatenate(
            [jnp.where(after, m_side[0, 8 + z], 0), jnp.where(before, m_side[1, 8 + z], 0)], axis=0
        )
        return (2.0 * PENALTY * lowest) * jnp.concatenate([cl[z], sides], axis=0).astype(F32)

    for z in range(-2, 10):
        s = S[z + 3]
        s_r = pltpu.roll(s, 39, 0)
        s_c = jnp.where(lane < 127, pltpu.roll(s, 127, 1), 0.0)
        h_ru = s + s_r
        h_rl = pltpu.roll(h_ru, 1, 0)
        f_cu = s + s_c
        f_cl = s + jnp.where(lane > 0, pltpu.roll(s, 1, 1), 0.0)
        HR[0, z + 2] = h_rl
        HR[1, z + 2] = h_ru
        HC[0, z + 2] = jnp.where(lane > 0, f_cl, 0.0)
        HC[1, z + 2] = jnp.where(lane < 127, f_cu, 0.0)
        f = [HZ[z + 2] + HZ[z + 3], h_rl + h_ru, f_cl + f_cu]
        total = f[0] + f[1] + f[2]
        if 0 <= z < 2:
            total = total + spring0(z)
        g0 = SG[0, z + 2] - SG[0, z + 4]
        x = SG[1, z + 3]
        g1 = pltpu.roll(x, 1, 0) - pltpu.roll(x, 39, 0)
        x = SG[2, z + 3]
        g2 = jnp.where(lane > 0, pltpu.roll(x, 1, 1), 0.0) - jnp.where(
            lane < 127, pltpu.roll(x, 127, 1), 0.0
        )
        for c, g in enumerate((g0, g1, g2)):
            d = total + f[c]
            w = jnp.where(s > 0.0, OMEGA / jnp.where(s > 0.0, d, 1.0), 0.0)
            BB[c, z + 2] = g
            WH[c, z + 2] = w
            if 0 <= z < 8:
                DD[c, z] = d
            V0[c, z + 2] = w * g

    def apply0(v, off, c, z):
        x = v[c, z + off]
        a = HZ[z + 2] * v[c, z + off - 1] + HZ[z + 3] * v[c, z + off + 1]
        b = HR[0, z + 2] * pltpu.roll(x, 1, 0) + HR[1, z + 2] * pltpu.roll(x, 39, 0)
        e = HC[0, z + 2] * pltpu.roll(x, 1, 1) + HC[1, z + 2] * pltpu.roll(x, 127, 1)
        return x, (a + b + e) + (a, b, e)[c]

    for z in range(-1, 9):
        for c in range(3):
            x, n = apply0(V0, 2, c, z)
            V1[c, z + 1] = KEEP * x + WH[c, z + 2] * (BB[c, z + 2] + n)

    for z in range(4):
        for c in range(3):
            total = None
            for k in range(2):
                x, n = apply0(V1, 1, c, 2 * z + k)
                r = BB[c, 2 * z + k + 2] + n - DD[c, 2 * z + k] * x
                total = r[0:32] if total is None else total + r[0:32]
            RS[c, z] = total

    def row_pairs(ref, c, n):
        return jnp.concatenate(
            [ref[c, z, pl.ds(0, n, 2)] + ref[c, z, pl.ds(1, n, 2)] for z in range(ref.shape[1])], axis=0
        )

    r0, r1, r2 = (row_pairs(RS, c, 16) for c in range(3))
    new = [dot(r0, take_lo) + dot(r1, take_hi), dot(r2, take_lo)]
    for t in range(2):
        value = new[t].reshape(4, 16, 128)
        for z in range(4):
            BB1[t, z + 3, 0:16] = value[z]
            b1_stage[0, t, z] = value[z, 0:4]
            b1_stage[1, t, z] = value[z, 12:16]

    def b1_refs(dt, dh):
        if dt == 0:
            first = 4 if dh > 0 else 3
            return BB1.at[:, pl.ds(first, 3), pl.ds(0, 16)], b1_vert.at[0 if dh > 0 else 1]
        side = 0 if dt < 0 else 1
        if dh == 0:
            return b1_stage.at[side], b1_side.at[side, 0]
        first = 2 if dh > 0 else 0
        return (
            b1_stage.at[side, :, pl.ds(first, 2)],
            b1_side.at[side, 2 if dh > 0 else 1, :, pl.ds(first, 2)],
        )

    b1_moves = near_copies(b1_send, b1_recv, b1_refs)
    start(b1_moves)
    start_far(q2_moves, False)

    lane1 = iota((24, 128), 1)
    col1 = lane1 % 64
    wait_recv(q1_moves)

    def both(x):
        return jnp.where(iota(x.shape, len(x.shape) - 1) < 64, x, 0.0)

    for z in range(-4, 8):
        if z < 0:
            centre = jnp.where(below, q1_vert[0, z + 4], 0.0)
            lo = jnp.where(jnp.logical_and(below, before), q1_side[1, 2, z + 4], 0.0)
            hi = jnp.where(jnp.logical_and(below, after), q1_side[0, 2, z + 4], 0.0)
        elif z < 4:
            centre = q1[z]
            lo = jnp.where(before, q1_side[1, 1, z], 0.0)
            hi = jnp.where(after, q1_side[0, 1, z], 0.0)
        else:
            centre = jnp.where(above, q1_vert[1, z - 4], 0.0)
            lo = jnp.where(jnp.logical_and(above, before), q1_side[1, 0, z - 4], 0.0)
            hi = jnp.where(jnp.logical_and(above, after), q1_side[0, 0, z - 4], 0.0)
        q = jnp.concatenate([centre, hi, lo], axis=0)
        other = pltpu.roll(q, 64, 1)
        S1[z + 4] = jnp.where(lane1 < 64, q, other)
        if z == 0:
            spring1 = jnp.where(lane1 < 64, other, q)
    for z in range(-4, 7):
        HZ1[z + 4] = S1[z + 4] + S1[z + 5]
    for z in range(-3, 7):
        s = S1[z + 4]
        h_ru = s + pltpu.roll(s, 23, 0)
        h_rl = pltpu.roll(h_ru, 1, 0)
        f_cu = s + jnp.where(col1 < 63, pltpu.roll(s, 127, 1), 0.0)
        f_cl = s + jnp.where(col1 > 0, pltpu.roll(s, 1, 1), 0.0)
        HR1[0, z + 3] = h_rl
        HR1[1, z + 3] = h_ru
        HC1[0, z + 3] = jnp.where(col1 > 0, f_cl, 0.0)
        HC1[1, z + 3] = jnp.where(col1 < 63, f_cu, 0.0)
        f = [HZ1[z + 3] + HZ1[z + 4], h_rl + h_ru, f_cl + f_cu]
        total = f[0] + f[1] + f[2]
        if z == 0:
            total = total + spring1
        for t in range(2):
            d = total + (jnp.where(lane1 < 64, f[0], f[1]) if t == 0 else f[2])
            WH1[t, z + 3] = jnp.where(s > 0.0, OMEGA / jnp.where(s > 0.0, d, 1.0), 0.0)
            if 0 <= z < 4:
                DD1[t, z] = d

    wait_recv(b1_moves)
    start_far(q2_moves, True)
    for t in range(2):
        for z in range(-3, 7):
            if z < 0:
                BB1[t, z + 3, 0:16] = jnp.where(below, b1_vert[0, t, z + 3], 0.0)
                if z < -2:
                    lo = jnp.zeros((4, 128), F32)
                    hi = lo
                else:
                    lo = jnp.where(jnp.logical_and(below, before), b1_side[1, 2, t, z + 4], 0.0)
                    hi = jnp.where(jnp.logical_and(below, after), b1_side[0, 2, t, z + 4], 0.0)
            elif z < 4:
                lo = jnp.where(before, b1_side[1, 0, t, z], 0.0)
                hi = jnp.where(after, b1_side[0, 0, t, z], 0.0)
            else:
                BB1[t, z + 3, 0:16] = jnp.where(above, b1_vert[1, t, z - 4], 0.0)
                if z > 5:
                    lo = jnp.zeros((4, 128), F32)
                    hi = lo
                else:
                    lo = jnp.where(jnp.logical_and(above, before), b1_side[1, 1, t, z - 4], 0.0)
                    hi = jnp.where(jnp.logical_and(above, after), b1_side[0, 1, t, z - 4], 0.0)
            BB1[t, z + 3, 16:24] = jnp.concatenate([hi, lo], axis=0)

    for z in range(-3, 7):
        for t in range(2):
            VA1[t, z + 3] = WH1[t, z + 3] * BB1[t, z + 3]

    def apply1(v, off, t, z):
        x = v[t, z + off]
        a = HZ1[z + 3] * v[t, z + off - 1] + HZ1[z + 4] * v[t, z + off + 1]
        b = HR1[0, z + 3] * pltpu.roll(x, 1, 0) + HR1[1, z + 3] * pltpu.roll(x, 23, 0)
        e = HC1[0, z + 3] * pltpu.roll(x, 1, 1) + HC1[1, z + 3] * pltpu.roll(x, 127, 1)
        return x, (a + b + e) + (jnp.where(lane1 < 64, a, b) if t == 0 else e)

    for z in range(-2, 6):
        for t in range(2):
            x, n = apply1(VA1, 3, t, z)
            VB1[t, z + 2] = KEEP * x + WH1[t, z + 3] * (BB1[t, z + 3] + n)
    for z in range(2):
        for t in range(2):
            total = None
            for k in range(2):
                x, n = apply1(VB1, 2, t, 2 * z + k)
                r = BB1[t, 2 * z + k + 3] + n - DD1[t, 2 * z + k] * x
                total = r[0:16] if total is None else total + r[0:16]
            RS1[t, z] = total
    down_a = one_hot((128, 128), lambda l, j: l // 2 == j)
    down_b = one_hot((128, 128), lambda l, j: jnp.logical_and(l < 64, l // 2 == j - 64))
    b2_own[...] = (dot(row_pairs(RS1, 0, 8), down_a) + dot(row_pairs(RS1, 1, 8), down_b)).reshape(2, 8, 128)
    b2_moves = far_copies(b2_send, b2_recv, b2_own, b2)
    start(b2_moves)
    b2[pl.ds(2 * h, 2), 16:24] = b2_own[...]

    lane2 = iota((40, 128), 1)
    row2 = iota((40, 128), 0)
    col2 = lane2 % 32
    real = lane2 < 96
    slot = row2 // 8 + (i - 2)
    inside = jnp.logical_and(slot >= 0, slot < tiles)
    keep = jnp.logical_and(inside, real)
    wait_recv(q2_moves)

    def pick(a, b, e):
        return jnp.where(lane2 < 32, a, jnp.where(lane2 < 64, b, e))

    q = jnp.where(inside, q2[0], 0.0)
    spring2 = pick(pltpu.roll(q, 32, 1), pltpu.roll(q, 64, 1), pltpu.roll(q, 96, 1))
    odd_row, odd_col = row2 % 2 == 1, lane2 % 2 == 1

    def pair_sum(x):
        x = x + jnp.where(odd_row, pltpu.roll(x, 1, 0), pltpu.roll(x, 39, 0))
        return x + jnp.where(odd_col, pltpu.roll(x, 1, 1), pltpu.roll(x, 127, 1))

    def faces(s_of, depth, step, spring, hz, hr, hc, wh, dd):
        for z in range(depth - 1):
            hz[z] = s_of(z) + s_of(z + 1)
        for z in range(depth):
            s = s_of(z)
            h_ru = s + pltpu.roll(s, 40 - step, 0)
            h_rl = pltpu.roll(h_ru, step, 0)
            first, last = col2 < step, col2 >= 32 - step
            f_cu = s + jnp.where(last, 0.0, pltpu.roll(s, 128 - step, 1))
            f_cl = s + jnp.where(first, 0.0, pltpu.roll(s, step, 1))
            hr[0, z] = h_rl
            hr[1, z] = h_ru
            hc[0, z] = jnp.where(first, 0.0, f_cl)
            hc[1, z] = jnp.where(last, 0.0, f_cu)
            f_z = (hz[z - 1] if z > 0 else s) + (hz[z] if z < depth - 1 else s)
            f_r, f_c = h_rl + h_ru, f_cl + f_cu
            d = (f_z + f_r + f_c) + pick(f_z, f_r, f_c)
            if z == 0:
                d = d + spring
            wh[z] = jnp.where(s > 0.0, OMEGA / jnp.where(s > 0.0, d, 1.0), 0.0)
            if dd is not None:
                dd[z] = d

    def s2(z):
        return jnp.where(keep, q2[z], 0.0)

    faces(s2, 8, 1, spring2, HZ2, HR2, HC2, WH2, DD2)
    for z in range(4):
        S3[z] = 0.5 * pair_sum(s2(2 * z) + s2(2 * z + 1))
    faces(lambda z: S3[z], 4, 2, pair_sum(spring2), HZ3, HR3, HC3, WH3, None)

    def apply2(v, z, depth, step, hz, hr, hc):
        x = v[z]
        a = None
        if z > 0:
            a = hz[z - 1] * v[z - 1]
        if z < depth - 1:
            up = hz[z] * v[z + 1]
            a = up if a is None else a + up
        b = hr[0, z] * pltpu.roll(x, step, 0) + hr[1, z] * pltpu.roll(x, 40 - step, 0)
        e = hc[0, z] * pltpu.roll(x, step, 1) + hc[1, z] * pltpu.roll(x, 128 - step, 1)
        return x, (a + b + e) + pick(a, b, e)

    wait_recv(b2_moves)
    for z in range(8):
        b = jnp.where(keep, b2[z], 0.0)
        b2[z] = b
        VA2[z] = WH2[z] * b
    for z in range(8):
        x, n = apply2(VA2, z, 8, 1, HZ2, HR2, HC2)
        VB2[z] = KEEP * x + WH2[z] * (b2[z] + n)
    for z in range(4):
        total = None
        for k in range(2):
            x, n = apply2(VB2, 2 * z + k, 8, 1, HZ2, HR2, HC2)
            r = b2[2 * z + k] + n - DD2[2 * z + k] * x
            total = r if total is None else total + r
        total = pair_sum(total)
        BB3[z] = total
        V3[0, z] = WH3[z] * total
    for turn in range(5):
        now, later = turn % 2, (turn + 1) % 2
        for z in range(4):
            x, n = apply2(V3.at[now], z, 4, 2, HZ3, HR3, HC3)
            V3[later, z] = KEEP * x + WH3[z] * (BB3[z] + n)
    for z in range(8):
        VB2[z] = VB2[z] + V3[1, z // 2]
    PO2[0] = jnp.zeros((24, 128), F32)
    PO2[9] = jnp.zeros((24, 128), F32)
    for z in range(8):
        x, n = apply2(VB2, z, 8, 1, HZ2, HR2, HC2)
        PO2[z + 1] = (KEEP * x + WH2[z] * (b2[z] + n))[8:32]

    up_a = one_hot((128, 128), lambda l, j: l == j // 2)
    up_b = one_hot((128, 128), lambda l, j: jnp.logical_and(j < 64, l == 64 + j // 2))
    coarse = PO2[pl.ds(2 * h, 4)].reshape(96, 128)
    for t, m in enumerate((up_a, up_b)):
        e = dot(coarse, m).reshape(4, 24, 128)
        for k in range(4):
            T1[t, k, pl.ds(0, 24, 2)] = e[k]
            T1[t, k, pl.ds(1, 24, 2)] = e[k]
    for z in range(-2, 6):
        for t in range(2):
            k = (z + 2) // 2
            tail = jnp.where(sub8 < 4, T1[t, k, 32:40], T1[t, k, 8:16])
            e = jnp.concatenate([T1[t, k, 16:32], tail], axis=0)
            VB1[t, z + 2] = VB1[t, z + 2] + e
    for z in range(-1, 5):
        for t in range(2):
            x, n = apply1(VB1, 2, t, z)
            PO1[t, z + 1] = KEEP * x + WH1[t, z + 3] * (BB1[t, z + 3] + n)

    up_lo = one_hot((128, 128), lambda l, j: l == j // 2)
    up_hi = one_hot((128, 128), lambda l, j: l == 64 + j // 2)
    for c in range(3):
        e = dot(PO1[c // 2].reshape(144, 128), up_hi if c == 1 else up_lo).reshape(6, 24, 128)
        for k in range(6):
            T0[c, k, pl.ds(0, 24, 2)] = e[k]
            T0[c, k, pl.ds(1, 24, 2)] = e[k]
    for z in range(-1, 9):
        for c in range(3):
            k = (z + 2) // 2
            tail = jnp.where(sub8 < 4, T0[c, k, 32:40], T0[c, k, 40:48])
            V1[c, z + 1] = V1[c, z + 1] + jnp.concatenate([T0[c, k, 0:32], tail], axis=0)
    for z in range(8):
        for c in range(3):
            x, n = apply0(V1, 1, c, z)
            out[c, z] = (KEEP * x + WH[c, z + 2] * (BB[c, z + 2] + n))[0:32]

    for moves in (label_moves, q1_moves, q2_moves, b1_moves, b2_moves):
        wait_send(moves)


def solution(mesh):
    heights, tiles = mesh.shape["height"], mesh.shape["tile"]

    def vmem(*shape, dtype=F32):
        return pltpu.VMEM(shape, dtype)

    i32 = jnp.int32
    scratch = [
        pltpu.SMEM((3,), F32), pltpu.SMEM((3, 3), F32),
        vmem(8, 32, 128, dtype=i32), vmem(2, 32, 128, dtype=i32),
        vmem(3, 32, 128, dtype=i32), vmem(3, 32, 128, dtype=i32),
        vmem(2, 10, 4, 128, dtype=i32), vmem(2, 2, 2, 4, 128, dtype=i32), vmem(2, 10, 4, 128, dtype=i32),
        vmem(4, 16, 128), vmem(2, 4, 16, 128), vmem(2, 3, 4, 4, 128), vmem(2, 4, 4, 128),
        vmem(8, 40, 128), vmem(2, 8, 128),
        vmem(2, 2, 3, 16, 128), vmem(2, 3, 2, 4, 4, 128), vmem(2, 2, 4, 4, 128),
        vmem(8, 40, 128), vmem(2, 8, 128),
        vmem(14, 40, 128), vmem(3, 14, 40, 128), vmem(13, 40, 128), vmem(2, 12, 40, 128), vmem(2, 12, 40, 128),
        vmem(3, 12, 40, 128), vmem(3, 12, 40, 128), vmem(3, 8, 40, 128), vmem(3, 12, 40, 128),
        vmem(3, 10, 40, 128), vmem(3, 4, 32, 128),
        vmem(12, 24, 128), vmem(11, 24, 128), vmem(2, 10, 24, 128), vmem(2, 10, 24, 128), vmem(2, 10, 24, 128),
        vmem(2, 10, 24, 128), vmem(2, 4, 24, 128), vmem(2, 10, 24, 128), vmem(2, 8, 24, 128),
        vmem(2, 2, 16, 128), vmem(2, 6, 24, 128),
        vmem(7, 40, 128), vmem(2, 8, 40, 128), vmem(2, 8, 40, 128), vmem(8, 40, 128), vmem(8, 40, 128),
        vmem(8, 40, 128), vmem(8, 40, 128), vmem(10, 24, 128), vmem(2, 4, 48, 128),
        vmem(4, 40, 128), vmem(3, 40, 128), vmem(2, 4, 40, 128), vmem(2, 4, 40, 128), vmem(4, 40, 128),
        vmem(4, 40, 128), vmem(2, 4, 40, 128),
        vmem(3, 6, 48, 128), vmem(2, 4, 32, 128),
        pltpu.SemaphoreType.DMA((4,)),
    ]
    for count in (8, 8, 19, 8, 19):
        scratch += [pltpu.SemaphoreType.DMA((count,)), pltpu.SemaphoreType.DMA((count,))]

    def local(material, clamped, stiffness_table, eigenstrain):
        return pl.pallas_call(
            functools.partial(kernel, heights, tiles),
            out_shape=jax.ShapeDtypeStruct((3, 8, 32, 128), F32),
            in_specs=[
                pl.BlockSpec(memory_space=pltpu.HBM),
                pl.BlockSpec(memory_space=pltpu.HBM),
                pl.BlockSpec(memory_space=pltpu.HBM),
                pl.BlockSpec(memory_space=pltpu.HBM),
            ],
            out_specs=pl.BlockSpec(memory_space=pltpu.VMEM),
            scratch_shapes=scratch,
            compiler_params=pltpu.CompilerParams(
                collective_id=0, has_side_effects=True, vmem_limit_bytes=40 * 1024 * 1024
            ),
        )(*(pltpu.with_memory_space_constraint(x, pltpu.HBM) for x in (material, clamped, stiffness_table, eigenstrain)))

    in_specs = (P("height", "tile", None), P("height", "tile", None), P(), P())
    out_specs = P(None, "height", "tile", None)
    return jax.shard_map(local, mesh=mesh, in_specs=in_specs, out_specs=out_specs, check_vma=False)
```

```python
import functools

import jax
import jax.numpy as jnp
from jax import lax
from jax.experimental import pallas as pl
from jax.experimental.pallas import tpu as pltpu
from jax.sharding import PartitionSpec as P

PENALTY = 50.0
OMEGA = 0.6
KEEP = 1.0 - OMEGA
F32 = jnp.float32
HI = lax.Precision.HIGHEST
NEAR = ((-1, -1), (-1, 1), (1, -1), (1, 1), (-1, 0), (1, 0), (0, -1), (0, 1))
UPDOWN = ((0, -1), (0, 1))
FAR = tuple(
    sorted(
        ((dt, k) for dt in (-2, -1, 0, 1, 2) for k in (0, 1, 2, 3) if (dt, k) != (0, 0)),
        key=lambda move: (-abs(move[0]), -min(move[1], 4 - move[1]), move),
    )
)


def iota(shape, axis):
    return lax.broadcasted_iota(jnp.int32, shape, axis)


def one_hot(shape, cond):
    return jnp.where(cond(iota(shape, 0), iota(shape, 1)), 1.0, 0.0).astype(F32)


def dot(a, b):
    return jnp.dot(a, b, preferred_element_type=F32, precision=HI)


def kernel(
    heights,
    tiles,
    mat_hbm,
    clamp_hbm,
    table_hbm,
    eigen_hbm,
    out,
    table,
    eigen,
    mat,
    cl,
    m_lo, m_hi, m_side, m_corner, m_stage,
    q1, q1_vert, q1_side, q1_stage,
    q2, q2_own,
    b1_vert,
    b2, b2_own,
    S, SG, HZ, HR, HC, BB, WH, DD, V0, V1, RS, EX,
    S1, HZ1, HR1, HC1, BB1, WH1, DD1, VA1, VB1, RS1, PO1,
    HZ2, HR2, HC2, WH2, DD2, VA2, VB2, PO2, T1,
    S3, HZ3, HR3, HC3, WH3, BB3, V3,
    T0, R4,
    local_sem,
    m_send, m_recv, q1_send, q1_recv, q2_send, q2_recv, b1_send, b1_recv, b2_send, b2_recv,
):
    i = lax.axis_index("tile")
    h = lax.axis_index("height")

    in_mat = pltpu.make_async_copy(mat_hbm, mat, local_sem.at[0])
    in_cl = pltpu.make_async_copy(clamp_hbm.at[pl.ds(0, 2)], cl, local_sem.at[1])
    in_table = pltpu.make_async_copy(table_hbm, table, local_sem.at[2])
    in_eigen = pltpu.make_async_copy(eigen_hbm, eigen, local_sem.at[3])

    def tile_ok(dt):
        return jnp.logical_and(i + dt >= 0, i + dt < tiles)

    def near_ok(dt, dh):
        return jnp.logical_and(tile_ok(dt), jnp.logical_and(h + dh >= 0, h + dh < heights))

    def far_id(dt, k):
        return {"tile": i + dt, "height": lax.rem(h + k, heights)}

    in_mat.start()
    barrier = pltpu.get_barrier_semaphore()
    for dt, dh in NEAR:
        @pl.when(near_ok(dt, dh))
        def _():
            pl.semaphore_signal(
                barrier, inc=1, device_id={"tile": i + dt, "height": h + dh},
                device_id_type=pl.DeviceIdType.MESH,
            )
    reach = sum(near_ok(dt, dh).astype(jnp.int32) for dt, dh in NEAR)

    in_cl.start()
    in_table.start()
    in_eigen.start()
    in_mat.wait()
    in_cl.wait()
    for side, first, edge in ((0, 0, 8), (1, 24, 23)):
        for z in range(8):
            m_stage[side, z] = mat[z, first : first + 8]
        for z in range(2):
            m_stage[side, 8 + z] = cl[z, first : first + 8]
        m_stage[side, 10] = mat[:, edge]

    pl.semaphore_wait(barrier, reach)

    def near_copies(send, recv, refs, moves=NEAR):
        copies = []
        for k, (dt, dh) in enumerate(moves):
            src, dst = refs(dt, dh)
            copy = pltpu.make_async_remote_copy(
                src_ref=src, dst_ref=dst, send_sem=send.at[k], recv_sem=recv.at[k],
                device_id={"tile": i + dt, "height": h + dh},
                device_id_type=pl.DeviceIdType.MESH,
            )
            copies.append((copy, near_ok(dt, dh), near_ok(-dt, -dh)))
        return copies

    def far_copies(send, recv, own, field):
        copies = []
        for k, (dt, dh) in enumerate(FAR):
            copy = pltpu.make_async_remote_copy(
                src_ref=own,
                dst_ref=field.at[pl.ds(2 * h, 2), pl.ds(8 * (2 - dt), 8)],
                send_sem=send.at[k], recv_sem=recv.at[k],
                device_id=far_id(dt, dh), device_id_type=pl.DeviceIdType.MESH,
            )
            copies.append((copy, tile_ok(dt), tile_ok(-dt)))
        return copies

    def ends_apart(dh):
        if dh == 1:
            return h == heights - 1
        if dh == 3:
            return h == 0
        return None

    def start_far(copies, apart):
        for (_, dh), (copy, sends, _) in zip(FAR, copies):
            wide = ends_apart(dh)
            if wide is None:
                if apart:
                    continue
                cond = sends
            else:
                cond = jnp.logical_and(sends, wide if apart else jnp.logical_not(wide))

            @pl.when(cond)
            def _():
                copy.start()

    def start(copies):
        for copy, sends, _ in copies:
            @pl.when(sends)
            def _():
                copy.start()

    def wait_recv(copies):
        for copy, _, receives in copies:
            @pl.when(receives)
            def _():
                copy.wait_recv()

    def wait_send(copies):
        for copy, sends, _ in copies:
            @pl.when(sends)
            def _():
                copy.wait_send()

    def label_refs(dt, dh):
        if dt == 0:
            return (mat.at[pl.ds(5, 3)], m_lo) if dh > 0 else (mat.at[pl.ds(0, 3)], m_hi)
        side = 0 if dt < 0 else 1
        if dh == 0:
            return m_stage.at[side], m_side.at[side]
        first = 5 if dh > 0 else 0
        return m_stage.at[side, pl.ds(first, 3)], m_corner.at[side, 0 if dh < 0 else 1]

    label_moves = near_copies(m_send, m_recv, label_refs)
    start(label_moves)

    in_table.wait()
    in_eigen.wait()

    st = [table[n] for n in range(3)]
    stress = [[table[n] * eigen[n, c] for c in range(3)] for n in range(3)]

    def look(m, values):
        return jnp.where(
            m == 0, values[0], jnp.where(m == 1, values[1], jnp.where(m == 2, values[2], 0.0))
        )

    take_lo = one_hot((128, 128), lambda l, j: jnp.logical_and(j < 64, l // 2 == j))
    take_hi = one_hot((128, 128), lambda l, j: l // 2 == j - 64)
    lowest = jnp.where(h == 0, 1.0, 0.0).astype(F32)

    for z in range(4):
        R4[0, z] = look(mat[2 * z], st) + look(mat[2 * z + 1], st)
    R4[1, 0] = (cl[0] + cl[1]).astype(F32)
    s_rows = jnp.concatenate(
        [R4[0, z, pl.ds(0, 16, 2)] + R4[0, z, pl.ds(1, 16, 2)] for z in range(4)], axis=0
    )
    p_rows = R4[1, 0, pl.ds(0, 16, 2)] + R4[1, 0, pl.ds(1, 16, 2)]
    s_one = dot(0.5 * s_rows, take_lo).reshape(4, 16, 128)
    p_one = dot((2.0 * PENALTY * lowest) * p_rows, take_hi)
    q1[0] = s_one[0] + p_one
    for z in range(1, 4):
        q1[z] = s_one[z]
    for z in range(4):
        q1_stage[0, z] = q1[z, 0:4]
        q1_stage[1, z] = q1[z, 12:16]

    def q1_refs(dt, dh):
        if dt == 0:
            return q1, q1_vert.at[0 if dh > 0 else 1]
        side = 0 if dt < 0 else 1
        return q1_stage.at[side], q1_side.at[side, dh + 1]

    q1_moves = near_copies(q1_send, q1_recv, q1_refs)
    start(q1_moves)

    for z in range(2):
        R4[1, z, 0:16] = q1[2 * z] + q1[2 * z + 1]
    q_rows = jnp.concatenate(
        [R4[1, z, pl.ds(0, 8, 2)] + R4[1, z, pl.ds(1, 8, 2)] for z in range(2)], axis=0
    )
    l, j = iota((128, 128), 0), iota((128, 128), 1)
    down_q = jnp.where(
        jnp.logical_and(j < 96, jnp.logical_and(l < 64, l // 2 == j % 32)), 0.5,
        jnp.where(jnp.logical_and(j >= 96, l // 2 == j - 64), 1.0, 0.0),
    ).astype(F32)
    q2_own[...] = dot(q_rows, down_q).reshape(2, 8, 128)
    q2_moves = far_copies(q2_send, q2_recv, q2_own, q2)
    q2[pl.ds(2 * h, 2), 16:24] = q2_own[...]

    lane = iota((48, 128), 1)
    row = iota((48, 128), 0)
    sub8 = iota((8, 128), 0)
    wait_recv(label_moves)
    below, above = h > 0, h < heights - 1
    before, after = i > 0, i < tiles - 1

    def labels(z):
        if 0 <= z < 8:
            centre, hi, lo = mat[z], m_side[0, z], m_side[1, z]
            centre_ok, hi_ok, lo_ok = None, after, before
        else:
            centre_ok = below if z < 0 else above
            k = z + 3 if z < 0 else z - 8
            end = 1 if z < 0 else 0
            centre = (m_lo if z < 0 else m_hi)[k]
            hi, lo = m_corner[0, end, k], m_corner[1, end, k]
            hi_ok, lo_ok = jnp.logical_and(centre_ok, after), jnp.logical_and(centre_ok, before)
            centre = jnp.where(centre_ok, centre, -1)
        return jnp.concatenate([centre, jnp.where(hi_ok, hi, -1), jnp.where(lo_ok, lo, -1)], axis=0)

    for z in range(-3, 11):
        m = labels(z)
        S[z + 3] = look(m, st)
        for c in range(3):
            SG[c, z + 3] = look(m, [stress[n][c] for n in range(3)])
    for side, ok in ((0, after), (1, before)):
        m = jnp.where(ok, m_side[side, 10], -1)
        EX[side, 0] = look(m, st)
        EX[side, 1] = look(m, [stress[n][1] for n in range(3)])
    for z in range(-3, 10):
        HZ[z + 3] = S[z + 3] + S[z + 4]

    def spring0(z):
        sides = jnp.concatenate(
            [jnp.where(after, m_side[0, 8 + z], 0), jnp.where(before, m_side[1, 8 + z], 0)],
            axis=0,
        )
        return (2.0 * PENALTY * lowest) * jnp.concatenate([cl[z], sides], axis=0).astype(F32)

    for z in range(-2, 10):
        s = S[z + 3]
        s_r = pltpu.roll(s, 47, 0)
        if 0 <= z < 8:
            s_r = jnp.where(row == 39, EX[0, 0, z : z + 1], s_r)
        s_c = jnp.where(lane < 127, pltpu.roll(s, 127, 1), 0.0)
        h_ru = s + s_r
        h_rl = pltpu.roll(h_ru, 1, 0)
        if 0 <= z < 8:
            h_rl = jnp.where(row == 40, s + EX[1, 0, z : z + 1], h_rl)
        f_cu = s + s_c
        f_cl = s + jnp.where(lane > 0, pltpu.roll(s, 1, 1), 0.0)
        HR[0, z + 2] = h_rl
        HR[1, z + 2] = h_ru
        HC[0, z + 2] = jnp.where(lane > 0, f_cl, 0.0)
        HC[1, z + 2] = jnp.where(lane < 127, f_cu, 0.0)
        f = [HZ[z + 2] + HZ[z + 3], h_rl + h_ru, f_cl + f_cu]
        total = f[0] + f[1] + f[2]
        if 0 <= z < 2:
            total = total + spring0(z)
        g0 = SG[0, z + 2] - SG[0, z + 4]
        x = SG[1, z + 3]
        x_l, x_u = pltpu.roll(x, 1, 0), pltpu.roll(x, 47, 0)
        if 0 <= z < 8:
            x_l = jnp.where(row == 40, EX[1, 1, z : z + 1], x_l)
            x_u = jnp.where(row == 39, EX[0, 1, z : z + 1], x_u)
        g1 = x_l - x_u
        x = SG[2, z + 3]
        g2 = jnp.where(lane > 0, pltpu.roll(x, 1, 1), 0.0) - jnp.where(
            lane < 127, pltpu.roll(x, 127, 1), 0.0
        )
        for c, g in enumerate((g0, g1, g2)):
            d = total + f[c]
            w = jnp.where(s > 0.0, OMEGA / jnp.where(s > 0.0, d, 1.0), 0.0)
            BB[c, z + 2] = g
            WH[c, z + 2] = w
            if 0 <= z < 8:
                DD[c, z] = d
            V0[c, z + 2] = w * g

    def apply0(v, off, c, z):
        x = v[c, z + off]
        a = HZ[z + 2] * v[c, z + off - 1] + HZ[z + 3] * v[c, z + off + 1]
        b = HR[0, z + 2] * pltpu.roll(x, 1, 0) + HR[1, z + 2] * pltpu.roll(x, 47, 0)
        e = HC[0, z + 2] * pltpu.roll(x, 1, 1) + HC[1, z + 2] * pltpu.roll(x, 127, 1)
        return x, (a + b + e) + (a, b, e)[c]

    for z in range(-1, 9):
        for c in range(3):
            x, n = apply0(V0, 2, c, z)
            V1[c, z + 1] = KEEP * x + WH[c, z + 2] * (BB[c, z + 2] + n)

    for z in range(4):
        for c in range(3):
            total = None
            for k in range(2):
                x, n = apply0(V1, 1, c, 2 * z + k)
                r = BB[c, 2 * z + k + 2] + n - DD[c, 2 * z + k] * x
                total = r if total is None else total + r
            RS[c, z] = total

    def row_pairs(ref, c, n):
        return jnp.concatenate(
            [ref[c, z, pl.ds(0, n, 2)] + ref[c, z, pl.ds(1, n, 2)] for z in range(ref.shape[1])], axis=0
        )

    r0, r1, r2 = (row_pairs(RS, c, 24) for c in range(3))
    new = [dot(r0, take_lo) + dot(r1, take_hi), dot(r2, take_lo)]
    for t in range(2):
        value = new[t].reshape(4, 24, 128)
        for z in range(4):
            BB1[t, z + 3] = value[z]

    def b1_refs(dt, dh):
        first = 4 if dh > 0 else 3
        return BB1.at[:, pl.ds(first, 3)], b1_vert.at[0 if dh > 0 else 1]

    b1_moves = near_copies(b1_send, b1_recv, b1_refs, UPDOWN)
    start(b1_moves)
    start_far(q2_moves, False)

    lane1 = iota((24, 128), 1)
    col1 = lane1 % 64
    wait_recv(q1_moves)

    def both(x):
        return jnp.where(iota(x.shape, len(x.shape) - 1) < 64, x, 0.0)

    for z in range(-4, 8):
        if z < 0:
            centre = jnp.where(below, q1_vert[0, z + 4], 0.0)
            lo = jnp.where(jnp.logical_and(below, before), q1_side[1, 2, z + 4], 0.0)
            hi = jnp.where(jnp.logical_and(below, after), q1_side[0, 2, z + 4], 0.0)
        elif z < 4:
            centre = q1[z]
            lo = jnp.where(before, q1_side[1, 1, z], 0.0)
            hi = jnp.where(after, q1_side[0, 1, z], 0.0)
        else:
            centre = jnp.where(above, q1_vert[1, z - 4], 0.0)
            lo = jnp.where(jnp.logical_and(above, before), q1_side[1, 0, z - 4], 0.0)
            hi = jnp.where(jnp.logical_and(above, after), q1_side[0, 0, z - 4], 0.0)
        q = jnp.concatenate([centre, hi, lo], axis=0)
        other = pltpu.roll(q, 64, 1)
        S1[z + 4] = jnp.where(lane1 < 64, q, other)
        if z == 0:
            spring1 = jnp.where(lane1 < 64, other, q)
    for z in range(-4, 7):
        HZ1[z + 4] = S1[z + 4] + S1[z + 5]
    for z in range(-3, 7):
        s = S1[z + 4]
        h_ru = s + pltpu.roll(s, 23, 0)
        h_rl = pltpu.roll(h_ru, 1, 0)
        f_cu = s + jnp.where(col1 < 63, pltpu.roll(s, 127, 1), 0.0)
        f_cl = s + jnp.where(col1 > 0, pltpu.roll(s, 1, 1), 0.0)
        HR1[0, z + 3] = h_rl
        HR1[1, z + 3] = h_ru
        HC1[0, z + 3] = jnp.where(col1 > 0, f_cl, 0.0)
        HC1[1, z + 3] = jnp.where(col1 < 63, f_cu, 0.0)
        f = [HZ1[z + 3] + HZ1[z + 4], h_rl + h_ru, f_cl + f_cu]
        total = f[0] + f[1] + f[2]
        if z == 0:
            total = total + spring1
        for t in range(2):
            d = total + (jnp.where(lane1 < 64, f[0], f[1]) if t == 0 else f[2])
            WH1[t, z + 3] = jnp.where(s > 0.0, OMEGA / jnp.where(s > 0.0, d, 1.0), 0.0)
            if 0 <= z < 4:
                DD1[t, z] = d

    wait_recv(b1_moves)
    start_far(q2_moves, True)
    for t in range(2):
        for z in range(3):
            BB1[t, z] = jnp.where(below, b1_vert[0, t, z], 0.0)
            BB1[t, z + 7] = jnp.where(above, b1_vert[1, t, z], 0.0)

    for z in range(-3, 7):
        for t in range(2):
            VA1[t, z + 3] = WH1[t, z + 3] * BB1[t, z + 3]

    def apply1(v, off, t, z):
        x = v[t, z + off]
        a = HZ1[z + 3] * v[t, z + off - 1] + HZ1[z + 4] * v[t, z + off + 1]
        b = HR1[0, z + 3] * pltpu.roll(x, 1, 0) + HR1[1, z + 3] * pltpu.roll(x, 23, 0)
        e = HC1[0, z + 3] * pltpu.roll(x, 1, 1) + HC1[1, z + 3] * pltpu.roll(x, 127, 1)
        return x, (a + b + e) + (jnp.where(lane1 < 64, a, b) if t == 0 else e)

    for z in range(-2, 6):
        for t in range(2):
            x, n = apply1(VA1, 3, t, z)
            VB1[t, z + 2] = KEEP * x + WH1[t, z + 3] * (BB1[t, z + 3] + n)
    for z in range(2):
        for t in range(2):
            total = None
            for k in range(2):
                x, n = apply1(VB1, 2, t, 2 * z + k)
                r = BB1[t, 2 * z + k + 3] + n - DD1[t, 2 * z + k] * x
                total = r[0:16] if total is None else total + r[0:16]
            RS1[t, z] = total
    down_a = one_hot((128, 128), lambda l, j: l // 2 == j)
    down_b = one_hot((128, 128), lambda l, j: jnp.logical_and(l < 64, l // 2 == j - 64))
    b2_own[...] = (dot(row_pairs(RS1, 0, 8), down_a) + dot(row_pairs(RS1, 1, 8), down_b)).reshape(2, 8, 128)
    b2_moves = far_copies(b2_send, b2_recv, b2_own, b2)
    start(b2_moves)
    b2[pl.ds(2 * h, 2), 16:24] = b2_own[...]

    lane2 = iota((40, 128), 1)
    row2 = iota((40, 128), 0)
    col2 = lane2 % 32
    real = lane2 < 96
    slot = row2 // 8 + (i - 2)
    inside = jnp.logical_and(slot >= 0, slot < tiles)
    keep = jnp.logical_and(inside, real)
    wait_recv(q2_moves)

    def pick(a, b, e):
        return jnp.where(lane2 < 32, a, jnp.where(lane2 < 64, b, e))

    q = jnp.where(inside, q2[0], 0.0)
    spring2 = pick(pltpu.roll(q, 32, 1), pltpu.roll(q, 64, 1), pltpu.roll(q, 96, 1))
    odd_row, odd_col = row2 % 2 == 1, lane2 % 2 == 1

    def pair_sum(x):
        x = x + jnp.where(odd_row, pltpu.roll(x, 1, 0), pltpu.roll(x, 39, 0))
        return x + jnp.where(odd_col, pltpu.roll(x, 1, 1), pltpu.roll(x, 127, 1))

    def faces(s_of, depth, step, spring, hz, hr, hc, wh, dd):
        for z in range(depth - 1):
            hz[z] = s_of(z) + s_of(z + 1)
        for z in range(depth):
            s = s_of(z)
            h_ru = s + pltpu.roll(s, 40 - step, 0)
            h_rl = pltpu.roll(h_ru, step, 0)
            first, last = col2 < step, col2 >= 32 - step
            f_cu = s + jnp.where(last, 0.0, pltpu.roll(s, 128 - step, 1))
            f_cl = s + jnp.where(first, 0.0, pltpu.roll(s, step, 1))
            hr[0, z] = h_rl
            hr[1, z] = h_ru
            hc[0, z] = jnp.where(first, 0.0, f_cl)
            hc[1, z] = jnp.where(last, 0.0, f_cu)
            f_z = (hz[z - 1] if z > 0 else s) + (hz[z] if z < depth - 1 else s)
            f_r, f_c = h_rl + h_ru, f_cl + f_cu
            d = (f_z + f_r + f_c) + pick(f_z, f_r, f_c)
            if z == 0:
                d = d + spring
            wh[z] = jnp.where(s > 0.0, OMEGA / jnp.where(s > 0.0, d, 1.0), 0.0)
            if dd is not None:
                dd[z] = d

    def s2(z):
        return jnp.where(keep, q2[z], 0.0)

    faces(s2, 8, 1, spring2, HZ2, HR2, HC2, WH2, DD2)
    for z in range(4):
        S3[z] = 0.5 * pair_sum(s2(2 * z) + s2(2 * z + 1))
    faces(lambda z: S3[z], 4, 2, pair_sum(spring2), HZ3, HR3, HC3, WH3, None)

    def apply2(v, z, depth, step, hz, hr, hc):
        x = v[z]
        a = None
        if z > 0:
            a = hz[z - 1] * v[z - 1]
        if z < depth - 1:
            up = hz[z] * v[z + 1]
            a = up if a is None else a + up
        b = hr[0, z] * pltpu.roll(x, step, 0) + hr[1, z] * pltpu.roll(x, 40 - step, 0)
        e = hc[0, z] * pltpu.roll(x, step, 1) + hc[1, z] * pltpu.roll(x, 128 - step, 1)
        return x, (a + b + e) + pick(a, b, e)

    wait_recv(b2_moves)
    for z in range(8):
        b = jnp.where(keep, b2[z], 0.0)
        b2[z] = b
        VA2[z] = WH2[z] * b
    for z in range(8):
        x, n = apply2(VA2, z, 8, 1, HZ2, HR2, HC2)
        VB2[z] = KEEP * x + WH2[z] * (b2[z] + n)
    for z in range(4):
        total = None
        for k in range(2):
            x, n = apply2(VB2, 2 * z + k, 8, 1, HZ2, HR2, HC2)
            r = b2[2 * z + k] + n - DD2[2 * z + k] * x
            total = r if total is None else total + r
        total = pair_sum(total)
        BB3[z] = total
        V3[0, z] = WH3[z] * total
    for turn in range(5):
        now, later = turn % 2, (turn + 1) % 2
        for z in range(4):
            x, n = apply2(V3.at[now], z, 4, 2, HZ3, HR3, HC3)
            V3[later, z] = KEEP * x + WH3[z] * (BB3[z] + n)
    for z in range(8):
        VB2[z] = VB2[z] + V3[1, z // 2]
    PO2[0] = jnp.zeros((24, 128), F32)
    PO2[9] = jnp.zeros((24, 128), F32)
    for z in range(8):
        x, n = apply2(VB2, z, 8, 1, HZ2, HR2, HC2)
        PO2[z + 1] = (KEEP * x + WH2[z] * (b2[z] + n))[8:32]

    up_a = one_hot((128, 128), lambda l, j: l == j // 2)
    up_b = one_hot((128, 128), lambda l, j: jnp.logical_and(j < 64, l == 64 + j // 2))
    coarse = PO2[pl.ds(2 * h, 4)].reshape(96, 128)
    for t, m in enumerate((up_a, up_b)):
        e = dot(coarse, m).reshape(4, 24, 128)
        for k in range(4):
            T1[t, k, pl.ds(0, 24, 2)] = e[k]
            T1[t, k, pl.ds(1, 24, 2)] = e[k]
    for z in range(-2, 6):
        for t in range(2):
            k = (z + 2) // 2
            tail = jnp.where(sub8 < 4, T1[t, k, 32:40], T1[t, k, 8:16])
            e = jnp.concatenate([T1[t, k, 16:32], tail], axis=0)
            VB1[t, z + 2] = VB1[t, z + 2] + e
    for z in range(-1, 5):
        for t in range(2):
            x, n = apply1(VB1, 2, t, z)
            PO1[t, z + 1] = KEEP * x + WH1[t, z + 3] * (BB1[t, z + 3] + n)

    up_lo = one_hot((128, 128), lambda l, j: l == j // 2)
    up_hi = one_hot((128, 128), lambda l, j: l == 64 + j // 2)
    for c in range(3):
        e = dot(PO1[c // 2].reshape(144, 128), up_hi if c == 1 else up_lo).reshape(6, 24, 128)
        for k in range(6):
            T0[c, k, pl.ds(0, 24, 2)] = e[k]
            T0[c, k, pl.ds(1, 24, 2)] = e[k]
    for z in range(-1, 9):
        for c in range(3):
            k = (z + 2) // 2
            V1[c, z + 1] = V1[c, z + 1] + T0[c, k]
    for z in range(8):
        for c in range(3):
            x, n = apply0(V1, 1, c, z)
            out[c, z] = (KEEP * x + WH[c, z + 2] * (BB[c, z + 2] + n))[0:32]

    for moves in (label_moves, q1_moves, q2_moves, b1_moves, b2_moves):
        wait_send(moves)


def solution(mesh):
    heights, tiles = mesh.shape["height"], mesh.shape["tile"]

    def vmem(*shape, dtype=F32):
        return pltpu.VMEM(shape, dtype)

    i32 = jnp.int32
    scratch = [
        pltpu.SMEM((3,), F32), pltpu.SMEM((3, 3), F32),
        vmem(8, 32, 128, dtype=i32), vmem(2, 32, 128, dtype=i32),
        vmem(3, 32, 128, dtype=i32), vmem(3, 32, 128, dtype=i32),
        vmem(2, 11, 8, 128, dtype=i32), vmem(2, 2, 3, 8, 128, dtype=i32), vmem(2, 11, 8, 128, dtype=i32),
        vmem(4, 16, 128), vmem(2, 4, 16, 128), vmem(2, 3, 4, 4, 128), vmem(2, 4, 4, 128),
        vmem(8, 40, 128), vmem(2, 8, 128),
        vmem(2, 2, 3, 24, 128),
        vmem(8, 40, 128), vmem(2, 8, 128),
        vmem(14, 48, 128), vmem(3, 14, 48, 128), vmem(13, 48, 128), vmem(2, 12, 48, 128), vmem(2, 12, 48, 128),
        vmem(3, 12, 48, 128), vmem(3, 12, 48, 128), vmem(3, 8, 48, 128), vmem(3, 12, 48, 128),
        vmem(3, 10, 48, 128), vmem(3, 4, 48, 128), vmem(2, 2, 8, 128),
        vmem(12, 24, 128), vmem(11, 24, 128), vmem(2, 10, 24, 128), vmem(2, 10, 24, 128), vmem(2, 10, 24, 128),
        vmem(2, 10, 24, 128), vmem(2, 4, 24, 128), vmem(2, 10, 24, 128), vmem(2, 8, 24, 128),
        vmem(2, 2, 16, 128), vmem(2, 6, 24, 128),
        vmem(7, 40, 128), vmem(2, 8, 40, 128), vmem(2, 8, 40, 128), vmem(8, 40, 128), vmem(8, 40, 128),
        vmem(8, 40, 128), vmem(8, 40, 128), vmem(10, 24, 128), vmem(2, 4, 48, 128),
        vmem(4, 40, 128), vmem(3, 40, 128), vmem(2, 4, 40, 128), vmem(2, 4, 40, 128), vmem(4, 40, 128),
        vmem(4, 40, 128), vmem(2, 4, 40, 128),
        vmem(3, 6, 48, 128), vmem(2, 4, 32, 128),
        pltpu.SemaphoreType.DMA((4,)),
    ]
    for count in (8, 8, 19, 2, 19):
        scratch += [pltpu.SemaphoreType.DMA((count,)), pltpu.SemaphoreType.DMA((count,))]

    def local(material, clamped, stiffness_table, eigenstrain):
        return pl.pallas_call(
            functools.partial(kernel, heights, tiles),
            out_shape=jax.ShapeDtypeStruct((3, 8, 32, 128), F32),
            in_specs=[
                pl.BlockSpec(memory_space=pltpu.HBM),
                pl.BlockSpec(memory_space=pltpu.HBM),
                pl.BlockSpec(memory_space=pltpu.HBM),
                pl.BlockSpec(memory_space=pltpu.HBM),
            ],
            out_specs=pl.BlockSpec(memory_space=pltpu.VMEM),
            scratch_shapes=scratch,
            compiler_params=pltpu.CompilerParams(
                collective_id=0, has_side_effects=True, vmem_limit_bytes=40 * 1024 * 1024
            ),
        )(*(pltpu.with_memory_space_constraint(x, pltpu.HBM) for x in (material, clamped, stiffness_table, eigenstrain)))

    in_specs = (P("height", "tile", None), P("height", "tile", None), P(), P())
    out_specs = P(None, "height", "tile", None)
    return jax.shard_map(local, mesh=mesh, in_specs=in_specs, out_specs=out_specs, check_vma=False)
```

```python
import functools

import jax
import jax.numpy as jnp
from jax import lax
from jax.experimental import pallas as pl
from jax.experimental.pallas import tpu as pltpu
from jax.sharding import PartitionSpec as P

PENALTY = 50.0
OMEGA = 0.6
KEEP = 1.0 - OMEGA
F32 = jnp.float32
BF16 = jnp.bfloat16
NEAR = ((-1, -1), (-1, 1), (1, -1), (1, 1), (-1, 0), (1, 0), (0, -1), (0, 1))
UPDOWN = ((0, -1), (0, 1))
DEEP = tuple(move for move in NEAR if move[1] != 0)
FAR = tuple(
    sorted(
        ((dt, k) for dt in (-2, -1, 0, 1, 2) for k in (0, 1, 2, 3) if (dt, k) != (0, 0)),
        key=lambda move: (-abs(move[0]), -min(move[1], 4 - move[1]), move),
    )
)


def iota(shape, axis):
    return lax.broadcasted_iota(jnp.int32, shape, axis)


def one_hot(shape, cond):
    return jnp.where(cond(iota(shape, 0), iota(shape, 1)), 1.0, 0.0).astype(BF16)


def dot(a, b):
    hi = a.astype(BF16)
    rest = a - hi.astype(F32)
    mid = rest.astype(BF16)
    lo = (rest - mid.astype(F32)).astype(BF16)
    parts = (jnp.dot(x, b, preferred_element_type=F32) for x in (lo, mid, hi))
    return sum(parts)


def kernel(
    heights,
    tiles,
    mat_hbm,
    clamp_hbm,
    table_hbm,
    eigen_hbm,
    out,
    table,
    eigen,
    mat,
    cl,
    m_lo, m_hi, m_side, m_corner, m_stage,
    q1, q1_vert, q1_side, q1_stage,
    q2, q2_own,
    b1_vert,
    b2, b2_own,
    S, SG, HZ, HR, HC, BB, WH, DD, V0, V1, RS, EX,
    S1, HZ1, HR1, HC1, BB1, WH1, DD1, VA1, VB1, RS1, PO1,
    HZ2, HR2, HC2, WH2, DD2, VA2, VB2, PO2, T1,
    S3, HZ3, HR3, HC3, WH3, BB3, V3,
    T0, R4,
    local_sem,
    m_send, m_recv, d_send, d_recv, q1_send, q1_recv, q2_send, q2_recv, b1_send, b1_recv, b2_send, b2_recv,
):
    i = lax.axis_index("tile")
    h = lax.axis_index("height")

    in_mat = pltpu.make_async_copy(mat_hbm, mat, local_sem.at[0])
    in_cl = pltpu.make_async_copy(clamp_hbm.at[pl.ds(0, 2)], cl, local_sem.at[1])
    in_table = pltpu.make_async_copy(table_hbm, table, local_sem.at[2])
    in_eigen = pltpu.make_async_copy(eigen_hbm, eigen, local_sem.at[3])

    def tile_ok(dt):
        return jnp.logical_and(i + dt >= 0, i + dt < tiles)

    def near_ok(dt, dh):
        return jnp.logical_and(tile_ok(dt), jnp.logical_and(h + dh >= 0, h + dh < heights))

    def far_id(dt, k):
        return {"tile": i + dt, "height": lax.rem(h + k, heights)}

    in_mat.start()
    barrier = pltpu.get_barrier_semaphore()
    ring = [(dt, k) for dt in (-1, 1, 0) for k in (1, 3, 0) if (dt, k) != (0, 0)]
    for dt, k in ring:
        @pl.when(tile_ok(dt))
        def _():
            pl.semaphore_signal(
                barrier, inc=1, device_id=far_id(dt, k), device_id_type=pl.DeviceIdType.MESH
            )
    reach = 3 * (tile_ok(-1).astype(jnp.int32) + tile_ok(1).astype(jnp.int32)) + 2

    in_cl.start()
    in_table.start()
    in_eigen.start()
    in_mat.wait()
    in_cl.wait()
    for side, first, edge in ((0, 0, 8), (1, 24, 23)):
        for z in range(8):
            m_stage[side, z] = mat[z, first : first + 8]
        for z in range(2):
            m_stage[side, 8 + z] = cl[z, first : first + 8]
        m_stage[side, 10] = mat[:, edge]

    pl.semaphore_wait(barrier, reach)

    def near_copies(send, recv, refs, moves=NEAR):
        copies = []
        for k, (dt, dh) in enumerate(moves):
            src, dst = refs(dt, dh)
            copy = pltpu.make_async_remote_copy(
                src_ref=src, dst_ref=dst, send_sem=send.at[k], recv_sem=recv.at[k],
                device_id={"tile": i + dt, "height": h + dh},
                device_id_type=pl.DeviceIdType.MESH,
            )
            copies.append((copy, near_ok(dt, dh), near_ok(-dt, -dh)))
        return copies

    def far_copies(send, recv, own, field):
        copies = []
        for k, (dt, dh) in enumerate(FAR):
            copy = pltpu.make_async_remote_copy(
                src_ref=own,
                dst_ref=field.at[pl.ds(2 * h, 2), pl.ds(8 * (2 - dt), 8)],
                send_sem=send.at[k], recv_sem=recv.at[k],
                device_id=far_id(dt, dh), device_id_type=pl.DeviceIdType.MESH,
            )
            copies.append((copy, tile_ok(dt), tile_ok(-dt)))
        return copies

    def start(copies):
        for copy, sends, _ in copies:
            @pl.when(sends)
            def _():
                copy.start()

    def wait_recv(copies):
        for copy, _, receives in copies:
            @pl.when(receives)
            def _():
                copy.wait_recv()

    def wait_send(copies):
        for copy, sends, _ in copies:
            @pl.when(sends)
            def _():
                copy.wait_send()

    def label_refs(dt, dh):
        if dt == 0:
            if dh > 0:
                return mat.at[pl.ds(5, 3)], m_lo.at[pl.ds(4, 3)]
            return mat.at[pl.ds(0, 3)], m_hi.at[pl.ds(0, 3)]
        side = 0 if dt < 0 else 1
        if dh == 0:
            return m_stage.at[side], m_side.at[side]
        if dh > 0:
            return m_stage.at[side, pl.ds(5, 3)], m_corner.at[side, 1, pl.ds(4, 3)]
        return m_stage.at[side, pl.ds(0, 3)], m_corner.at[side, 0, pl.ds(0, 3)]

    def deep_refs(dt, dh):
        if dt == 0:
            if dh > 0:
                return mat.at[pl.ds(1, 4)], m_lo.at[pl.ds(0, 4)]
            return mat.at[pl.ds(3, 4)], m_hi.at[pl.ds(3, 4)]
        side = 0 if dt < 0 else 1
        if dh > 0:
            return m_stage.at[side, pl.ds(1, 4)], m_corner.at[side, 1, pl.ds(0, 4)]
        return m_stage.at[side, pl.ds(3, 4)], m_corner.at[side, 0, pl.ds(3, 4)]

    label_moves = near_copies(m_send, m_recv, label_refs)
    start(label_moves)
    deep_moves = near_copies(d_send, d_recv, deep_refs, DEEP)
    start(deep_moves)
    in_table.wait()
    in_eigen.wait()

    st = [table[n] for n in range(3)]
    stress = [[table[n] * eigen[n, c] for c in range(3)] for n in range(3)]

    def look(m, values):
        return jnp.where(
            m == 0, values[0], jnp.where(m == 1, values[1], jnp.where(m == 2, values[2], 0.0))
        )

    take_lo = one_hot((128, 128), lambda l, j: jnp.logical_and(j < 64, l // 2 == j))
    take_hi = one_hot((128, 128), lambda l, j: l // 2 == j - 64)
    lowest = jnp.where(h == 0, 1.0, 0.0).astype(F32)

    for z in range(4):
        R4[0, z] = look(mat[2 * z], st) + look(mat[2 * z + 1], st)
    R4[1, 0] = (cl[0] + cl[1]).astype(F32)
    s_rows = jnp.concatenate(
        [R4[0, z, pl.ds(0, 16, 2)] + R4[0, z, pl.ds(1, 16, 2)] for z in range(4)], axis=0
    )
    p_rows = R4[1, 0, pl.ds(0, 16, 2)] + R4[1, 0, pl.ds(1, 16, 2)]
    s_one = dot(0.5 * s_rows, take_lo).reshape(4, 16, 128)
    p_one = dot((2.0 * PENALTY * lowest) * p_rows, take_hi)
    q1[0] = s_one[0] + p_one
    for z in range(1, 4):
        q1[z] = s_one[z]
    for z in range(4):
        q1_stage[0, z] = q1[z, 0:4]
        q1_stage[1, z] = q1[z, 12:16]

    def q1_refs(dt, dh):
        if dt == 0:
            return q1, q1_vert.at[0 if dh > 0 else 1]
        side = 0 if dt < 0 else 1
        return q1_stage.at[side], q1_side.at[side, dh + 1]

    q1_moves = near_copies(q1_send, q1_recv, q1_refs)
    start(q1_moves)

    for z in range(2):
        R4[1, z, 0:16] = q1[2 * z] + q1[2 * z + 1]
    q_rows = jnp.concatenate(
        [R4[1, z, pl.ds(0, 8, 2)] + R4[1, z, pl.ds(1, 8, 2)] for z in range(2)], axis=0
    )
    l, j = iota((128, 128), 0), iota((128, 128), 1)
    down_q = jnp.where(
        jnp.logical_and(j < 96, jnp.logical_and(l < 64, l // 2 == j % 32)), 0.5,
        jnp.where(jnp.logical_and(j >= 96, l // 2 == j - 64), 1.0, 0.0),
    ).astype(BF16)
    q2_own[...] = dot(q_rows, down_q).reshape(2, 8, 128)
    q2_moves = far_copies(q2_send, q2_recv, q2_own, q2)
    q2[pl.ds(2 * h, 2), 16:24] = q2_own[...]

    lane = iota((48, 128), 1)
    row = iota((48, 128), 0)
    sub8 = iota((8, 128), 0)
    wait_recv(label_moves)
    start(q2_moves)
    below, above = h > 0, h < heights - 1
    before, after = i > 0, i < tiles - 1

    def labels(z):
        if 0 <= z < 8:
            centre, hi, lo = mat[z], m_side[0, z], m_side[1, z]
            centre_ok, hi_ok, lo_ok = None, after, before
        else:
            centre_ok = below if z < 0 else above
            end = 1 if z < 0 else 0
            k = z + 7 if z < 0 else z - 8
            centre = jnp.where(centre_ok, (m_lo if z < 0 else m_hi)[k], -1)
            hi, lo = m_corner[0, end, k], m_corner[1, end, k]
            hi_ok, lo_ok = jnp.logical_and(centre_ok, after), jnp.logical_and(centre_ok, before)
        return jnp.concatenate([centre, jnp.where(hi_ok, hi, -1), jnp.where(lo_ok, lo, -1)], axis=0)

    def build(zs):
        for z in zs:
            m = labels(z)
            S[z + 7] = look(m, st)
            for c in range(3):
                SG[c, z + 7] = look(m, [stress[n][c] for n in range(3)])

    build(range(-3, 11))
    for side, ok in ((0, after), (1, before)):
        m = jnp.where(ok, m_side[side, 10], -1)
        EX[side, 0] = look(m, st)
        EX[side, 1] = look(m, [stress[n][1] for n in range(3)])
    def between(zs):
        for z in zs:
            HZ[z + 7] = S[z + 7] + S[z + 8]

    between(range(-3, 10))

    def spring0(z):
        sides = jnp.concatenate(
            [jnp.where(after, m_side[0, 8 + z], 0), jnp.where(before, m_side[1, 8 + z], 0)],
            axis=0,
        )
        return (2.0 * PENALTY * lowest) * jnp.concatenate([cl[z], sides], axis=0).astype(F32)

    def first_sweep(z):
        s = S[z + 7]
        s_r = pltpu.roll(s, 47, 0)
        if 0 <= z < 8:
            s_r = jnp.where(row == 39, EX[0, 0, z : z + 1], s_r)
        s_c = jnp.where(lane < 127, pltpu.roll(s, 127, 1), 0.0)
        h_ru = s + s_r
        h_rl = pltpu.roll(h_ru, 1, 0)
        if 0 <= z < 8:
            h_rl = jnp.where(row == 40, s + EX[1, 0, z : z + 1], h_rl)
        f_cu = s + s_c
        f_cl = s + jnp.where(lane > 0, pltpu.roll(s, 1, 1), 0.0)
        HR[0, z + 6] = h_rl
        HR[1, z + 6] = h_ru
        HC[0, z + 6] = jnp.where(lane > 0, f_cl, 0.0)
        HC[1, z + 6] = jnp.where(lane < 127, f_cu, 0.0)
        f = [HZ[z + 6] + HZ[z + 7], h_rl + h_ru, f_cl + f_cu]
        total = f[0] + f[1] + f[2]
        if 0 <= z < 2:
            total = total + spring0(z)
        g0 = SG[0, z + 6] - SG[0, z + 8]
        x = SG[1, z + 7]
        x_l, x_u = pltpu.roll(x, 1, 0), pltpu.roll(x, 47, 0)
        if 0 <= z < 8:
            x_l = jnp.where(row == 40, EX[1, 1, z : z + 1], x_l)
            x_u = jnp.where(row == 39, EX[0, 1, z : z + 1], x_u)
        g1 = x_l - x_u
        x = SG[2, z + 7]
        g2 = jnp.where(lane > 0, pltpu.roll(x, 1, 1), 0.0) - jnp.where(
            lane < 127, pltpu.roll(x, 127, 1), 0.0
        )
        for c, g in enumerate((g0, g1, g2)):
            d = total + f[c]
            w = jnp.where(s > 0.0, OMEGA / jnp.where(s > 0.0, d, 1.0), 0.0)
            BB[c, z + 6] = g
            WH[c, z + 6] = w
            if -4 <= z < 12:
                DD[c, z + 4] = d
            V0[c, z + 6] = w * g

    for z in range(-2, 10):
        first_sweep(z)

    def apply0(v, off, c, z):
        x = v[c, z + off]
        a = HZ[z + 6] * v[c, z + off - 1] + HZ[z + 7] * v[c, z + off + 1]
        b = HR[0, z + 6] * pltpu.roll(x, 1, 0) + HR[1, z + 6] * pltpu.roll(x, 47, 0)
        e = HC[0, z + 6] * pltpu.roll(x, 1, 1) + HC[1, z + 6] * pltpu.roll(x, 127, 1)
        return x, (a + b + e) + (a, b, e)[c]

    def second_sweep(zs):
        for z in zs:
            for c in range(3):
                x, n = apply0(V0, 6, c, z)
                V1[c, z + 5] = KEEP * x + WH[c, z + 6] * (BB[c, z + 6] + n)

    def pairs(ref, c, z, n):
        return ref[c, z, pl.ds(0, n, 2)] + ref[c, z, pl.ds(1, n, 2)]

    def restrict(zs):
        for z in zs:
            for c in range(3):
                total = None
                for k in range(2):
                    x, n = apply0(V1, 5, c, 2 * z + k)
                    r = BB[c, 2 * z + k + 6] + n - DD[c, 2 * z + k + 4] * x
                    total = r if total is None else total + r
                RS[c, z + 2] = total
            BB1[0, z + 3] = dot(pairs(RS, 0, z + 2, 24), take_lo) + dot(pairs(RS, 1, z + 2, 24), take_hi)
            BB1[1, z + 3] = dot(pairs(RS, 2, z + 2, 24), take_lo)

    second_sweep(range(-1, 9))
    restrict(range(0, 4))

    def b1_refs(dt, dh):
        return BB1.at[:, 4 if dh > 0 else 5], b1_vert.at[0 if dh > 0 else 1]

    b1_moves = near_copies(b1_send, b1_recv, b1_refs, UPDOWN)
    start(b1_moves)

    wait_recv(deep_moves)
    build((*range(-7, -3), *range(11, 15)))
    between((*range(-7, -3), *range(10, 14)))
    for z in (*range(-6, -2), *range(10, 14)):
        first_sweep(z)
    second_sweep((*range(-5, -1), *range(9, 13)))
    restrict((-2, -1, 4, 5))

    lane1 = iota((24, 128), 1)
    col1 = lane1 % 64
    wait_recv(q1_moves)

    def both(x):
        return jnp.where(iota(x.shape, len(x.shape) - 1) < 64, x, 0.0)

    for z in range(-4, 8):
        if z < 0:
            centre = jnp.where(below, q1_vert[0, z + 4], 0.0)
            lo = jnp.where(jnp.logical_and(below, before), q1_side[1, 2, z + 4], 0.0)
            hi = jnp.where(jnp.logical_and(below, after), q1_side[0, 2, z + 4], 0.0)
        elif z < 4:
            centre = q1[z]
            lo = jnp.where(before, q1_side[1, 1, z], 0.0)
            hi = jnp.where(after, q1_side[0, 1, z], 0.0)
        else:
            centre = jnp.where(above, q1_vert[1, z - 4], 0.0)
            lo = jnp.where(jnp.logical_and(above, before), q1_side[1, 0, z - 4], 0.0)
            hi = jnp.where(jnp.logical_and(above, after), q1_side[0, 0, z - 4], 0.0)
        q = jnp.concatenate([centre, hi, lo], axis=0)
        other = pltpu.roll(q, 64, 1)
        S1[z + 4] = jnp.where(lane1 < 64, q, other)
        if z == 0:
            spring1 = jnp.where(lane1 < 64, other, q)
    for z in range(-4, 7):
        HZ1[z + 4] = S1[z + 4] + S1[z + 5]
    for z in range(-3, 7):
        s = S1[z + 4]
        h_ru = s + pltpu.roll(s, 23, 0)
        h_rl = pltpu.roll(h_ru, 1, 0)
        f_cu = s + jnp.where(col1 < 63, pltpu.roll(s, 127, 1), 0.0)
        f_cl = s + jnp.where(col1 > 0, pltpu.roll(s, 1, 1), 0.0)
        HR1[0, z + 3] = h_rl
        HR1[1, z + 3] = h_ru
        HC1[0, z + 3] = jnp.where(col1 > 0, f_cl, 0.0)
        HC1[1, z + 3] = jnp.where(col1 < 63, f_cu, 0.0)
        f = [HZ1[z + 3] + HZ1[z + 4], h_rl + h_ru, f_cl + f_cu]
        total = f[0] + f[1] + f[2]
        if z == 0:
            total = total + spring1
        for t in range(2):
            d = total + (jnp.where(lane1 < 64, f[0], f[1]) if t == 0 else f[2])
            WH1[t, z + 3] = jnp.where(s > 0.0, OMEGA / jnp.where(s > 0.0, d, 1.0), 0.0)
            if 0 <= z < 4:
                DD1[t, z] = d

    for z in range(-2, 6):
        for t in range(2):
            if z < 0:
                BB1[t, z + 3] = jnp.where(below, BB1[t, z + 3], 0.0)
            if z > 3:
                BB1[t, z + 3] = jnp.where(above, BB1[t, z + 3], 0.0)
            VA1[t, z + 3] = WH1[t, z + 3] * BB1[t, z + 3]

    def apply1(v, off, t, z):
        x = v[t, z + off]
        a = HZ1[z + 3] * v[t, z + off - 1] + HZ1[z + 4] * v[t, z + off + 1]
        b = HR1[0, z + 3] * pltpu.roll(x, 1, 0) + HR1[1, z + 3] * pltpu.roll(x, 23, 0)
        e = HC1[0, z + 3] * pltpu.roll(x, 1, 1) + HC1[1, z + 3] * pltpu.roll(x, 127, 1)
        return x, (a + b + e) + (jnp.where(lane1 < 64, a, b) if t == 0 else e)

    def second_sweep1(zs):
        for z in zs:
            for t in range(2):
                x, n = apply1(VA1, 3, t, z)
                VB1[t, z + 2] = KEEP * x + WH1[t, z + 3] * (BB1[t, z + 3] + n)

    second_sweep1(range(-1, 5))
    down_a = one_hot((128, 128), lambda l, j: l // 2 == j)
    down_b = one_hot((128, 128), lambda l, j: jnp.logical_and(l < 64, l // 2 == j - 64))
    for z in range(2):
        for t in range(2):
            total = None
            for k in range(2):
                x, n = apply1(VB1, 2, t, 2 * z + k)
                r = BB1[t, 2 * z + k + 3] + n - DD1[t, 2 * z + k] * x
                total = r[0:16] if total is None else total + r[0:16]
            RS1[t, z] = total
        b2_own[z] = dot(pairs(RS1, 0, z, 8), down_a) + dot(pairs(RS1, 1, z, 8), down_b)
    b2_moves = far_copies(b2_send, b2_recv, b2_own, b2)
    start(b2_moves)
    b2[pl.ds(2 * h, 2), 16:24] = b2_own[...]

    wait_recv(b1_moves)
    for t in range(2):
        VA1[t, 0] = WH1[t, 0] * jnp.where(below, b1_vert[0, t], 0.0)
        VA1[t, 9] = WH1[t, 9] * jnp.where(above, b1_vert[1, t], 0.0)
    second_sweep1((-2, 5))

    lane2 = iota((40, 128), 1)
    row2 = iota((40, 128), 0)
    col2 = lane2 % 32
    real = lane2 < 96
    slot = row2 // 8 + (i - 2)
    inside = jnp.logical_and(slot >= 0, slot < tiles)
    keep = jnp.logical_and(inside, real)
    wait_recv(q2_moves)

    def pick(a, b, e):
        return jnp.where(lane2 < 32, a, jnp.where(lane2 < 64, b, e))

    q = jnp.where(inside, q2[0], 0.0)
    spring2 = pick(pltpu.roll(q, 32, 1), pltpu.roll(q, 64, 1), pltpu.roll(q, 96, 1))
    odd_row, odd_col = row2 % 2 == 1, lane2 % 2 == 1

    def pair_sum(x):
        x = x + jnp.where(odd_row, pltpu.roll(x, 1, 0), pltpu.roll(x, 39, 0))
        return x + jnp.where(odd_col, pltpu.roll(x, 1, 1), pltpu.roll(x, 127, 1))

    def faces(s_of, depth, step, spring, hz, hr, hc, wh, dd):
        for z in range(depth - 1):
            hz[z] = s_of(z) + s_of(z + 1)
        for z in range(depth):
            s = s_of(z)
            h_ru = s + pltpu.roll(s, 40 - step, 0)
            h_rl = pltpu.roll(h_ru, step, 0)
            first, last = col2 < step, col2 >= 32 - step
            f_cu = s + jnp.where(last, 0.0, pltpu.roll(s, 128 - step, 1))
            f_cl = s + jnp.where(first, 0.0, pltpu.roll(s, step, 1))
            hr[0, z] = h_rl
            hr[1, z] = h_ru
            hc[0, z] = jnp.where(first, 0.0, f_cl)
            hc[1, z] = jnp.where(last, 0.0, f_cu)
            f_z = (hz[z - 1] if z > 0 else s) + (hz[z] if z < depth - 1 else s)
            f_r, f_c = h_rl + h_ru, f_cl + f_cu
            d = (f_z + f_r + f_c) + pick(f_z, f_r, f_c)
            if z == 0:
                d = d + spring
            wh[z] = jnp.where(s > 0.0, OMEGA / jnp.where(s > 0.0, d, 1.0), 0.0)
            if dd is not None:
                dd[z] = d

    def s2(z):
        return jnp.where(keep, q2[z], 0.0)

    faces(s2, 8, 1, spring2, HZ2, HR2, HC2, WH2, DD2)
    for z in range(4):
        S3[z] = 0.5 * pair_sum(s2(2 * z) + s2(2 * z + 1))
    faces(lambda z: S3[z], 4, 2, pair_sum(spring2), HZ3, HR3, HC3, WH3, None)

    def apply2(v, z, depth, step, hz, hr, hc):
        x = v[z]
        a = None
        if z > 0:
            a = hz[z - 1] * v[z - 1]
        if z < depth - 1:
            up = hz[z] * v[z + 1]
            a = up if a is None else a + up
        b = hr[0, z] * pltpu.roll(x, step, 0) + hr[1, z] * pltpu.roll(x, 40 - step, 0)
        e = hc[0, z] * pltpu.roll(x, step, 1) + hc[1, z] * pltpu.roll(x, 128 - step, 1)
        return x, (a + b + e) + pick(a, b, e)

    wait_recv(b2_moves)
    for z in range(8):
        b = jnp.where(keep, b2[z], 0.0)
        b2[z] = b
        VA2[z] = WH2[z] * b
    for z in range(8):
        x, n = apply2(VA2, z, 8, 1, HZ2, HR2, HC2)
        VB2[z] = KEEP * x + WH2[z] * (b2[z] + n)
    for z in range(4):
        total = None
        for k in range(2):
            x, n = apply2(VB2, 2 * z + k, 8, 1, HZ2, HR2, HC2)
            r = b2[2 * z + k] + n - DD2[2 * z + k] * x
            total = r if total is None else total + r
        total = pair_sum(total)
        BB3[z] = total
        V3[0, z] = WH3[z] * total
    for turn in range(5):
        now, later = turn % 2, (turn + 1) % 2
        for z in range(4):
            x, n = apply2(V3.at[now], z, 4, 2, HZ3, HR3, HC3)
            V3[later, z] = KEEP * x + WH3[z] * (BB3[z] + n)
    for z in range(8):
        VB2[z] = VB2[z] + V3[1, z // 2]
    PO2[0] = jnp.zeros((24, 128), F32)
    PO2[9] = jnp.zeros((24, 128), F32)
    for z in range(8):
        x, n = apply2(VB2, z, 8, 1, HZ2, HR2, HC2)
        PO2[z + 1] = (KEEP * x + WH2[z] * (b2[z] + n))[8:32]

    up_a = one_hot((128, 128), lambda l, j: l == j // 2)
    up_b = one_hot((128, 128), lambda l, j: jnp.logical_and(j < 64, l == 64 + j // 2))
    for k in range(4):
        coarse = PO2[2 * h + k]
        for t, m in enumerate((up_a, up_b)):
            e = dot(coarse, m)
            T1[t, k, pl.ds(0, 24, 2)] = e
            T1[t, k, pl.ds(1, 24, 2)] = e
            tail = jnp.where(sub8 < 4, T1[t, k, 32:40], T1[t, k, 8:16])
            e = jnp.concatenate([T1[t, k, 16:32], tail], axis=0)
            for z in (2 * k, 2 * k + 1):
                VB1[t, z] = VB1[t, z] + e
    for z in range(-1, 5):
        for t in range(2):
            x, n = apply1(VB1, 2, t, z)
            PO1[t, z + 1] = KEEP * x + WH1[t, z + 3] * (BB1[t, z + 3] + n)

    up_lo = one_hot((128, 128), lambda l, j: l == j // 2)
    up_hi = one_hot((128, 128), lambda l, j: l == 64 + j // 2)
    for k in range(6):
        for c in range(3):
            e = dot(PO1[c // 2, k], up_hi if c == 1 else up_lo)
            T0[c, k, pl.ds(0, 24, 2)] = e
            T0[c, k, pl.ds(1, 24, 2)] = e
            for z in (2 * k - 2, 2 * k - 1):
                if -1 <= z < 9:
                    V1[c, z + 5] = V1[c, z + 5] + T0[c, k]
    for z in range(8):
        for c in range(3):
            x, n = apply0(V1, 5, c, z)
            out[c, z] = (KEEP * x + WH[c, z + 6] * (BB[c, z + 6] + n))[0:32]

    for moves in (label_moves, deep_moves, q1_moves, q2_moves, b1_moves, b2_moves):
        wait_send(moves)


def solution(mesh):
    heights, tiles = mesh.shape["height"], mesh.shape["tile"]

    def vmem(*shape, dtype=F32):
        return pltpu.VMEM(shape, dtype)

    i32 = jnp.int32
    scratch = [
        pltpu.SMEM((3,), F32), pltpu.SMEM((3, 3), F32),
        vmem(8, 32, 128, dtype=i32), vmem(2, 32, 128, dtype=i32),
        vmem(7, 32, 128, dtype=i32), vmem(7, 32, 128, dtype=i32),
        vmem(2, 11, 8, 128, dtype=i32), vmem(2, 2, 7, 8, 128, dtype=i32), vmem(2, 11, 8, 128, dtype=i32),
        vmem(4, 16, 128), vmem(2, 4, 16, 128), vmem(2, 3, 4, 4, 128), vmem(2, 4, 4, 128),
        vmem(8, 40, 128), vmem(2, 8, 128),
        vmem(2, 2, 24, 128),
        vmem(8, 40, 128), vmem(2, 8, 128),
        vmem(22, 48, 128), vmem(3, 22, 48, 128), vmem(21, 48, 128), vmem(2, 20, 48, 128), vmem(2, 20, 48, 128),
        vmem(3, 20, 48, 128), vmem(3, 20, 48, 128), vmem(3, 16, 48, 128), vmem(3, 20, 48, 128),
        vmem(3, 18, 48, 128), vmem(3, 8, 48, 128), vmem(2, 2, 8, 128),
        vmem(12, 24, 128), vmem(11, 24, 128), vmem(2, 10, 24, 128), vmem(2, 10, 24, 128), vmem(2, 10, 24, 128),
        vmem(2, 10, 24, 128), vmem(2, 4, 24, 128), vmem(2, 10, 24, 128), vmem(2, 8, 24, 128),
        vmem(2, 2, 16, 128), vmem(2, 6, 24, 128),
        vmem(7, 40, 128), vmem(2, 8, 40, 128), vmem(2, 8, 40, 128), vmem(8, 40, 128), vmem(8, 40, 128),
        vmem(8, 40, 128), vmem(8, 40, 128), vmem(10, 24, 128), vmem(2, 4, 48, 128),
        vmem(4, 40, 128), vmem(3, 40, 128), vmem(2, 4, 40, 128), vmem(2, 4, 40, 128), vmem(4, 40, 128),
        vmem(4, 40, 128), vmem(2, 4, 40, 128),
        vmem(3, 6, 48, 128), vmem(2, 4, 32, 128),
        pltpu.SemaphoreType.DMA((4,)),
    ]
    for count in (8, 6, 8, 19, 2, 19):
        scratch += [pltpu.SemaphoreType.DMA((count,)), pltpu.SemaphoreType.DMA((count,))]

    def local(material, clamped, stiffness_table, eigenstrain):
        return pl.pallas_call(
            functools.partial(kernel, heights, tiles),
            out_shape=jax.ShapeDtypeStruct((3, 8, 32, 128), F32),
            in_specs=[
                pl.BlockSpec(memory_space=pltpu.HBM),
                pl.BlockSpec(memory_space=pltpu.HBM),
                pl.BlockSpec(memory_space=pltpu.HBM),
                pl.BlockSpec(memory_space=pltpu.HBM),
            ],
            out_specs=pl.BlockSpec(memory_space=pltpu.VMEM),
            scratch_shapes=scratch,
            compiler_params=pltpu.CompilerParams(
                collective_id=0, has_side_effects=True, vmem_limit_bytes=40 * 1024 * 1024
            ),
        )(*(pltpu.with_memory_space_constraint(x, pltpu.HBM) for x in (material, clamped, stiffness_table, eigenstrain)))

    in_specs = (P("height", "tile", None), P("height", "tile", None), P(), P())
    out_specs = P(None, "height", "tile", None)
    return jax.shard_map(local, mesh=mesh, in_specs=in_specs, out_specs=out_specs, check_vma=False)
```

```python
import functools

import jax
import jax.numpy as jnp
from jax import lax
from jax.experimental import pallas as pl
from jax.experimental.pallas import tpu as pltpu
from jax.sharding import PartitionSpec as P

PENALTY = 50.0
OMEGA = 0.6
KEEP = 1.0 - OMEGA
F32 = jnp.float32
BF16 = jnp.bfloat16
NEAR = ((-1, -1), (-1, 1), (1, -1), (1, 1), (-1, 0), (1, 0), (0, -1), (0, 1))
UPDOWN = ((0, -1), (0, 1))
DEEP = tuple(move for move in NEAR if move[1] != 0)
FAR = tuple(
    sorted(
        ((dt, k) for dt in (-2, -1, 0, 1, 2) for k in (0, 1, 2, 3) if (dt, k) != (0, 0)),
        key=lambda move: (-abs(move[0]), -min(move[1], 4 - move[1]), move),
    )
)


def iota(shape, axis):
    return lax.broadcasted_iota(jnp.int32, shape, axis)


def one_hot(shape, cond):
    return jnp.where(cond(iota(shape, 0), iota(shape, 1)), 1.0, 0.0).astype(BF16)


def dot(a, b):
    hi = a.astype(BF16)
    rest = a - hi.astype(F32)
    mid = rest.astype(BF16)
    lo = (rest - mid.astype(F32)).astype(BF16)
    parts = (jnp.dot(x, b, preferred_element_type=F32) for x in (lo, mid, hi))
    return sum(parts)


def kernel(
    heights,
    tiles,
    mat_hbm,
    clamp_hbm,
    table_hbm,
    eigen_hbm,
    out,
    table,
    eigen,
    mat,
    cl,
    m_lo, m_hi, m_side, m_corner, m_stage,
    q1, q1_vert, q1_side, q1_stage,
    q2, q2_own,
    b1_vert,
    b2, b2_own,
    S, SG, HZ, HR, HC, BB, WH, DD, V0, V1, RS, EX,
    S1, HZ1, HR1, HC1, BB1, WH1, DD1, VA1, VB1, RS1, PO1,
    HZ2, HR2, HC2, WH2, DD2, VA2, VB2, PO2, T1,
    S3, HZ3, HR3, HC3, WH3, BB3, V3,
    T0, R4,
    local_sem,
    met,
    m_send, m_recv, d_send, d_recv, q1_send, q1_recv, q2_send, q2_recv, b1_send, b1_recv, b2_send, b2_recv,
):
    i = lax.axis_index("tile")
    h = lax.axis_index("height")

    in_mat = pltpu.make_async_copy(mat_hbm, mat, local_sem.at[0])
    in_cl = pltpu.make_async_copy(clamp_hbm.at[pl.ds(0, 2)], cl, local_sem.at[1])
    in_table = pltpu.make_async_copy(table_hbm, table, local_sem.at[2])
    in_eigen = pltpu.make_async_copy(eigen_hbm, eigen, local_sem.at[3])

    def tile_ok(dt):
        return jnp.logical_and(i + dt >= 0, i + dt < tiles)

    def near_ok(dt, dh):
        return jnp.logical_and(tile_ok(dt), jnp.logical_and(h + dh >= 0, h + dh < heights))

    def far_id(dt, k):
        return {"tile": i + dt, "height": lax.rem(h + k, heights)}

    in_mat.start()
    barrier = pltpu.get_barrier_semaphore()
    for dt, dh in NEAR:
        @pl.when(near_ok(dt, dh))
        def _():
            pl.semaphore_signal(
                barrier, inc=1, device_id={"tile": i + dt, "height": h + dh},
                device_id_type=pl.DeviceIdType.MESH,
            )
    reach = sum(near_ok(dt, dh).astype(jnp.int32) for dt, dh in NEAR)

    in_cl.start()
    in_table.start()
    in_eigen.start()
    in_mat.wait()
    in_cl.wait()
    for side, first, edge in ((0, 0, 8), (1, 24, 23)):
        for z in range(8):
            m_stage[side, z] = mat[z, first : first + 8]
        for z in range(2):
            m_stage[side, 8 + z] = cl[z, first : first + 8]
        m_stage[side, 10] = mat[:, edge]

    pl.semaphore_wait(barrier, reach)

    def near_copies(send, recv, refs, moves=NEAR):
        copies = []
        for k, (dt, dh) in enumerate(moves):
            src, dst = refs(dt, dh)
            copy = pltpu.make_async_remote_copy(
                src_ref=src, dst_ref=dst, send_sem=send.at[k], recv_sem=recv.at[k],
                device_id={"tile": i + dt, "height": h + dh},
                device_id_type=pl.DeviceIdType.MESH,
            )
            copies.append((copy, near_ok(dt, dh), near_ok(-dt, -dh)))
        return copies

    def far_copies(send, recv, own, field):
        copies = []
        for k, (dt, dh) in enumerate(FAR):
            copy = pltpu.make_async_remote_copy(
                src_ref=own,
                dst_ref=field.at[pl.ds(2 * h, 2), pl.ds(8 * (2 - dt), 8)],
                send_sem=send.at[k], recv_sem=recv.at[k],
                device_id=far_id(dt, dh), device_id_type=pl.DeviceIdType.MESH,
            )
            copies.append((copy, tile_ok(dt), tile_ok(-dt)))
        return copies

    def start_far(copies, apart):
        for (_, dh), (copy, sends, _) in zip(FAR, copies):
            if dh == 1:
                wide = h == heights - 1
            elif dh == 3:
                wide = h == 0
            elif apart:
                continue
            else:
                wide = h < 0

            @pl.when(jnp.logical_and(sends, wide if apart else jnp.logical_not(wide)))
            def _():
                copy.start()

    def start(copies):
        for copy, sends, _ in copies:
            @pl.when(sends)
            def _():
                copy.start()

    def wait_recv(copies):
        for copy, _, receives in copies:
            @pl.when(receives)
            def _():
                copy.wait_recv()

    def wait_send(copies):
        for copy, sends, _ in copies:
            @pl.when(sends)
            def _():
                copy.wait_send()

    def label_refs(dt, dh):
        if dt == 0:
            if dh > 0:
                return mat.at[pl.ds(5, 3)], m_lo.at[pl.ds(4, 3)]
            return mat.at[pl.ds(0, 3)], m_hi.at[pl.ds(0, 3)]
        side = 0 if dt < 0 else 1
        if dh == 0:
            return m_stage.at[side], m_side.at[side]
        if dh > 0:
            return m_stage.at[side, pl.ds(5, 3)], m_corner.at[side, 1, pl.ds(4, 3)]
        return m_stage.at[side, pl.ds(0, 3)], m_corner.at[side, 0, pl.ds(0, 3)]

    def deep_refs(dt, dh):
        if dt == 0:
            if dh > 0:
                return mat.at[pl.ds(1, 4)], m_lo.at[pl.ds(0, 4)]
            return mat.at[pl.ds(3, 4)], m_hi.at[pl.ds(3, 4)]
        side = 0 if dt < 0 else 1
        if dh > 0:
            return m_stage.at[side, pl.ds(1, 4)], m_corner.at[side, 1, pl.ds(0, 4)]
        return m_stage.at[side, pl.ds(3, 4)], m_corner.at[side, 0, pl.ds(3, 4)]

    label_moves = near_copies(m_send, m_recv, label_refs)
    start(label_moves)
    deep_moves = near_copies(d_send, d_recv, deep_refs, DEEP)
    start(deep_moves)
    in_table.wait()
    in_eigen.wait()

    st = [table[n] for n in range(3)]
    stress = [[table[n] * eigen[n, c] for c in range(3)] for n in range(3)]

    def look(m, values):
        return jnp.where(
            m == 0, values[0], jnp.where(m == 1, values[1], jnp.where(m == 2, values[2], 0.0))
        )

    take_lo = one_hot((128, 128), lambda l, j: jnp.logical_and(j < 64, l // 2 == j))
    take_hi = one_hot((128, 128), lambda l, j: l // 2 == j - 64)
    lowest = jnp.where(h == 0, 1.0, 0.0).astype(F32)

    for z in range(4):
        R4[0, z] = look(mat[2 * z], st) + look(mat[2 * z + 1], st)
    R4[1, 0] = (cl[0] + cl[1]).astype(F32)
    s_rows = jnp.concatenate(
        [R4[0, z, pl.ds(0, 16, 2)] + R4[0, z, pl.ds(1, 16, 2)] for z in range(4)], axis=0
    )
    p_rows = R4[1, 0, pl.ds(0, 16, 2)] + R4[1, 0, pl.ds(1, 16, 2)]
    s_one = dot(0.5 * s_rows, take_lo).reshape(4, 16, 128)
    p_one = dot((2.0 * PENALTY * lowest) * p_rows, take_hi)
    q1[0] = s_one[0] + p_one
    for z in range(1, 4):
        q1[z] = s_one[z]
    for z in range(4):
        q1_stage[0, z] = q1[z, 0:4]
        q1_stage[1, z] = q1[z, 12:16]

    def q1_refs(dt, dh):
        if dt == 0:
            return q1, q1_vert.at[0 if dh > 0 else 1]
        side = 0 if dt < 0 else 1
        return q1_stage.at[side], q1_side.at[side, dh + 1]

    q1_moves = near_copies(q1_send, q1_recv, q1_refs)
    start(q1_moves)

    for z in range(2):
        R4[1, z, 0:16] = q1[2 * z] + q1[2 * z + 1]
    q_rows = jnp.concatenate(
        [R4[1, z, pl.ds(0, 8, 2)] + R4[1, z, pl.ds(1, 8, 2)] for z in range(2)], axis=0
    )
    l, j = iota((128, 128), 0), iota((128, 128), 1)
    down_q = jnp.where(
        jnp.logical_and(j < 96, jnp.logical_and(l < 64, l // 2 == j % 32)), 0.5,
        jnp.where(jnp.logical_and(j >= 96, l // 2 == j - 64), 1.0, 0.0),
    ).astype(BF16)
    q2_own[...] = dot(q_rows, down_q).reshape(2, 8, 128)
    q2_moves = far_copies(q2_send, q2_recv, q2_own, q2)
    q2[pl.ds(2 * h, 2), 16:24] = q2_own[...]

    lane = iota((48, 128), 1)
    row = iota((48, 128), 0)
    sub8 = iota((8, 128), 0)
    wait_recv(label_moves)
    for dh in (-1, 1):
        @pl.when(near_ok(0, dh))
        def _():
            pl.semaphore_signal(
                met, inc=1, device_id={"tile": i, "height": h + dh},
                device_id_type=pl.DeviceIdType.MESH,
            )
    start_far(q2_moves, False)
    below, above = h > 0, h < heights - 1
    before, after = i > 0, i < tiles - 1

    def labels(z):
        if 0 <= z < 8:
            centre, hi, lo = mat[z], m_side[0, z], m_side[1, z]
            centre_ok, hi_ok, lo_ok = None, after, before
        else:
            centre_ok = below if z < 0 else above
            end = 1 if z < 0 else 0
            k = z + 7 if z < 0 else z - 8
            centre = jnp.where(centre_ok, (m_lo if z < 0 else m_hi)[k], -1)
            hi, lo = m_corner[0, end, k], m_corner[1, end, k]
            hi_ok, lo_ok = jnp.logical_and(centre_ok, after), jnp.logical_and(centre_ok, before)
        return jnp.concatenate([centre, jnp.where(hi_ok, hi, -1), jnp.where(lo_ok, lo, -1)], axis=0)

    def build(zs):
        for z in zs:
            m = labels(z)
            S[z + 7] = look(m, st)
            for c in range(3):
                SG[c, z + 7] = look(m, [stress[n][c] for n in range(3)])

    build(range(-3, 11))
    for side, ok in ((0, after), (1, before)):
        m = jnp.where(ok, m_side[side, 10], -1)
        EX[side, 0] = look(m, st)
        EX[side, 1] = look(m, [stress[n][1] for n in range(3)])
    def between(zs):
        for z in zs:
            HZ[z + 7] = S[z + 7] + S[z + 8]

    between(range(-3, 10))

    def spring0(z):
        sides = jnp.concatenate(
            [jnp.where(after, m_side[0, 8 + z], 0), jnp.where(before, m_side[1, 8 + z], 0)],
            axis=0,
        )
        return (2.0 * PENALTY * lowest) * jnp.concatenate([cl[z], sides], axis=0).astype(F32)

    def first_sweep(z):
        s = S[z + 7]
        s_r = pltpu.roll(s, 47, 0)
        if 0 <= z < 8:
            s_r = jnp.where(row == 39, EX[0, 0, z : z + 1], s_r)
        s_c = jnp.where(lane < 127, pltpu.roll(s, 127, 1), 0.0)
        h_ru = s + s_r
        h_rl = pltpu.roll(h_ru, 1, 0)
        if 0 <= z < 8:
            h_rl = jnp.where(row == 40, s + EX[1, 0, z : z + 1], h_rl)
        f_cu = s + s_c
        f_cl = s + jnp.where(lane > 0, pltpu.roll(s, 1, 1), 0.0)
        HR[0, z + 6] = h_rl
        HR[1, z + 6] = h_ru
        HC[0, z + 6] = jnp.where(lane > 0, f_cl, 0.0)
        HC[1, z + 6] = jnp.where(lane < 127, f_cu, 0.0)
        f = [HZ[z + 6] + HZ[z + 7], h_rl + h_ru, f_cl + f_cu]
        total = f[0] + f[1] + f[2]
        if 0 <= z < 2:
            total = total + spring0(z)
        g0 = SG[0, z + 6] - SG[0, z + 8]
        x = SG[1, z + 7]
        x_l, x_u = pltpu.roll(x, 1, 0), pltpu.roll(x, 47, 0)
        if 0 <= z < 8:
            x_l = jnp.where(row == 40, EX[1, 1, z : z + 1], x_l)
            x_u = jnp.where(row == 39, EX[0, 1, z : z + 1], x_u)
        g1 = x_l - x_u
        x = SG[2, z + 7]
        g2 = jnp.where(lane > 0, pltpu.roll(x, 1, 1), 0.0) - jnp.where(
            lane < 127, pltpu.roll(x, 127, 1), 0.0
        )
        for c, g in enumerate((g0, g1, g2)):
            d = total + f[c]
            w = jnp.where(s > 0.0, OMEGA / jnp.where(s > 0.0, d, 1.0), 0.0)
            BB[c, z + 6] = g
            WH[c, z + 6] = w
            if -4 <= z < 12:
                DD[c, z + 4] = d
            V0[c, z + 6] = w * g

    for z in range(-2, 10):
        first_sweep(z)

    def apply0(v, off, c, z):
        x = v[c, z + off]
        a = HZ[z + 6] * v[c, z + off - 1] + HZ[z + 7] * v[c, z + off + 1]
        b = HR[0, z + 6] * pltpu.roll(x, 1, 0) + HR[1, z + 6] * pltpu.roll(x, 47, 0)
        e = HC[0, z + 6] * pltpu.roll(x, 1, 1) + HC[1, z + 6] * pltpu.roll(x, 127, 1)
        return x, (a + b + e) + (a, b, e)[c]

    def second_sweep(zs):
        for z in zs:
            for c in range(3):
                x, n = apply0(V0, 6, c, z)
                V1[c, z + 5] = KEEP * x + WH[c, z + 6] * (BB[c, z + 6] + n)

    def pairs(ref, c, z, n):
        return ref[c, z, pl.ds(0, n, 2)] + ref[c, z, pl.ds(1, n, 2)]

    def restrict(zs):
        for z in zs:
            for c in range(3):
                total = None
                for k in range(2):
                    x, n = apply0(V1, 5, c, 2 * z + k)
                    r = BB[c, 2 * z + k + 6] + n - DD[c, 2 * z + k + 4] * x
                    total = r if total is None else total + r
                RS[c, z + 2] = total
            BB1[0, z + 3] = dot(pairs(RS, 0, z + 2, 24), take_lo) + dot(pairs(RS, 1, z + 2, 24), take_hi)
            BB1[1, z + 3] = dot(pairs(RS, 2, z + 2, 24), take_lo)

    second_sweep(range(-1, 9))
    restrict(range(0, 4))

    def b1_refs(dt, dh):
        return BB1.at[:, 4 if dh > 0 else 5], b1_vert.at[0 if dh > 0 else 1]

    b1_moves = near_copies(b1_send, b1_recv, b1_refs, UPDOWN)
    start(b1_moves)

    wait_recv(deep_moves)
    build((*range(-7, -3), *range(11, 15)))
    between((*range(-7, -3), *range(10, 14)))
    for z in (*range(-6, -2), *range(10, 14)):
        first_sweep(z)
    second_sweep((*range(-5, -1), *range(9, 13)))
    restrict((-2, -1, 4, 5))

    pl.semaphore_wait(met, near_ok(0, -1).astype(jnp.int32) + near_ok(0, 1).astype(jnp.int32))
    start_far(q2_moves, True)

    lane1 = iota((24, 128), 1)
    col1 = lane1 % 64
    wait_recv(q1_moves)

    def both(x):
        return jnp.where(iota(x.shape, len(x.shape) - 1) < 64, x, 0.0)

    for z in range(-4, 8):
        if z < 0:
            centre = jnp.where(below, q1_vert[0, z + 4], 0.0)
            lo = jnp.where(jnp.logical_and(below, before), q1_side[1, 2, z + 4], 0.0)
            hi = jnp.where(jnp.logical_and(below, after), q1_side[0, 2, z + 4], 0.0)
        elif z < 4:
            centre = q1[z]
            lo = jnp.where(before, q1_side[1, 1, z], 0.0)
            hi = jnp.where(after, q1_side[0, 1, z], 0.0)
        else:
            centre = jnp.where(above, q1_vert[1, z - 4], 0.0)
            lo = jnp.where(jnp.logical_and(above, before), q1_side[1, 0, z - 4], 0.0)
            hi = jnp.where(jnp.logical_and(above, after), q1_side[0, 0, z - 4], 0.0)
        q = jnp.concatenate([centre, hi, lo], axis=0)
        other = pltpu.roll(q, 64, 1)
        S1[z + 4] = jnp.where(lane1 < 64, q, other)
        if z == 0:
            spring1 = jnp.where(lane1 < 64, other, q)
    for z in range(-4, 7):
        HZ1[z + 4] = S1[z + 4] + S1[z + 5]
    for z in range(-3, 7):
        s = S1[z + 4]
        h_ru = s + pltpu.roll(s, 23, 0)
        h_rl = pltpu.roll(h_ru, 1, 0)
        f_cu = s + jnp.where(col1 < 63, pltpu.roll(s, 127, 1), 0.0)
        f_cl = s + jnp.where(col1 > 0, pltpu.roll(s, 1, 1), 0.0)
        HR1[0, z + 3] = h_rl
        HR1[1, z + 3] = h_ru
        HC1[0, z + 3] = jnp.where(col1 > 0, f_cl, 0.0)
        HC1[1, z + 3] = jnp.where(col1 < 63, f_cu, 0.0)
        f = [HZ1[z + 3] + HZ1[z + 4], h_rl + h_ru, f_cl + f_cu]
        total = f[0] + f[1] + f[2]
        if z == 0:
            total = total + spring1
        for t in range(2):
            d = total + (jnp.where(lane1 < 64, f[0], f[1]) if t == 0 else f[2])
            WH1[t, z + 3] = jnp.where(s > 0.0, OMEGA / jnp.where(s > 0.0, d, 1.0), 0.0)
            if 0 <= z < 4:
                DD1[t, z] = d

    for z in range(-2, 6):
        for t in range(2):
            if z < 0:
                BB1[t, z + 3] = jnp.where(below, BB1[t, z + 3], 0.0)
            if z > 3:
                BB1[t, z + 3] = jnp.where(above, BB1[t, z + 3], 0.0)
            VA1[t, z + 3] = WH1[t, z + 3] * BB1[t, z + 3]

    def apply1(v, off, t, z):
        x = v[t, z + off]
        a = HZ1[z + 3] * v[t, z + off - 1] + HZ1[z + 4] * v[t, z + off + 1]
        b = HR1[0, z + 3] * pltpu.roll(x, 1, 0) + HR1[1, z + 3] * pltpu.roll(x, 23, 0)
        e = HC1[0, z + 3] * pltpu.roll(x, 1, 1) + HC1[1, z + 3] * pltpu.roll(x, 127, 1)
        return x, (a + b + e) + (jnp.where(lane1 < 64, a, b) if t == 0 else e)

    def second_sweep1(zs):
        for z in zs:
            for t in range(2):
                x, n = apply1(VA1, 3, t, z)
                VB1[t, z + 2] = KEEP * x + WH1[t, z + 3] * (BB1[t, z + 3] + n)

    second_sweep1(range(-1, 5))
    down_a = one_hot((128, 128), lambda l, j: l // 2 == j)
    down_b = one_hot((128, 128), lambda l, j: jnp.logical_and(l < 64, l // 2 == j - 64))
    for z in range(2):
        for t in range(2):
            total = None
            for k in range(2):
                x, n = apply1(VB1, 2, t, 2 * z + k)
                r = BB1[t, 2 * z + k + 3] + n - DD1[t, 2 * z + k] * x
                total = r[0:16] if total is None else total + r[0:16]
            RS1[t, z] = total
        b2_own[z] = dot(pairs(RS1, 0, z, 8), down_a) + dot(pairs(RS1, 1, z, 8), down_b)
    b2_moves = far_copies(b2_send, b2_recv, b2_own, b2)
    start(b2_moves)
    b2[pl.ds(2 * h, 2), 16:24] = b2_own[...]

    wait_recv(b1_moves)
    for t in range(2):
        VA1[t, 0] = WH1[t, 0] * jnp.where(below, b1_vert[0, t], 0.0)
        VA1[t, 9] = WH1[t, 9] * jnp.where(above, b1_vert[1, t], 0.0)
    second_sweep1((-2, 5))

    lane2 = iota((40, 128), 1)
    row2 = iota((40, 128), 0)
    col2 = lane2 % 32
    real = lane2 < 96
    slot = row2 // 8 + (i - 2)
    inside = jnp.logical_and(slot >= 0, slot < tiles)
    keep = jnp.logical_and(inside, real)
    wait_recv(q2_moves)

    def pick(a, b, e):
        return jnp.where(lane2 < 32, a, jnp.where(lane2 < 64, b, e))

    q = jnp.where(inside, q2[0], 0.0)
    spring2 = pick(pltpu.roll(q, 32, 1), pltpu.roll(q, 64, 1), pltpu.roll(q, 96, 1))
    odd_row, odd_col = row2 % 2 == 1, lane2 % 2 == 1

    def pair_sum(x):
        x = x + jnp.where(odd_row, pltpu.roll(x, 1, 0), pltpu.roll(x, 39, 0))
        return x + jnp.where(odd_col, pltpu.roll(x, 1, 1), pltpu.roll(x, 127, 1))

    def faces(s_of, depth, step, spring, hz, hr, hc, wh, dd):
        for z in range(depth - 1):
            hz[z] = s_of(z) + s_of(z + 1)
        for z in range(depth):
            s = s_of(z)
            h_ru = s + pltpu.roll(s, 40 - step, 0)
            h_rl = pltpu.roll(h_ru, step, 0)
            first, last = col2 < step, col2 >= 32 - step
            f_cu = s + jnp.where(last, 0.0, pltpu.roll(s, 128 - step, 1))
            f_cl = s + jnp.where(first, 0.0, pltpu.roll(s, step, 1))
            hr[0, z] = h_rl
            hr[1, z] = h_ru
            hc[0, z] = jnp.where(first, 0.0, f_cl)
            hc[1, z] = jnp.where(last, 0.0, f_cu)
            f_z = (hz[z - 1] if z > 0 else s) + (hz[z] if z < depth - 1 else s)
            f_r, f_c = h_rl + h_ru, f_cl + f_cu
            d = (f_z + f_r + f_c) + pick(f_z, f_r, f_c)
            if z == 0:
                d = d + spring
            wh[z] = jnp.where(s > 0.0, OMEGA / jnp.where(s > 0.0, d, 1.0), 0.0)
            if dd is not None:
                dd[z] = d

    def s2(z):
        return jnp.where(keep, q2[z], 0.0)

    faces(s2, 8, 1, spring2, HZ2, HR2, HC2, WH2, DD2)
    for z in range(4):
        S3[z] = 0.5 * pair_sum(s2(2 * z) + s2(2 * z + 1))
    faces(lambda z: S3[z], 4, 2, pair_sum(spring2), HZ3, HR3, HC3, WH3, None)

    def apply2(v, z, depth, step, hz, hr, hc):
        x = v[z]
        a = None
        if z > 0:
            a = hz[z - 1] * v[z - 1]
        if z < depth - 1:
            up = hz[z] * v[z + 1]
            a = up if a is None else a + up
        b = hr[0, z] * pltpu.roll(x, step, 0) + hr[1, z] * pltpu.roll(x, 40 - step, 0)
        e = hc[0, z] * pltpu.roll(x, step, 1) + hc[1, z] * pltpu.roll(x, 128 - step, 1)
        return x, (a + b + e) + pick(a, b, e)

    wait_recv(b2_moves)
    for z in range(8):
        b = jnp.where(keep, b2[z], 0.0)
        b2[z] = b
        VA2[z] = WH2[z] * b
    for z in range(8):
        x, n = apply2(VA2, z, 8, 1, HZ2, HR2, HC2)
        VB2[z] = KEEP * x + WH2[z] * (b2[z] + n)
    for z in range(4):
        total = None
        for k in range(2):
            x, n = apply2(VB2, 2 * z + k, 8, 1, HZ2, HR2, HC2)
            r = b2[2 * z + k] + n - DD2[2 * z + k] * x
            total = r if total is None else total + r
        total = pair_sum(total)
        BB3[z] = total
        V3[0, z] = WH3[z] * total
    for turn in range(5):
        now, later = turn % 2, (turn + 1) % 2
        for z in range(4):
            x, n = apply2(V3.at[now], z, 4, 2, HZ3, HR3, HC3)
            V3[later, z] = KEEP * x + WH3[z] * (BB3[z] + n)
    for z in range(8):
        VB2[z] = VB2[z] + V3[1, z // 2]
    PO2[0] = jnp.zeros((24, 128), F32)
    PO2[9] = jnp.zeros((24, 128), F32)
    for z in range(8):
        x, n = apply2(VB2, z, 8, 1, HZ2, HR2, HC2)
        PO2[z + 1] = (KEEP * x + WH2[z] * (b2[z] + n))[8:32]

    up_a = one_hot((128, 128), lambda l, j: l == j // 2)
    up_b = one_hot((128, 128), lambda l, j: jnp.logical_and(j < 64, l == 64 + j // 2))
    for k in range(4):
        coarse = PO2[2 * h + k]
        for t, m in enumerate((up_a, up_b)):
            e = dot(coarse, m)
            T1[t, k, pl.ds(0, 24, 2)] = e
            T1[t, k, pl.ds(1, 24, 2)] = e
            tail = jnp.where(sub8 < 4, T1[t, k, 32:40], T1[t, k, 8:16])
            e = jnp.concatenate([T1[t, k, 16:32], tail], axis=0)
            for z in (2 * k, 2 * k + 1):
                VB1[t, z] = VB1[t, z] + e
    for z in range(-1, 5):
        for t in range(2):
            x, n = apply1(VB1, 2, t, z)
            PO1[t, z + 1] = KEEP * x + WH1[t, z + 3] * (BB1[t, z + 3] + n)

    up_lo = one_hot((128, 128), lambda l, j: l == j // 2)
    up_hi = one_hot((128, 128), lambda l, j: l == 64 + j // 2)
    for k in range(6):
        for c in range(3):
            e = dot(PO1[c // 2, k], up_hi if c == 1 else up_lo)
            T0[c, k, pl.ds(0, 24, 2)] = e
            T0[c, k, pl.ds(1, 24, 2)] = e
            for z in (2 * k - 2, 2 * k - 1):
                if -1 <= z < 9:
                    V1[c, z + 5] = V1[c, z + 5] + T0[c, k]
    for z in range(8):
        for c in range(3):
            x, n = apply0(V1, 5, c, z)
            out[c, z] = (KEEP * x + WH[c, z + 6] * (BB[c, z + 6] + n))[0:32]

    for moves in (label_moves, deep_moves, q1_moves, q2_moves, b1_moves, b2_moves):
        wait_send(moves)


def solution(mesh):
    heights, tiles = mesh.shape["height"], mesh.shape["tile"]

    def vmem(*shape, dtype=F32):
        return pltpu.VMEM(shape, dtype)

    i32 = jnp.int32
    scratch = [
        pltpu.SMEM((3,), F32), pltpu.SMEM((3, 3), F32),
        vmem(8, 32, 128, dtype=i32), vmem(2, 32, 128, dtype=i32),
        vmem(7, 32, 128, dtype=i32), vmem(7, 32, 128, dtype=i32),
        vmem(2, 11, 8, 128, dtype=i32), vmem(2, 2, 7, 8, 128, dtype=i32), vmem(2, 11, 8, 128, dtype=i32),
        vmem(4, 16, 128), vmem(2, 4, 16, 128), vmem(2, 3, 4, 4, 128), vmem(2, 4, 4, 128),
        vmem(8, 40, 128), vmem(2, 8, 128),
        vmem(2, 2, 24, 128),
        vmem(8, 40, 128), vmem(2, 8, 128),
        vmem(22, 48, 128), vmem(3, 22, 48, 128), vmem(21, 48, 128), vmem(2, 20, 48, 128), vmem(2, 20, 48, 128),
        vmem(3, 20, 48, 128), vmem(3, 20, 48, 128), vmem(3, 16, 48, 128), vmem(3, 20, 48, 128),
        vmem(3, 18, 48, 128), vmem(3, 8, 48, 128), vmem(2, 2, 8, 128),
        vmem(12, 24, 128), vmem(11, 24, 128), vmem(2, 10, 24, 128), vmem(2, 10, 24, 128), vmem(2, 10, 24, 128),
        vmem(2, 10, 24, 128), vmem(2, 4, 24, 128), vmem(2, 10, 24, 128), vmem(2, 8, 24, 128),
        vmem(2, 2, 16, 128), vmem(2, 6, 24, 128),
        vmem(7, 40, 128), vmem(2, 8, 40, 128), vmem(2, 8, 40, 128), vmem(8, 40, 128), vmem(8, 40, 128),
        vmem(8, 40, 128), vmem(8, 40, 128), vmem(10, 24, 128), vmem(2, 4, 48, 128),
        vmem(4, 40, 128), vmem(3, 40, 128), vmem(2, 4, 40, 128), vmem(2, 4, 40, 128), vmem(4, 40, 128),
        vmem(4, 40, 128), vmem(2, 4, 40, 128),
        vmem(3, 6, 48, 128), vmem(2, 4, 32, 128),
        pltpu.SemaphoreType.DMA((4,)),
        pltpu.SemaphoreType.REGULAR,
    ]
    for count in (8, 6, 8, 19, 2, 19):
        scratch += [pltpu.SemaphoreType.DMA((count,)), pltpu.SemaphoreType.DMA((count,))]

    def local(material, clamped, stiffness_table, eigenstrain):
        return pl.pallas_call(
            functools.partial(kernel, heights, tiles),
            out_shape=jax.ShapeDtypeStruct((3, 8, 32, 128), F32),
            in_specs=[
                pl.BlockSpec(memory_space=pltpu.HBM),
                pl.BlockSpec(memory_space=pltpu.HBM),
                pl.BlockSpec(memory_space=pltpu.HBM),
                pl.BlockSpec(memory_space=pltpu.HBM),
            ],
            out_specs=pl.BlockSpec(memory_space=pltpu.VMEM),
            scratch_shapes=scratch,
            compiler_params=pltpu.CompilerParams(
                collective_id=0, has_side_effects=True, vmem_limit_bytes=40 * 1024 * 1024
            ),
        )(*(pltpu.with_memory_space_constraint(x, pltpu.HBM) for x in (material, clamped, stiffness_table, eigenstrain)))

    in_specs = (P("height", "tile", None), P("height", "tile", None), P(), P())
    out_specs = P(None, "height", "tile", None)
    return jax.shard_map(local, mesh=mesh, in_specs=in_specs, out_specs=out_specs, check_vma=False)
```

```python
import functools

import jax
import jax.numpy as jnp
from jax import lax
from jax.experimental import pallas as pl
from jax.experimental.pallas import tpu as pltpu
from jax.sharding import PartitionSpec as P

PENALTY = 50.0
OMEGA = 0.6
KEEP = 1.0 - OMEGA
F32 = jnp.float32
BF16 = jnp.bfloat16
NEAR = ((-1, -1), (-1, 1), (1, -1), (1, 1), (-1, 0), (1, 0), (0, -1), (0, 1))
UPDOWN = ((0, -1), (0, 1))
DEEP = tuple(move for move in NEAR if move[1] != 0)
FAR = tuple(
    sorted(
        ((dt, k) for dt in (-2, -1, 0, 1, 2) for k in (0, 1, 2, 3) if (dt, k) != (0, 0)),
        key=lambda move: (-abs(move[0]), -min(move[1], 4 - move[1]), move),
    )
)


def iota(shape, axis):
    return lax.broadcasted_iota(jnp.int32, shape, axis)


def one_hot(shape, cond):
    return jnp.where(cond(iota(shape, 0), iota(shape, 1)), 1.0, 0.0).astype(BF16)


def dot(a, b):
    hi = a.astype(BF16)
    rest = a - hi.astype(F32)
    mid = rest.astype(BF16)
    lo = (rest - mid.astype(F32)).astype(BF16)
    parts = (jnp.dot(x, b, preferred_element_type=F32) for x in (lo, mid, hi))
    return sum(parts)


def kernel(
    heights,
    tiles,
    mat_hbm,
    clamp_hbm,
    table_hbm,
    eigen_hbm,
    out,
    table,
    eigen,
    mat,
    cl,
    m_lo, m_hi, m_side, m_corner, m_stage,
    q1, q1_vert, q1_side, q1_stage,
    q2, q2_own,
    b1_vert,
    b2, b2_own,
    S, SG, HZ, HR, HC, BB, WH, DD, V0, V1, RS, EX,
    S1, HZ1, HR1, HC1, BB1, WH1, DD1, VA1, VB1, RS1, PO1,
    HZ2, HR2, HC2, WH2, DD2, VA2, VB2, PO2, T1,
    S3, HZ3, HR3, HC3, WH3, BB3, V3,
    T0, R4,
    local_sem,
    m_send, m_recv, d_send, d_recv, q1_send, q1_recv, q2_send, q2_recv, b1_send, b1_recv, b2_send, b2_recv,
):
    i = lax.axis_index("tile")
    h = lax.axis_index("height")

    in_mat = pltpu.make_async_copy(mat_hbm, mat, local_sem.at[0])
    in_cl = pltpu.make_async_copy(clamp_hbm.at[pl.ds(0, 2)], cl, local_sem.at[1])
    in_table = pltpu.make_async_copy(table_hbm, table, local_sem.at[2])
    in_eigen = pltpu.make_async_copy(eigen_hbm, eigen, local_sem.at[3])

    def tile_ok(dt):
        return jnp.logical_and(i + dt >= 0, i + dt < tiles)

    def near_ok(dt, dh):
        return jnp.logical_and(tile_ok(dt), jnp.logical_and(h + dh >= 0, h + dh < heights))

    def far_id(dt, k):
        return {"tile": i + dt, "height": lax.rem(h + k, heights)}

    in_mat.start()
    barrier = pltpu.get_barrier_semaphore()
    ring = [(dt, k) for dt in (-1, 1, 0) for k in (1, 3, 0) if (dt, k) != (0, 0)]
    for dt, k in ring:
        @pl.when(tile_ok(dt))
        def _():
            pl.semaphore_signal(
                barrier, inc=1, device_id=far_id(dt, k), device_id_type=pl.DeviceIdType.MESH
            )
    reach = 3 * (tile_ok(-1).astype(jnp.int32) + tile_ok(1).astype(jnp.int32)) + 2

    in_cl.start()
    in_table.start()
    in_eigen.start()
    in_mat.wait()
    in_cl.wait()
    for side, first, edge in ((0, 0, 8), (1, 24, 23)):
        for z in range(8):
            m_stage[side, z] = mat[z, first : first + 8]
        for z in range(2):
            m_stage[side, 8 + z] = cl[z, first : first + 8]
        m_stage[side, 10] = mat[:, edge]

    pl.semaphore_wait(barrier, reach)

    def near_copies(send, recv, refs, moves=NEAR):
        copies = []
        for k, (dt, dh) in enumerate(moves):
            src, dst = refs(dt, dh)
            copy = pltpu.make_async_remote_copy(
                src_ref=src, dst_ref=dst, send_sem=send.at[k], recv_sem=recv.at[k],
                device_id={"tile": i + dt, "height": h + dh},
                device_id_type=pl.DeviceIdType.MESH,
            )
            copies.append((copy, near_ok(dt, dh), near_ok(-dt, -dh)))
        return copies

    def far_copies(send, recv, own, field):
        copies = []
        for k, (dt, dh) in enumerate(FAR):
            copy = pltpu.make_async_remote_copy(
                src_ref=own,
                dst_ref=field.at[pl.ds(2 * h, 2), pl.ds(8 * (2 - dt), 8)],
                send_sem=send.at[k], recv_sem=recv.at[k],
                device_id=far_id(dt, dh), device_id_type=pl.DeviceIdType.MESH,
            )
            copies.append((copy, tile_ok(dt), tile_ok(-dt)))
        return copies

    def start(copies):
        for copy, sends, _ in copies:
            @pl.when(sends)
            def _():
                copy.start()

    def wait_recv(copies):
        for copy, _, receives in copies:
            @pl.when(receives)
            def _():
                copy.wait_recv()

    def wait_send(copies):
        for copy, sends, _ in copies:
            @pl.when(sends)
            def _():
                copy.wait_send()

    def label_refs(dt, dh):
        if dt == 0:
            if dh > 0:
                return mat.at[pl.ds(5, 3)], m_lo.at[pl.ds(4, 3)]
            return mat.at[pl.ds(0, 3)], m_hi.at[pl.ds(0, 3)]
        side = 0 if dt < 0 else 1
        if dh == 0:
            return m_stage.at[side], m_side.at[side]
        if dh > 0:
            return m_stage.at[side, pl.ds(5, 3)], m_corner.at[side, 1, pl.ds(4, 3)]
        return m_stage.at[side, pl.ds(0, 3)], m_corner.at[side, 0, pl.ds(0, 3)]

    def deep_refs(dt, dh):
        if dt == 0:
            if dh > 0:
                return mat.at[pl.ds(1, 4)], m_lo.at[pl.ds(0, 4)]
            return mat.at[pl.ds(3, 4)], m_hi.at[pl.ds(3, 4)]
        side = 0 if dt < 0 else 1
        if dh > 0:
            return m_stage.at[side, pl.ds(1, 4)], m_corner.at[side, 1, pl.ds(0, 4)]
        return m_stage.at[side, pl.ds(3, 4)], m_corner.at[side, 0, pl.ds(3, 4)]

    label_moves = near_copies(m_send, m_recv, label_refs)
    start(label_moves)
    deep_moves = near_copies(d_send, d_recv, deep_refs, DEEP)
    start(deep_moves)
    in_table.wait()
    in_eigen.wait()

    st = [table[n] for n in range(3)]
    stress = [[table[n] * eigen[n, c] for c in range(3)] for n in range(3)]

    def look(m, values):
        return jnp.where(
            m == 0, values[0], jnp.where(m == 1, values[1], jnp.where(m == 2, values[2], 0.0))
        )

    take_lo = one_hot((128, 128), lambda l, j: jnp.logical_and(j < 64, l // 2 == j))
    take_hi = one_hot((128, 128), lambda l, j: l // 2 == j - 64)
    lowest = jnp.where(h == 0, 1.0, 0.0).astype(F32)

    for z in range(4):
        R4[0, z] = look(mat[2 * z], st) + look(mat[2 * z + 1], st)
    R4[1, 0] = (cl[0] + cl[1]).astype(F32)
    s_rows = jnp.concatenate(
        [R4[0, z, pl.ds(0, 16, 2)] + R4[0, z, pl.ds(1, 16, 2)] for z in range(4)], axis=0
    )
    p_rows = R4[1, 0, pl.ds(0, 16, 2)] + R4[1, 0, pl.ds(1, 16, 2)]
    s_one = dot(0.5 * s_rows, take_lo).reshape(4, 16, 128)
    p_one = dot((2.0 * PENALTY * lowest) * p_rows, take_hi)
    q1[0] = s_one[0] + p_one
    for z in range(1, 4):
        q1[z] = s_one[z]
    for z in range(4):
        q1_stage[0, z] = q1[z, 0:4]
        q1_stage[1, z] = q1[z, 12:16]

    def q1_refs(dt, dh):
        if dt == 0:
            return q1, q1_vert.at[0 if dh > 0 else 1]
        side = 0 if dt < 0 else 1
        return q1_stage.at[side], q1_side.at[side, dh + 1]

    q1_moves = near_copies(q1_send, q1_recv, q1_refs)
    start(q1_moves)

    for z in range(2):
        R4[1, z, 0:16] = q1[2 * z] + q1[2 * z + 1]
    q_rows = jnp.concatenate(
        [R4[1, z, pl.ds(0, 8, 2)] + R4[1, z, pl.ds(1, 8, 2)] for z in range(2)], axis=0
    )
    l, j = iota((128, 128), 0), iota((128, 128), 1)
    down_q = jnp.where(
        jnp.logical_and(j < 96, jnp.logical_and(l < 64, l // 2 == j % 32)), 0.5,
        jnp.where(jnp.logical_and(j >= 96, l // 2 == j - 64), 1.0, 0.0),
    ).astype(BF16)
    q2_own[...] = dot(q_rows, down_q).reshape(2, 8, 128)
    q2_moves = far_copies(q2_send, q2_recv, q2_own, q2)
    q2[pl.ds(2 * h, 2), 16:24] = q2_own[...]

    lane = iota((48, 128), 1)
    row = iota((48, 128), 0)
    sub8 = iota((8, 128), 0)
    wait_recv(label_moves)
    start(q2_moves)
    below, above = h > 0, h < heights - 1
    before, after = i > 0, i < tiles - 1

    def labels(z):
        if 0 <= z < 8:
            centre, hi, lo = mat[z], m_side[0, z], m_side[1, z]
            centre_ok, hi_ok, lo_ok = None, after, before
        else:
            centre_ok = below if z < 0 else above
            end = 1 if z < 0 else 0
            k = z + 7 if z < 0 else z - 8
            centre = jnp.where(centre_ok, (m_lo if z < 0 else m_hi)[k], -1)
            hi, lo = m_corner[0, end, k], m_corner[1, end, k]
            hi_ok, lo_ok = jnp.logical_and(centre_ok, after), jnp.logical_and(centre_ok, before)
        return jnp.concatenate([centre, jnp.where(hi_ok, hi, -1), jnp.where(lo_ok, lo, -1)], axis=0)

    def build(zs):
        for z in zs:
            m = labels(z)
            S[z + 7] = look(m, st)
            for c in range(3):
                SG[c, z + 7] = look(m, [stress[n][c] for n in range(3)])

    build(range(-3, 11))
    for side, ok in ((0, after), (1, before)):
        m = jnp.where(ok, m_side[side, 10], -1)
        EX[side, 0] = look(m, st)
        EX[side, 1] = look(m, [stress[n][1] for n in range(3)])
    def between(zs):
        for z in zs:
            HZ[z + 7] = S[z + 7] + S[z + 8]

    between(range(-3, 10))

    def spring0(z):
        sides = jnp.concatenate(
            [jnp.where(after, m_side[0, 8 + z], 0), jnp.where(before, m_side[1, 8 + z], 0)],
            axis=0,
        )
        return (2.0 * PENALTY * lowest) * jnp.concatenate([cl[z], sides], axis=0).astype(F32)

    def first_sweep(z):
        s = S[z + 7]
        s_r = pltpu.roll(s, 47, 0)
        if 0 <= z < 8:
            s_r = jnp.where(row == 39, EX[0, 0, z : z + 1], s_r)
        s_c = jnp.where(lane < 127, pltpu.roll(s, 127, 1), 0.0)
        h_ru = s + s_r
        h_rl = pltpu.roll(h_ru, 1, 0)
        if 0 <= z < 8:
            h_rl = jnp.where(row == 40, s + EX[1, 0, z : z + 1], h_rl)
        f_cu = s + s_c
        f_cl = s + jnp.where(lane > 0, pltpu.roll(s, 1, 1), 0.0)
        HR[0, z + 6] = h_rl
        HR[1, z + 6] = h_ru
        HC[0, z + 6] = jnp.where(lane > 0, f_cl, 0.0)
        HC[1, z + 6] = jnp.where(lane < 127, f_cu, 0.0)
        f = [HZ[z + 6] + HZ[z + 7], h_rl + h_ru, f_cl + f_cu]
        total = f[0] + f[1] + f[2]
        if 0 <= z < 2:
            total = total + spring0(z)
        g0 = SG[0, z + 6] - SG[0, z + 8]
        x = SG[1, z + 7]
        x_l, x_u = pltpu.roll(x, 1, 0), pltpu.roll(x, 47, 0)
        if 0 <= z < 8:
            x_l = jnp.where(row == 40, EX[1, 1, z : z + 1], x_l)
            x_u = jnp.where(row == 39, EX[0, 1, z : z + 1], x_u)
        g1 = x_l - x_u
        x = SG[2, z + 7]
        g2 = jnp.where(lane > 0, pltpu.roll(x, 1, 1), 0.0) - jnp.where(
            lane < 127, pltpu.roll(x, 127, 1), 0.0
        )
        for c, g in enumerate((g0, g1, g2)):
            d = total + f[c]
            w = jnp.where(s > 0.0, OMEGA / jnp.where(s > 0.0, d, 1.0), 0.0)
            BB[c, z + 6] = g
            WH[c, z + 6] = w
            if -4 <= z < 12:
                DD[c, z + 4] = d
            V0[c, z + 6] = w * g

    for z in range(-2, 10):
        first_sweep(z)

    def apply0(v, off, c, z):
        x = v[c, z + off]
        a = HZ[z + 6] * v[c, z + off - 1] + HZ[z + 7] * v[c, z + off + 1]
        b = HR[0, z + 6] * pltpu.roll(x, 1, 0) + HR[1, z + 6] * pltpu.roll(x, 47, 0)
        e = HC[0, z + 6] * pltpu.roll(x, 1, 1) + HC[1, z + 6] * pltpu.roll(x, 127, 1)
        return x, (a + b + e) + (a, b, e)[c]

    def second_sweep(zs):
        for z in zs:
            for c in range(3):
                x, n = apply0(V0, 6, c, z)
                V1[c, z + 5] = KEEP * x + WH[c, z + 6] * (BB[c, z + 6] + n)

    def pairs(ref, c, z, n):
        return ref[c, z, pl.ds(0, n, 2)] + ref[c, z, pl.ds(1, n, 2)]

    def restrict(zs):
        for z in zs:
            for c in range(3):
                total = None
                for k in range(2):
                    x, n = apply0(V1, 5, c, 2 * z + k)
                    r = BB[c, 2 * z + k + 6] + n - DD[c, 2 * z + k + 4] * x
                    total = r if total is None else total + r
                RS[c, z + 2] = total
            BB1[0, z + 3] = dot(pairs(RS, 0, z + 2, 24), take_lo) + dot(pairs(RS, 1, z + 2, 24), take_hi)
            BB1[1, z + 3] = dot(pairs(RS, 2, z + 2, 24), take_lo)

    second_sweep(range(-1, 9))
    restrict(range(0, 4))

    def b1_refs(dt, dh):
        return BB1.at[:, 4 if dh > 0 else 5], b1_vert.at[0 if dh > 0 else 1]

    b1_moves = near_copies(b1_send, b1_recv, b1_refs, UPDOWN)
    start(b1_moves)

    wait_recv(deep_moves)
    build((*range(-7, -3), *range(11, 15)))
    between((*range(-7, -3), *range(10, 14)))
    for z in (*range(-6, -2), *range(10, 14)):
        first_sweep(z)
    second_sweep((*range(-5, -1), *range(9, 13)))
    restrict((-2, -1, 4, 5))

    lane1 = iota((24, 128), 1)
    col1 = lane1 % 64
    wait_recv(q1_moves)

    def both(x):
        return jnp.where(iota(x.shape, len(x.shape) - 1) < 64, x, 0.0)

    for z in range(-4, 8):
        if z < 0:
            centre = jnp.where(below, q1_vert[0, z + 4], 0.0)
            lo = jnp.where(jnp.logical_and(below, before), q1_side[1, 2, z + 4], 0.0)
            hi = jnp.where(jnp.logical_and(below, after), q1_side[0, 2, z + 4], 0.0)
        elif z < 4:
            centre = q1[z]
            lo = jnp.where(before, q1_side[1, 1, z], 0.0)
            hi = jnp.where(after, q1_side[0, 1, z], 0.0)
        else:
            centre = jnp.where(above, q1_vert[1, z - 4], 0.0)
            lo = jnp.where(jnp.logical_and(above, before), q1_side[1, 0, z - 4], 0.0)
            hi = jnp.where(jnp.logical_and(above, after), q1_side[0, 0, z - 4], 0.0)
        q = jnp.concatenate([centre, hi, lo], axis=0)
        other = pltpu.roll(q, 64, 1)
        S1[z + 4] = jnp.where(lane1 < 64, q, other)
        if z == 0:
            spring1 = jnp.where(lane1 < 64, other, q)
    for z in range(-4, 7):
        HZ1[z + 4] = S1[z + 4] + S1[z + 5]
    for z in range(-3, 7):
        s = S1[z + 4]
        h_ru = s + pltpu.roll(s, 23, 0)
        h_rl = pltpu.roll(h_ru, 1, 0)
        f_cu = s + jnp.where(col1 < 63, pltpu.roll(s, 127, 1), 0.0)
        f_cl = s + jnp.where(col1 > 0, pltpu.roll(s, 1, 1), 0.0)
        HR1[0, z + 3] = h_rl
        HR1[1, z + 3] = h_ru
        HC1[0, z + 3] = jnp.where(col1 > 0, f_cl, 0.0)
        HC1[1, z + 3] = jnp.where(col1 < 63, f_cu, 0.0)
        f = [HZ1[z + 3] + HZ1[z + 4], h_rl + h_ru, f_cl + f_cu]
        total = f[0] + f[1] + f[2]
        if z == 0:
            total = total + spring1
        for t in range(2):
            d = total + (jnp.where(lane1 < 64, f[0], f[1]) if t == 0 else f[2])
            WH1[t, z + 3] = jnp.where(s > 0.0, OMEGA / jnp.where(s > 0.0, d, 1.0), 0.0)
            if 0 <= z < 4:
                DD1[t, z] = d

    for z in range(-2, 6):
        for t in range(2):
            if z < 0:
                BB1[t, z + 3] = jnp.where(below, BB1[t, z + 3], 0.0)
            if z > 3:
                BB1[t, z + 3] = jnp.where(above, BB1[t, z + 3], 0.0)
            VA1[t, z + 3] = WH1[t, z + 3] * BB1[t, z + 3]

    def apply1(v, off, t, z):
        x = v[t, z + off]
        a = HZ1[z + 3] * v[t, z + off - 1] + HZ1[z + 4] * v[t, z + off + 1]
        b = HR1[0, z + 3] * pltpu.roll(x, 1, 0) + HR1[1, z + 3] * pltpu.roll(x, 23, 0)
        e = HC1[0, z + 3] * pltpu.roll(x, 1, 1) + HC1[1, z + 3] * pltpu.roll(x, 127, 1)
        return x, (a + b + e) + (jnp.where(lane1 < 64, a, b) if t == 0 else e)

    def second_sweep1(zs):
        for z in zs:
            for t in range(2):
                x, n = apply1(VA1, 3, t, z)
                VB1[t, z + 2] = KEEP * x + WH1[t, z + 3] * (BB1[t, z + 3] + n)

    second_sweep1(range(-1, 5))
    down_a = one_hot((128, 128), lambda l, j: l // 2 == j)
    down_b = one_hot((128, 128), lambda l, j: jnp.logical_and(l < 64, l // 2 == j - 64))
    for z in range(2):
        for t in range(2):
            total = None
            for k in range(2):
                x, n = apply1(VB1, 2, t, 2 * z + k)
                r = BB1[t, 2 * z + k + 3] + n - DD1[t, 2 * z + k] * x
                total = r[0:16] if total is None else total + r[0:16]
            RS1[t, z] = total
        b2_own[z] = dot(pairs(RS1, 0, z, 8), down_a) + dot(pairs(RS1, 1, z, 8), down_b)
    b2_moves = far_copies(b2_send, b2_recv, b2_own, b2)
    start(b2_moves)
    b2[pl.ds(2 * h, 2), 16:24] = b2_own[...]

    wait_recv(b1_moves)
    for t in range(2):
        VA1[t, 0] = WH1[t, 0] * jnp.where(below, b1_vert[0, t], 0.0)
        VA1[t, 9] = WH1[t, 9] * jnp.where(above, b1_vert[1, t], 0.0)
    second_sweep1((-2, 5))

    lane2 = iota((40, 128), 1)
    row2 = iota((40, 128), 0)
    col2 = lane2 % 32
    real = lane2 < 96
    slot = row2 // 8 + (i - 2)
    inside = jnp.logical_and(slot >= 0, slot < tiles)
    keep = jnp.logical_and(inside, real)
    wait_recv(q2_moves)

    def pick(a, b, e):
        return jnp.where(lane2 < 32, a, jnp.where(lane2 < 64, b, e))

    q = jnp.where(inside, q2[0], 0.0)
    spring2 = pick(pltpu.roll(q, 32, 1), pltpu.roll(q, 64, 1), pltpu.roll(q, 96, 1))
    odd_row, odd_col = row2 % 2 == 1, lane2 % 2 == 1

    def pair_sum(x):
        x = x + jnp.where(odd_row, pltpu.roll(x, 1, 0), pltpu.roll(x, 39, 0))
        return x + jnp.where(odd_col, pltpu.roll(x, 1, 1), pltpu.roll(x, 127, 1))

    def faces(s_of, depth, step, spring, hz, hr, hc, wh, dd):
        for z in range(depth - 1):
            hz[z] = s_of(z) + s_of(z + 1)
        for z in range(depth):
            s = s_of(z)
            h_ru = s + pltpu.roll(s, 40 - step, 0)
            h_rl = pltpu.roll(h_ru, step, 0)
            first, last = col2 < step, col2 >= 32 - step
            f_cu = s + jnp.where(last, 0.0, pltpu.roll(s, 128 - step, 1))
            f_cl = s + jnp.where(first, 0.0, pltpu.roll(s, step, 1))
            hr[0, z] = h_rl
            hr[1, z] = h_ru
            hc[0, z] = jnp.where(first, 0.0, f_cl)
            hc[1, z] = jnp.where(last, 0.0, f_cu)
            f_z = (hz[z - 1] if z > 0 else s) + (hz[z] if z < depth - 1 else s)
            f_r, f_c = h_rl + h_ru, f_cl + f_cu
            d = (f_z + f_r + f_c) + pick(f_z, f_r, f_c)
            if z == 0:
                d = d + spring
            wh[z] = jnp.where(s > 0.0, OMEGA / jnp.where(s > 0.0, d, 1.0), 0.0)
            if dd is not None:
                dd[z] = d

    def s2(z):
        return jnp.where(keep, q2[z], 0.0)

    faces(s2, 8, 1, spring2, HZ2, HR2, HC2, WH2, DD2)
    for z in range(4):
        S3[z] = 0.5 * pair_sum(s2(2 * z) + s2(2 * z + 1))
    faces(lambda z: S3[z], 4, 2, pair_sum(spring2), HZ3, HR3, HC3, WH3, None)

    def apply2(v, z, depth, step, hz, hr, hc):
        x = v[z]
        a = None
        if z > 0:
            a = hz[z - 1] * v[z - 1]
        if z < depth - 1:
            up = hz[z] * v[z + 1]
            a = up if a is None else a + up
        b = hr[0, z] * pltpu.roll(x, step, 0) + hr[1, z] * pltpu.roll(x, 40 - step, 0)
        e = hc[0, z] * pltpu.roll(x, step, 1) + hc[1, z] * pltpu.roll(x, 128 - step, 1)
        return x, (a + b + e) + pick(a, b, e)

    wait_recv(b2_moves)
    for z in range(8):
        b = jnp.where(keep, b2[z], 0.0)
        b2[z] = b
        VA2[z] = WH2[z] * b
    for z in range(8):
        x, n = apply2(VA2, z, 8, 1, HZ2, HR2, HC2)
        VB2[z] = KEEP * x + WH2[z] * (b2[z] + n)
    for z in range(4):
        total = None
        for k in range(2):
            x, n = apply2(VB2, 2 * z + k, 8, 1, HZ2, HR2, HC2)
            r = b2[2 * z + k] + n - DD2[2 * z + k] * x
            total = r if total is None else total + r
        total = pair_sum(total)
        BB3[z] = total
        V3[0, z] = WH3[z] * total
    for turn in range(5):
        now, later = turn % 2, (turn + 1) % 2
        for z in range(4):
            x, n = apply2(V3.at[now], z, 4, 2, HZ3, HR3, HC3)
            new = KEEP * x + WH3[z] * (BB3[z] + n)
            if turn == 0:
                V3[later, z] = new
            else:
                V3[later, z, 8:32] = new[8:32]
    for z in range(8):
        VB2[z, 8:32] = VB2[z, 8:32] + V3[1, z // 2, 8:32]
    PO2[0] = jnp.zeros((24, 128), F32)
    PO2[9] = jnp.zeros((24, 128), F32)
    for z in range(8):
        x, n = apply2(VB2, z, 8, 1, HZ2, HR2, HC2)
        PO2[z + 1] = (KEEP * x + WH2[z] * (b2[z] + n))[8:32]

    up_a = one_hot((128, 128), lambda l, j: l == j // 2)
    up_b = one_hot((128, 128), lambda l, j: jnp.logical_and(j < 64, l == 64 + j // 2))
    for k in range(4):
        coarse = PO2[2 * h + k]
        for t, m in enumerate((up_a, up_b)):
            e = dot(coarse, m)
            T1[t, k, pl.ds(0, 24, 2)] = e
            T1[t, k, pl.ds(1, 24, 2)] = e
            tail = jnp.where(sub8 < 4, T1[t, k, 32:40], T1[t, k, 8:16])
            e = jnp.concatenate([T1[t, k, 16:32], tail], axis=0)
            for z in (2 * k, 2 * k + 1):
                VB1[t, z] = VB1[t, z] + e
    for z in range(-1, 5):
        for t in range(2):
            x, n = apply1(VB1, 2, t, z)
            PO1[t, z + 1] = KEEP * x + WH1[t, z + 3] * (BB1[t, z + 3] + n)

    up_lo = one_hot((128, 128), lambda l, j: l == j // 2)
    up_hi = one_hot((128, 128), lambda l, j: l == 64 + j // 2)
    for k in range(6):
        for c in range(3):
            e = dot(PO1[c // 2, k], up_hi if c == 1 else up_lo)
            T0[c, k, pl.ds(0, 24, 2)] = e
            T0[c, k, pl.ds(1, 24, 2)] = e
            for z in (2 * k - 2, 2 * k - 1):
                if -1 <= z < 9:
                    V1[c, z + 5] = V1[c, z + 5] + T0[c, k]
    for z in range(8):
        for c in range(3):
            x, n = apply0(V1, 5, c, z)
            out[c, z] = (KEEP * x + WH[c, z + 6] * (BB[c, z + 6] + n))[0:32]

    for moves in (label_moves, deep_moves, q1_moves, q2_moves, b1_moves, b2_moves):
        wait_send(moves)


def solution(mesh):
    heights, tiles = mesh.shape["height"], mesh.shape["tile"]

    def vmem(*shape, dtype=F32):
        return pltpu.VMEM(shape, dtype)

    i32 = jnp.int32
    scratch = [
        pltpu.SMEM((3,), F32), pltpu.SMEM((3, 3), F32),
        vmem(8, 32, 128, dtype=i32), vmem(2, 32, 128, dtype=i32),
        vmem(7, 32, 128, dtype=i32), vmem(7, 32, 128, dtype=i32),
        vmem(2, 11, 8, 128, dtype=i32), vmem(2, 2, 7, 8, 128, dtype=i32), vmem(2, 11, 8, 128, dtype=i32),
        vmem(4, 16, 128), vmem(2, 4, 16, 128), vmem(2, 3, 4, 4, 128), vmem(2, 4, 4, 128),
        vmem(8, 40, 128), vmem(2, 8, 128),
        vmem(2, 2, 24, 128),
        vmem(8, 40, 128), vmem(2, 8, 128),
        vmem(22, 48, 128), vmem(3, 22, 48, 128), vmem(21, 48, 128), vmem(2, 20, 48, 128), vmem(2, 20, 48, 128),
        vmem(3, 20, 48, 128), vmem(3, 20, 48, 128), vmem(3, 16, 48, 128), vmem(3, 20, 48, 128),
        vmem(3, 18, 48, 128), vmem(3, 8, 48, 128), vmem(2, 2, 8, 128),
        vmem(12, 24, 128), vmem(11, 24, 128), vmem(2, 10, 24, 128), vmem(2, 10, 24, 128), vmem(2, 10, 24, 128),
        vmem(2, 10, 24, 128), vmem(2, 4, 24, 128), vmem(2, 10, 24, 128), vmem(2, 8, 24, 128),
        vmem(2, 2, 16, 128), vmem(2, 6, 24, 128),
        vmem(7, 40, 128), vmem(2, 8, 40, 128), vmem(2, 8, 40, 128), vmem(8, 40, 128), vmem(8, 40, 128),
        vmem(8, 40, 128), vmem(8, 40, 128), vmem(10, 24, 128), vmem(2, 4, 48, 128),
        vmem(4, 40, 128), vmem(3, 40, 128), vmem(2, 4, 40, 128), vmem(2, 4, 40, 128), vmem(4, 40, 128),
        vmem(4, 40, 128), vmem(2, 4, 40, 128),
        vmem(3, 6, 48, 128), vmem(2, 4, 32, 128),
        pltpu.SemaphoreType.DMA((4,)),
    ]
    for count in (8, 6, 8, 19, 2, 19):
        scratch += [pltpu.SemaphoreType.DMA((count,)), pltpu.SemaphoreType.DMA((count,))]

    def local(material, clamped, stiffness_table, eigenstrain):
        return pl.pallas_call(
            functools.partial(kernel, heights, tiles),
            out_shape=jax.ShapeDtypeStruct((3, 8, 32, 128), F32),
            in_specs=[
                pl.BlockSpec(memory_space=pltpu.HBM),
                pl.BlockSpec(memory_space=pltpu.HBM),
                pl.BlockSpec(memory_space=pltpu.HBM),
                pl.BlockSpec(memory_space=pltpu.HBM),
            ],
            out_specs=pl.BlockSpec(memory_space=pltpu.VMEM),
            scratch_shapes=scratch,
            compiler_params=pltpu.CompilerParams(
                collective_id=0, has_side_effects=True, vmem_limit_bytes=40 * 1024 * 1024
            ),
        )(*(pltpu.with_memory_space_constraint(x, pltpu.HBM) for x in (material, clamped, stiffness_table, eigenstrain)))

    in_specs = (P("height", "tile", None), P("height", "tile", None), P(), P())
    out_specs = P(None, "height", "tile", None)
    return jax.shard_map(local, mesh=mesh, in_specs=in_specs, out_specs=out_specs, check_vma=False)
```

```python
import functools

import jax
import jax.numpy as jnp
from jax import lax
from jax.experimental import pallas as pl
from jax.experimental.pallas import tpu as pltpu
from jax.sharding import PartitionSpec as P

PENALTY = 50.0
OMEGA = 0.6
KEEP = 1.0 - OMEGA
F32 = jnp.float32
BF16 = jnp.bfloat16
NEAR = ((-1, -1), (-1, 1), (1, -1), (1, 1), (-1, 0), (1, 0), (0, -1), (0, 1))
UPDOWN = ((0, -1), (0, 1))
DEEP = tuple(move for move in NEAR if move[1] != 0)
FAR = tuple(
    sorted(
        ((dt, k) for dt in (-2, -1, 0, 1, 2) for k in (0, 1, 2, 3) if (dt, k) != (0, 0)),
        key=lambda move: (-abs(move[0]), -min(move[1], 4 - move[1]), move),
    )
)


def iota(shape, axis):
    return lax.broadcasted_iota(jnp.int32, shape, axis)


def one_hot(shape, cond):
    return jnp.where(cond(iota(shape, 0), iota(shape, 1)), 1.0, 0.0).astype(BF16)


def dot(a, b):
    hi = a.astype(BF16)
    rest = a - hi.astype(F32)
    mid = rest.astype(BF16)
    lo = (rest - mid.astype(F32)).astype(BF16)
    parts = (jnp.dot(x, b, preferred_element_type=F32) for x in (lo, mid, hi))
    return sum(parts)


def kernel(
    heights,
    tiles,
    mat_hbm,
    clamp_hbm,
    table_hbm,
    eigen_hbm,
    out,
    table,
    eigen,
    mat,
    cl,
    m_lo, m_hi, m_side, m_corner, m_stage,
    q1, q1_vert, q1_side, q1_stage,
    q2, q2_own,
    b1_vert,
    b2, b2_own,
    S, SG, HZ, HR, HC, BB, WH, DD, V0, V1, RS, EX,
    S1, HZ1, HR1, HC1, BB1, WH1, DD1, VA1, VB1, RS1, PO1,
    HZ2, HR2, HC2, WH2, DD2, VA2, VB2, PO2, T1,
    S3, HZ3, HR3, HC3, WH3, BB3, V3,
    T0, R4,
    local_sem,
    m_send, m_recv, d_send, d_recv, q1_send, q1_recv, q2_send, q2_recv, b1_send, b1_recv, b2_send, b2_recv,
):
    i = lax.axis_index("tile")
    h = lax.axis_index("height")

    in_mat = pltpu.make_async_copy(mat_hbm, mat, local_sem.at[0])
    in_cl = pltpu.make_async_copy(clamp_hbm.at[pl.ds(0, 2)], cl, local_sem.at[1])
    in_table = pltpu.make_async_copy(table_hbm, table, local_sem.at[2])
    in_eigen = pltpu.make_async_copy(eigen_hbm, eigen, local_sem.at[3])

    def tile_ok(dt):
        return jnp.logical_and(i + dt >= 0, i + dt < tiles)

    def near_ok(dt, dh):
        return jnp.logical_and(tile_ok(dt), jnp.logical_and(h + dh >= 0, h + dh < heights))

    def far_id(dt, k):
        return {"tile": i + dt, "height": lax.rem(h + k, heights)}

    in_mat.start()
    barrier = pltpu.get_barrier_semaphore()
    ring = [(dt, k) for dt in (-1, 1, 0) for k in (1, 3, 0) if (dt, k) != (0, 0)]
    for dt, k in ring:
        @pl.when(tile_ok(dt))
        def _():
            pl.semaphore_signal(
                barrier, inc=1, device_id=far_id(dt, k), device_id_type=pl.DeviceIdType.MESH
            )
    reach = 3 * (tile_ok(-1).astype(jnp.int32) + tile_ok(1).astype(jnp.int32)) + 2

    in_cl.start()
    in_table.start()
    in_eigen.start()
    in_mat.wait()
    in_cl.wait()
    for side, first, edge in ((0, 0, 8), (1, 24, 23)):
        for z in range(8):
            m_stage[side, z] = mat[z, first : first + 8]
        for z in range(2):
            m_stage[side, 8 + z] = cl[z, first : first + 8]
        m_stage[side, 10] = mat[:, edge]

    pl.semaphore_wait(barrier, reach)

    def near_copies(send, recv, refs, moves=NEAR):
        copies = []
        for k, (dt, dh) in enumerate(moves):
            src, dst = refs(dt, dh)
            copy = pltpu.make_async_remote_copy(
                src_ref=src, dst_ref=dst, send_sem=send.at[k], recv_sem=recv.at[k],
                device_id={"tile": i + dt, "height": h + dh},
                device_id_type=pl.DeviceIdType.MESH,
            )
            copies.append((copy, near_ok(dt, dh), near_ok(-dt, -dh)))
        return copies

    def far_copies(send, recv, own, field):
        copies = []
        for k, (dt, dh) in enumerate(FAR):
            copy = pltpu.make_async_remote_copy(
                src_ref=own,
                dst_ref=field.at[pl.ds(2 * h, 2), pl.ds(8 * (2 - dt), 8)],
                send_sem=send.at[k], recv_sem=recv.at[k],
                device_id=far_id(dt, dh), device_id_type=pl.DeviceIdType.MESH,
            )
            copies.append((copy, tile_ok(dt), tile_ok(-dt)))
        return copies

    def start(copies):
        for copy, sends, _ in copies:
            @pl.when(sends)
            def _():
                copy.start()

    def wait_recv(copies):
        for copy, _, receives in copies:
            @pl.when(receives)
            def _():
                copy.wait_recv()

    def wait_send(copies):
        for copy, sends, _ in copies:
            @pl.when(sends)
            def _():
                copy.wait_send()

    def label_refs(dt, dh):
        if dt == 0:
            if dh > 0:
                return mat.at[pl.ds(5, 3)], m_lo.at[pl.ds(4, 3)]
            return mat.at[pl.ds(0, 3)], m_hi.at[pl.ds(0, 3)]
        side = 0 if dt < 0 else 1
        if dh == 0:
            return m_stage.at[side], m_side.at[side]
        if dh > 0:
            return m_stage.at[side, pl.ds(5, 3)], m_corner.at[side, 1, pl.ds(4, 3)]
        return m_stage.at[side, pl.ds(0, 3)], m_corner.at[side, 0, pl.ds(0, 3)]

    def deep_refs(dt, dh):
        if dt == 0:
            if dh > 0:
                return mat.at[pl.ds(1, 4)], m_lo.at[pl.ds(0, 4)]
            return mat.at[pl.ds(3, 4)], m_hi.at[pl.ds(3, 4)]
        side = 0 if dt < 0 else 1
        if dh > 0:
            return m_stage.at[side, pl.ds(1, 4)], m_corner.at[side, 1, pl.ds(0, 4)]
        return m_stage.at[side, pl.ds(3, 4)], m_corner.at[side, 0, pl.ds(3, 4)]

    label_moves = near_copies(m_send, m_recv, label_refs)
    start(label_moves)
    deep_moves = near_copies(d_send, d_recv, deep_refs, DEEP)
    start(deep_moves)
    in_table.wait()
    in_eigen.wait()

    st = [table[n] for n in range(3)]
    stress = [[table[n] * eigen[n, c] for c in range(3)] for n in range(3)]

    def look(m, values):
        return jnp.where(
            m == 0, values[0], jnp.where(m == 1, values[1], jnp.where(m == 2, values[2], 0.0))
        )

    take_lo = one_hot((128, 128), lambda l, j: jnp.logical_and(j < 64, l // 2 == j))
    take_hi = one_hot((128, 128), lambda l, j: l // 2 == j - 64)
    lowest = jnp.where(h == 0, 1.0, 0.0).astype(F32)

    for z in range(4):
        R4[0, z] = look(mat[2 * z], st) + look(mat[2 * z + 1], st)
    R4[1, 0] = (cl[0] + cl[1]).astype(F32)
    s_rows = jnp.concatenate(
        [R4[0, z, pl.ds(0, 16, 2)] + R4[0, z, pl.ds(1, 16, 2)] for z in range(4)], axis=0
    )
    p_rows = R4[1, 0, pl.ds(0, 16, 2)] + R4[1, 0, pl.ds(1, 16, 2)]
    s_one = dot(0.5 * s_rows, take_lo).reshape(4, 16, 128)
    p_one = dot((2.0 * PENALTY * lowest) * p_rows, take_hi)
    q1[0] = s_one[0] + p_one
    for z in range(1, 4):
        q1[z] = s_one[z]
    for z in range(4):
        q1_stage[0, z] = q1[z, 0:4]
        q1_stage[1, z] = q1[z, 12:16]

    def q1_refs(dt, dh):
        if dt == 0:
            return q1, q1_vert.at[0 if dh > 0 else 1]
        side = 0 if dt < 0 else 1
        return q1_stage.at[side], q1_side.at[side, dh + 1]

    q1_moves = near_copies(q1_send, q1_recv, q1_refs)
    start(q1_moves)

    for z in range(2):
        R4[1, z, 0:16] = q1[2 * z] + q1[2 * z + 1]
    q_rows = jnp.concatenate(
        [R4[1, z, pl.ds(0, 8, 2)] + R4[1, z, pl.ds(1, 8, 2)] for z in range(2)], axis=0
    )
    l, j = iota((128, 128), 0), iota((128, 128), 1)
    down_q = jnp.where(
        jnp.logical_and(j < 96, jnp.logical_and(l < 64, l // 2 == j % 32)), 0.5,
        jnp.where(jnp.logical_and(j >= 96, l // 2 == j - 64), 1.0, 0.0),
    ).astype(BF16)
    q2_own[...] = dot(q_rows, down_q).reshape(2, 8, 128)
    q2_moves = far_copies(q2_send, q2_recv, q2_own, q2)
    q2[pl.ds(2 * h, 2), 16:24] = q2_own[...]

    lane = iota((48, 128), 1)
    row = iota((48, 128), 0)
    sub8 = iota((8, 128), 0)
    wait_recv(label_moves)
    start(q2_moves)
    below, above = h > 0, h < heights - 1
    before, after = i > 0, i < tiles - 1

    def labels(z):
        if 0 <= z < 8:
            centre, hi, lo = mat[z], m_side[0, z], m_side[1, z]
            centre_ok, hi_ok, lo_ok = None, after, before
        else:
            centre_ok = below if z < 0 else above
            end = 1 if z < 0 else 0
            k = z + 7 if z < 0 else z - 8
            centre = jnp.where(centre_ok, (m_lo if z < 0 else m_hi)[k], -1)
            hi, lo = m_corner[0, end, k], m_corner[1, end, k]
            hi_ok, lo_ok = jnp.logical_and(centre_ok, after), jnp.logical_and(centre_ok, before)
        return jnp.concatenate([centre, jnp.where(hi_ok, hi, -1), jnp.where(lo_ok, lo, -1)], axis=0)

    def build(zs):
        for z in zs:
            m = labels(z)
            S[z + 7] = look(m, st)
            for c in range(3):
                SG[c, z + 7] = look(m, [stress[n][c] for n in range(3)])

    build(range(-3, 11))
    for side, ok in ((0, after), (1, before)):
        m = jnp.where(ok, m_side[side, 10], -1)
        EX[side, 0] = look(m, st)
        EX[side, 1] = look(m, [stress[n][1] for n in range(3)])
    def between(zs):
        for z in zs:
            HZ[z + 7] = S[z + 7] + S[z + 8]

    between(range(-3, 10))

    def spring0(z):
        sides = jnp.concatenate(
            [jnp.where(after, m_side[0, 8 + z], 0), jnp.where(before, m_side[1, 8 + z], 0)],
            axis=0,
        )
        return (2.0 * PENALTY * lowest) * jnp.concatenate([cl[z], sides], axis=0).astype(F32)

    def first_sweep(z):
        s = S[z + 7]
        s_r = pltpu.roll(s, 47, 0)
        if 0 <= z < 8:
            s_r = jnp.where(row == 39, EX[0, 0, z : z + 1], s_r)
        s_c = jnp.where(lane < 127, pltpu.roll(s, 127, 1), 0.0)
        h_ru = s + s_r
        h_rl = pltpu.roll(h_ru, 1, 0)
        if 0 <= z < 8:
            h_rl = jnp.where(row == 40, s + EX[1, 0, z : z + 1], h_rl)
        f_cu = s + s_c
        f_cl = s + jnp.where(lane > 0, pltpu.roll(s, 1, 1), 0.0)
        HR[0, z + 6] = h_rl
        HR[1, z + 6] = h_ru
        HC[0, z + 6] = jnp.where(lane > 0, f_cl, 0.0)
        HC[1, z + 6] = jnp.where(lane < 127, f_cu, 0.0)
        f = [HZ[z + 6] + HZ[z + 7], h_rl + h_ru, f_cl + f_cu]
        total = f[0] + f[1] + f[2]
        if 0 <= z < 2:
            total = total + spring0(z)
        g0 = SG[0, z + 6] - SG[0, z + 8]
        x = SG[1, z + 7]
        x_l, x_u = pltpu.roll(x, 1, 0), pltpu.roll(x, 47, 0)
        if 0 <= z < 8:
            x_l = jnp.where(row == 40, EX[1, 1, z : z + 1], x_l)
            x_u = jnp.where(row == 39, EX[0, 1, z : z + 1], x_u)
        g1 = x_l - x_u
        x = SG[2, z + 7]
        g2 = jnp.where(lane > 0, pltpu.roll(x, 1, 1), 0.0) - jnp.where(
            lane < 127, pltpu.roll(x, 127, 1), 0.0
        )
        d = [total + f[c] for c in range(3)]
        d01 = d[0] * d[1]
        one = jnp.where(s > 0.0, OMEGA / (d01 * d[2]), 0.0)
        part = one * d[2]
        for c, (g, w) in enumerate(((g0, part * d[1]), (g1, part * d[0]), (g2, one * d01))):
            BB[c, z + 6] = g
            WH[c, z + 6] = w
            if -4 <= z < 12:
                DD[c, z + 4] = d[c]
            V0[c, z + 6] = w * g

    for z in range(-2, 10):
        first_sweep(z)

    def apply0(v, off, c, z):
        x = v[c, z + off]
        a = HZ[z + 6] * v[c, z + off - 1] + HZ[z + 7] * v[c, z + off + 1]
        b = HR[0, z + 6] * pltpu.roll(x, 1, 0) + HR[1, z + 6] * pltpu.roll(x, 47, 0)
        e = HC[0, z + 6] * pltpu.roll(x, 1, 1) + HC[1, z + 6] * pltpu.roll(x, 127, 1)
        return x, (a + b + e) + (a, b, e)[c]

    def second_sweep(zs):
        for z in zs:
            for c in range(3):
                x, n = apply0(V0, 6, c, z)
                V1[c, z + 5] = KEEP * x + WH[c, z + 6] * (BB[c, z + 6] + n)

    def pairs(ref, c, z, n):
        return ref[c, z, pl.ds(0, n, 2)] + ref[c, z, pl.ds(1, n, 2)]

    def restrict(zs):
        for z in zs:
            for c in range(3):
                total = None
                for k in range(2):
                    x, n = apply0(V1, 5, c, 2 * z + k)
                    r = BB[c, 2 * z + k + 6] + n - DD[c, 2 * z + k + 4] * x
                    total = r if total is None else total + r
                RS[c, z + 2] = total
            BB1[0, z + 3] = dot(pairs(RS, 0, z + 2, 24), take_lo) + dot(pairs(RS, 1, z + 2, 24), take_hi)
            BB1[1, z + 3] = dot(pairs(RS, 2, z + 2, 24), take_lo)

    second_sweep(range(-1, 9))
    restrict(range(0, 4))

    def b1_refs(dt, dh):
        return BB1.at[:, 4 if dh > 0 else 5], b1_vert.at[0 if dh > 0 else 1]

    b1_moves = near_copies(b1_send, b1_recv, b1_refs, UPDOWN)
    start(b1_moves)

    wait_recv(deep_moves)
    build((*range(-7, -3), *range(11, 15)))
    between((*range(-7, -3), *range(10, 14)))
    for z in (*range(-6, -2), *range(10, 14)):
        first_sweep(z)
    second_sweep((*range(-5, -1), *range(9, 13)))
    restrict((-2, -1, 4, 5))

    lane1 = iota((24, 128), 1)
    col1 = lane1 % 64
    wait_recv(q1_moves)

    def both(x):
        return jnp.where(iota(x.shape, len(x.shape) - 1) < 64, x, 0.0)

    for z in range(-4, 8):
        if z < 0:
            centre = jnp.where(below, q1_vert[0, z + 4], 0.0)
            lo = jnp.where(jnp.logical_and(below, before), q1_side[1, 2, z + 4], 0.0)
            hi = jnp.where(jnp.logical_and(below, after), q1_side[0, 2, z + 4], 0.0)
        elif z < 4:
            centre = q1[z]
            lo = jnp.where(before, q1_side[1, 1, z], 0.0)
            hi = jnp.where(after, q1_side[0, 1, z], 0.0)
        else:
            centre = jnp.where(above, q1_vert[1, z - 4], 0.0)
            lo = jnp.where(jnp.logical_and(above, before), q1_side[1, 0, z - 4], 0.0)
            hi = jnp.where(jnp.logical_and(above, after), q1_side[0, 0, z - 4], 0.0)
        q = jnp.concatenate([centre, hi, lo], axis=0)
        other = pltpu.roll(q, 64, 1)
        S1[z + 4] = jnp.where(lane1 < 64, q, other)
        if z == 0:
            spring1 = jnp.where(lane1 < 64, other, q)
    for z in range(-4, 7):
        HZ1[z + 4] = S1[z + 4] + S1[z + 5]
    for z in range(-3, 7):
        s = S1[z + 4]
        h_ru = s + pltpu.roll(s, 23, 0)
        h_rl = pltpu.roll(h_ru, 1, 0)
        f_cu = s + jnp.where(col1 < 63, pltpu.roll(s, 127, 1), 0.0)
        f_cl = s + jnp.where(col1 > 0, pltpu.roll(s, 1, 1), 0.0)
        HR1[0, z + 3] = h_rl
        HR1[1, z + 3] = h_ru
        HC1[0, z + 3] = jnp.where(col1 > 0, f_cl, 0.0)
        HC1[1, z + 3] = jnp.where(col1 < 63, f_cu, 0.0)
        f = [HZ1[z + 3] + HZ1[z + 4], h_rl + h_ru, f_cl + f_cu]
        total = f[0] + f[1] + f[2]
        if z == 0:
            total = total + spring1
        for t in range(2):
            d = total + (jnp.where(lane1 < 64, f[0], f[1]) if t == 0 else f[2])
            WH1[t, z + 3] = jnp.where(s > 0.0, OMEGA / jnp.where(s > 0.0, d, 1.0), 0.0)
            if 0 <= z < 4:
                DD1[t, z] = d

    for z in range(-2, 6):
        for t in range(2):
            if z < 0:
                BB1[t, z + 3] = jnp.where(below, BB1[t, z + 3], 0.0)
            if z > 3:
                BB1[t, z + 3] = jnp.where(above, BB1[t, z + 3], 0.0)
            VA1[t, z + 3] = WH1[t, z + 3] * BB1[t, z + 3]

    def apply1(v, off, t, z):
        x = v[t, z + off]
        a = HZ1[z + 3] * v[t, z + off - 1] + HZ1[z + 4] * v[t, z + off + 1]
        b = HR1[0, z + 3] * pltpu.roll(x, 1, 0) + HR1[1, z + 3] * pltpu.roll(x, 23, 0)
        e = HC1[0, z + 3] * pltpu.roll(x, 1, 1) + HC1[1, z + 3] * pltpu.roll(x, 127, 1)
        return x, (a + b + e) + (jnp.where(lane1 < 64, a, b) if t == 0 else e)

    def second_sweep1(zs):
        for z in zs:
            for t in range(2):
                x, n = apply1(VA1, 3, t, z)
                VB1[t, z + 2] = KEEP * x + WH1[t, z + 3] * (BB1[t, z + 3] + n)

    second_sweep1(range(-1, 5))
    down_a = one_hot((128, 128), lambda l, j: l // 2 == j)
    down_b = one_hot((128, 128), lambda l, j: jnp.logical_and(l < 64, l // 2 == j - 64))
    for z in range(2):
        for t in range(2):
            total = None
            for k in range(2):
                x, n = apply1(VB1, 2, t, 2 * z + k)
                r = BB1[t, 2 * z + k + 3] + n - DD1[t, 2 * z + k] * x
                total = r[0:16] if total is None else total + r[0:16]
            RS1[t, z] = total
        b2_own[z] = dot(pairs(RS1, 0, z, 8), down_a) + dot(pairs(RS1, 1, z, 8), down_b)
    b2_moves = far_copies(b2_send, b2_recv, b2_own, b2)
    start(b2_moves)
    b2[pl.ds(2 * h, 2), 16:24] = b2_own[...]

    wait_recv(b1_moves)
    for t in range(2):
        VA1[t, 0] = WH1[t, 0] * jnp.where(below, b1_vert[0, t], 0.0)
        VA1[t, 9] = WH1[t, 9] * jnp.where(above, b1_vert[1, t], 0.0)
    second_sweep1((-2, 5))

    lane2 = iota((40, 128), 1)
    row2 = iota((40, 128), 0)
    col2 = lane2 % 32
    real = lane2 < 96
    slot = row2 // 8 + (i - 2)
    inside = jnp.logical_and(slot >= 0, slot < tiles)
    keep = jnp.logical_and(inside, real)
    wait_recv(q2_moves)

    def pick(a, b, e):
        return jnp.where(lane2 < 32, a, jnp.where(lane2 < 64, b, e))

    q = jnp.where(inside, q2[0], 0.0)
    spring2 = pick(pltpu.roll(q, 32, 1), pltpu.roll(q, 64, 1), pltpu.roll(q, 96, 1))
    odd_row, odd_col = row2 % 2 == 1, lane2 % 2 == 1

    def pair_sum(x):
        x = x + jnp.where(odd_row, pltpu.roll(x, 1, 0), pltpu.roll(x, 39, 0))
        return x + jnp.where(odd_col, pltpu.roll(x, 1, 1), pltpu.roll(x, 127, 1))

    def faces(s_of, depth, step, spring, hz, hr, hc, wh, dd):
        for z in range(depth - 1):
            hz[z] = s_of(z) + s_of(z + 1)
        for z in range(depth):
            s = s_of(z)
            h_ru = s + pltpu.roll(s, 40 - step, 0)
            h_rl = pltpu.roll(h_ru, step, 0)
            first, last = col2 < step, col2 >= 32 - step
            f_cu = s + jnp.where(last, 0.0, pltpu.roll(s, 128 - step, 1))
            f_cl = s + jnp.where(first, 0.0, pltpu.roll(s, step, 1))
            hr[0, z] = h_rl
            hr[1, z] = h_ru
            hc[0, z] = jnp.where(first, 0.0, f_cl)
            hc[1, z] = jnp.where(last, 0.0, f_cu)
            f_z = (hz[z - 1] if z > 0 else s) + (hz[z] if z < depth - 1 else s)
            f_r, f_c = h_rl + h_ru, f_cl + f_cu
            d = (f_z + f_r + f_c) + pick(f_z, f_r, f_c)
            if z == 0:
                d = d + spring
            wh[z] = jnp.where(s > 0.0, OMEGA / jnp.where(s > 0.0, d, 1.0), 0.0)
            if dd is not None:
                dd[z] = d

    def s2(z):
        return jnp.where(keep, q2[z], 0.0)

    faces(s2, 8, 1, spring2, HZ2, HR2, HC2, WH2, DD2)
    for z in range(4):
        S3[z] = 0.5 * pair_sum(s2(2 * z) + s2(2 * z + 1))
    faces(lambda z: S3[z], 4, 2, pair_sum(spring2), HZ3, HR3, HC3, WH3, None)

    def apply2(v, z, depth, step, hz, hr, hc):
        x = v[z]
        a = None
        if z > 0:
            a = hz[z - 1] * v[z - 1]
        if z < depth - 1:
            up = hz[z] * v[z + 1]
            a = up if a is None else a + up
        b = hr[0, z] * pltpu.roll(x, step, 0) + hr[1, z] * pltpu.roll(x, 40 - step, 0)
        e = hc[0, z] * pltpu.roll(x, step, 1) + hc[1, z] * pltpu.roll(x, 128 - step, 1)
        return x, (a + b + e) + pick(a, b, e)

    wait_recv(b2_moves)
    for z in range(8):
        b = jnp.where(keep, b2[z], 0.0)
        b2[z] = b
        VA2[z] = WH2[z] * b
    for z in range(8):
        x, n = apply2(VA2, z, 8, 1, HZ2, HR2, HC2)
        VB2[z] = KEEP * x + WH2[z] * (b2[z] + n)
    for z in range(4):
        total = None
        for k in range(2):
            x, n = apply2(VB2, 2 * z + k, 8, 1, HZ2, HR2, HC2)
            r = b2[2 * z + k] + n - DD2[2 * z + k] * x
            total = r if total is None else total + r
        total = pair_sum(total)
        BB3[z] = total
        V3[0, z] = WH3[z] * total
    for turn in range(5):
        now, later = turn % 2, (turn + 1) % 2
        for z in range(4):
            x, n = apply2(V3.at[now], z, 4, 2, HZ3, HR3, HC3)
            new = KEEP * x + WH3[z] * (BB3[z] + n)
            if turn == 0:
                V3[later, z] = new
            else:
                V3[later, z, 8:32] = new[8:32]
    for z in range(8):
        VB2[z, 8:32] = VB2[z, 8:32] + V3[1, z // 2, 8:32]
    PO2[0] = jnp.zeros((24, 128), F32)
    PO2[9] = jnp.zeros((24, 128), F32)
    for z in range(8):
        x, n = apply2(VB2, z, 8, 1, HZ2, HR2, HC2)
        PO2[z + 1] = (KEEP * x + WH2[z] * (b2[z] + n))[8:32]

    up_a = one_hot((128, 128), lambda l, j: l == j // 2)
    up_b = one_hot((128, 128), lambda l, j: jnp.logical_and(j < 64, l == 64 + j // 2))
    for k in range(4):
        coarse = PO2[2 * h + k]
        for t, m in enumerate((up_a, up_b)):
            e = dot(coarse, m)
            T1[t, k, pl.ds(0, 24, 2)] = e
            T1[t, k, pl.ds(1, 24, 2)] = e
            tail = jnp.where(sub8 < 4, T1[t, k, 32:40], T1[t, k, 8:16])
            e = jnp.concatenate([T1[t, k, 16:32], tail], axis=0)
            for z in (2 * k, 2 * k + 1):
                VB1[t, z] = VB1[t, z] + e
    for z in range(-1, 5):
        for t in range(2):
            x, n = apply1(VB1, 2, t, z)
            PO1[t, z + 1] = KEEP * x + WH1[t, z + 3] * (BB1[t, z + 3] + n)

    up_lo = one_hot((128, 128), lambda l, j: l == j // 2)
    up_hi = one_hot((128, 128), lambda l, j: l == 64 + j // 2)
    for k in range(6):
        for c in range(3):
            e = dot(PO1[c // 2, k], up_hi if c == 1 else up_lo)
            T0[c, k, pl.ds(0, 24, 2)] = e
            T0[c, k, pl.ds(1, 24, 2)] = e
            for z in (2 * k - 2, 2 * k - 1):
                if -1 <= z < 9:
                    V1[c, z + 5] = V1[c, z + 5] + T0[c, k]
    for z in range(8):
        for c in range(3):
            x, n = apply0(V1, 5, c, z)
            out[c, z] = (KEEP * x + WH[c, z + 6] * (BB[c, z + 6] + n))[0:32]

    for moves in (label_moves, deep_moves, q1_moves, q2_moves, b1_moves, b2_moves):
        wait_send(moves)


def solution(mesh):
    heights, tiles = mesh.shape["height"], mesh.shape["tile"]

    def vmem(*shape, dtype=F32):
        return pltpu.VMEM(shape, dtype)

    i32 = jnp.int32
    scratch = [
        pltpu.SMEM((3,), F32), pltpu.SMEM((3, 3), F32),
        vmem(8, 32, 128, dtype=i32), vmem(2, 32, 128, dtype=i32),
        vmem(7, 32, 128, dtype=i32), vmem(7, 32, 128, dtype=i32),
        vmem(2, 11, 8, 128, dtype=i32), vmem(2, 2, 7, 8, 128, dtype=i32), vmem(2, 11, 8, 128, dtype=i32),
        vmem(4, 16, 128), vmem(2, 4, 16, 128), vmem(2, 3, 4, 4, 128), vmem(2, 4, 4, 128),
        vmem(8, 40, 128), vmem(2, 8, 128),
        vmem(2, 2, 24, 128),
        vmem(8, 40, 128), vmem(2, 8, 128),
        vmem(22, 48, 128), vmem(3, 22, 48, 128), vmem(21, 48, 128), vmem(2, 20, 48, 128), vmem(2, 20, 48, 128),
        vmem(3, 20, 48, 128), vmem(3, 20, 48, 128), vmem(3, 16, 48, 128), vmem(3, 20, 48, 128),
        vmem(3, 18, 48, 128), vmem(3, 8, 48, 128), vmem(2, 2, 8, 128),
        vmem(12, 24, 128), vmem(11, 24, 128), vmem(2, 10, 24, 128), vmem(2, 10, 24, 128), vmem(2, 10, 24, 128),
        vmem(2, 10, 24, 128), vmem(2, 4, 24, 128), vmem(2, 10, 24, 128), vmem(2, 8, 24, 128),
        vmem(2, 2, 16, 128), vmem(2, 6, 24, 128),
        vmem(7, 40, 128), vmem(2, 8, 40, 128), vmem(2, 8, 40, 128), vmem(8, 40, 128), vmem(8, 40, 128),
        vmem(8, 40, 128), vmem(8, 40, 128), vmem(10, 24, 128), vmem(2, 4, 48, 128),
        vmem(4, 40, 128), vmem(3, 40, 128), vmem(2, 4, 40, 128), vmem(2, 4, 40, 128), vmem(4, 40, 128),
        vmem(4, 40, 128), vmem(2, 4, 40, 128),
        vmem(3, 6, 48, 128), vmem(2, 4, 32, 128),
        pltpu.SemaphoreType.DMA((4,)),
    ]
    for count in (8, 6, 8, 19, 2, 19):
        scratch += [pltpu.SemaphoreType.DMA((count,)), pltpu.SemaphoreType.DMA((count,))]

    def local(material, clamped, stiffness_table, eigenstrain):
        return pl.pallas_call(
            functools.partial(kernel, heights, tiles),
            out_shape=jax.ShapeDtypeStruct((3, 8, 32, 128), F32),
            in_specs=[
                pl.BlockSpec(memory_space=pltpu.HBM),
                pl.BlockSpec(memory_space=pltpu.HBM),
                pl.BlockSpec(memory_space=pltpu.HBM),
                pl.BlockSpec(memory_space=pltpu.HBM),
            ],
            out_specs=pl.BlockSpec(memory_space=pltpu.VMEM),
            scratch_shapes=scratch,
            compiler_params=pltpu.CompilerParams(
                collective_id=0, has_side_effects=True, vmem_limit_bytes=40 * 1024 * 1024
            ),
        )(*(pltpu.with_memory_space_constraint(x, pltpu.HBM) for x in (material, clamped, stiffness_table, eigenstrain)))

    in_specs = (P("height", "tile", None), P("height", "tile", None), P(), P())
    out_specs = P(None, "height", "tile", None)
    return jax.shard_map(local, mesh=mesh, in_specs=in_specs, out_specs=out_specs, check_vma=False)
```
